32 devices in a mesh: dp: 4 (over z), seq: 8 (over y, x, core).
Axes of the slice: x: 2, y: 2, z: 4, core: 2. Of those that a mesh axis runs over, the one named last changes fastest.
Arguments:
- view_fine: bfloat16 [4, 768, 768], P('dp', 'seq'), may hold values from -6 to 6
- view_mid: bfloat16 [4, 384, 768], P('dp', 'seq'), may hold values from -6 to 6
- view_coarse: bfloat16 [4, 192, 768], P('dp', 'seq'), may hold values from -6 to 6
- grad_fine: bfloat16 [4, 768, 768], P('dp', 'seq'), may hold values from -6 to 6
- grad_mid: bfloat16 [4, 384, 768], P('dp', 'seq'), may hold values from -6 to 6
- grad_coarse: bfloat16 [4, 192, 768], P('dp', 'seq'), may hold values from -6 to 6
- clip_ids: int32 [4, 192], P('dp'), may hold values from 0 to 3, never falling along the last dimension, each value on 1 to 144 neighbouring positions
- attn_in: bfloat16 [6912, 768], P(('dp', 'seq')), may hold values from -0.21875 to 0.21875
- attn_out: bfloat16 [2304, 768], P(('dp', 'seq')), may hold values from -1.75 to 1.75
- mlp_w: bfloat16 [4608, 3072], P(('dp', 'seq')), may hold values from -0.21875 to 0.21875
- cross_in: bfloat16 [4608, 768], P(('dp', 'seq')), may hold values from -0.21875 to 0.21875
- cross_out: bfloat16 [1536, 768], P(('dp', 'seq')), may hold values from -1.75 to 1.75
- norm_gains: bfloat16 [10, 768], P(None, ('dp', 'seq')), may hold values from 0.5 to 1.5
- biases: bfloat16 [28, 768], P(None, ('dp', 'seq')), may hold values from -0.59765625 to 0.59765625
- ffn_bias: bfloat16 [3, 3072], P(None, ('dp', 'seq')), may hold values from -2 to 2
Outputs:
- out_fine: bfloat16 [4, 768, 768], P('dp', 'seq')
- out_mid: bfloat16 [4, 384, 768], P('dp', 'seq')
- out_coarse: bfloat16 [4, 192, 768], P('dp', 'seq')
- dx_fine: float32 [4, 768, 768], P('dp', 'seq')
- dx_mid: float32 [4, 384, 768], P('dp', 'seq')
- dx_coarse: float32 [4, 192, 768], P('dp', 'seq')
- grad_attn_in: float32 [6912, 768], P(('dp', 'seq'))
- grad_attn_out: float32 [2304, 768], P(('dp', 'seq'))
- grad_mlp: float32 [4608, 3072], P(('dp', 'seq'))
- grad_cross_in: float32 [4608, 768], P(('dp', 'seq'))
- grad_cross_out: float32 [1536, 768], P(('dp', 'seq'))
- grad_gains: float32 [10, 768], P(None, ('dp', 'seq'))
- grad_biases: float32 [28, 768], P(None, ('dp', 'seq'))
- grad_ffn_bias: float32 [3, 3072], P(None, ('dp', 'seq'))
The draws below stay inside these ranges and needn't reach their ends.
Inputs may be any that keep to these rules, and one draw needn't show every extreme that they name: `clip_ids`: along a row the ids never fall; each of the 4 clips holds 1 to 144 cells and one holds exactly 144; a cell is one coarse token, two middle tokens and four fine tokens, in order.
All inputs are finite; a program needn't handle non-finite values.
Results may differ from the reference program's by a relative error of at most 0.017.
Values may be sent and summed in bfloat16 or wider, within the bound.
No kernel may reach another device: no remote copies, remote signals or barrier semaphores. Data moves between devices by JAX's collectives and lax.ppermute only.
A program may use at most 384 MiB of HBM per device.

```python
import math
import jax
import jax.numpy as jnp
import numpy as np
from jax import lax

D = 768
FF = 3072
HEADS = 12
HEAD_DIM = 64
CLIPS = 4
COARSE_LEN = 192
MID_LEN = 384
FINE_LEN = 768
CLIP_MOST = 144
ROWS = 4


def level_of(rng, dims, split, smallest, top_value):
    def one(axis_at, parts):
        draws = jax.random.uniform(jax.random.fold_in(jax.random.fold_in(rng, 6), axis_at), (parts,), jnp.float32, smallest / len(split), top_value / len(split))
        return jnp.repeat(jnp.exp(draws), dims[axis_at] // parts).reshape((-1,) + (1,) * (len(dims) - axis_at - 1))

    factor_of = one(*split[0])
    for cut in split[1:]:
        factor_of = factor_of * one(*cut)
    return factor_of


def profile(number_of, total, limit, slope):
    loads = [(1 << 20) // math.isqrt(grade ** slope) + 1 for grade in range(2, number_of + 1)]
    surplus, holding = total - limit - (number_of - 1), [1] * (number_of - 1)
    while surplus > 0:
        candidates = [i for i in range(number_of - 1) if holding[i] < limit]
        pool, left = sum([loads[i] for i in candidates]), surplus
        for i in candidates:
            extra = min(limit - holding[i], max(1, left * loads[i] // pool), surplus)
            holding[i] = holding[i] + extra
            surplus = surplus - extra
    return np.array([limit] + holding)


def ragged_sizes(stream_key, amount, total, reach, lean):
    if amount == 2:
        one = jax.random.randint(stream_key, (), max(1, total - reach), min(reach, total - 1) + 1)
        return jnp.stack([one, total - one])
    tallies = jnp.asarray(profile(amount, total, reach, lean), jnp.int32)
    twos = (amount - 1) // 2
    donor, sink = tallies[1:1 + 2 * twos:2], tallies[2:2 + 2 * twos:2]
    slack = jnp.minimum(donor - 1, reach - sink)
    passed = jax.random.randint(jax.random.fold_in(stream_key, 1), (twos,), 0, 1 << 20) % (slack + 1)
    tallies = tallies.at[1:1 + 2 * twos:2].set(donor - passed).at[2:2 + 2 * twos:2].set(sink + passed)
    return tallies[jax.random.permutation(jax.random.fold_in(stream_key, 2), amount)]


def centred(rng, extent, deviation, reach, shards=(), kind=jnp.bfloat16):
    result = deviation * jax.random.normal(rng, extent, jnp.float32)
    if shards:
        result = result * level_of(rng, extent, shards, -0.22, 0.18)
    return jnp.clip(result, -reach, reach).astype(kind)


def setup_inputs(seed: int = 0) -> dict:
    streams_of = jax.random.split(jax.random.key(seed), 16)
    view_fine = centred(streams_of[0], (ROWS, FINE_LEN, D), 1.0, 6.0, ((0, 4), (1, 8)))
    view_mid = centred(streams_of[1], (ROWS, MID_LEN, D), 1.0, 6.0, ((0, 4), (1, 8)))
    view_coarse = centred(streams_of[2], (ROWS, COARSE_LEN, D), 1.0, 6.0, ((0, 4), (1, 8)))
    grad_fine = centred(streams_of[3], (ROWS, FINE_LEN, D), 1.0, 6.0, ((0, 4), (1, 8)))
    grad_mid = centred(streams_of[4], (ROWS, MID_LEN, D), 1.0, 6.0, ((0, 4), (1, 8)))
    grad_coarse = centred(streams_of[5], (ROWS, COARSE_LEN, D), 1.0, 6.0, ((0, 4), (1, 8)))
    clip_ids = jax.vmap(lambda own: jnp.searchsorted(jnp.cumsum(ragged_sizes(own, CLIPS, COARSE_LEN, CLIP_MOST, 2)), jnp.arange(COARSE_LEN), side="right"))(jax.random.split(streams_of[6], ROWS)).reshape((ROWS, COARSE_LEN)).astype(jnp.int32)
    attn_in = centred(streams_of[7], (9 * D, D), D ** -0.5, 0.21875, ((0, 32),))
    attn_out = centred(streams_of[8], (3 * D, D), (D // 64) ** -0.5, 1.75, ((0, 32),))
    mlp_w = centred(streams_of[9], (6 * D, FF), D ** -0.5, 0.21875, ((0, 32),))
    cross_in = centred(streams_of[10], (6 * D, D), D ** -0.5, 0.21875, ((0, 32),))
    cross_out = centred(streams_of[11], (2 * D, D), (D // 64) ** -0.5, 1.75, ((0, 32),))
    norm_gains = jnp.clip(1.0 + 0.1 * jax.random.normal(streams_of[12], (10, D), jnp.float32), 0.5, 1.5).astype(jnp.bfloat16)
    biases = centred(streams_of[13], (28, D), 0.1, 0.59765625, ((1, 32),))
    ffn_bias = centred(streams_of[14], (3, FF), 0.3, 2.0, ((1, 32),))
    return dict(view_fine=view_fine, view_mid=view_mid, view_coarse=view_coarse, grad_fine=grad_fine, grad_mid=grad_mid, grad_coarse=grad_coarse, clip_ids=clip_ids, attn_in=attn_in, attn_out=attn_out, mlp_w=mlp_w, cross_in=cross_in, cross_out=cross_out, norm_gains=norm_gains, biases=biases, ffn_bias=ffn_bias)


@jax.custom_vjp
def low(v):
    return lax.optimization_barrier(v.astype(jnp.bfloat16)).astype(jnp.float32)

@jax.custom_vjp
def low_back(v):
    return v

def low_keep(v):
    return (low(v), None)

def low_pass(kept, grad):
    return (grad,)

def back_keep(v):
    return (v, None)

def back_low(kept, grad):
    return (low(grad),)
low.defvjp(low_keep, low_pass)
low_back.defvjp(back_keep, back_low)
eps_norm = 1e-06
neg_large = -1e+30

def product(left_side, right_side):
    return jnp.dot(left_side, right_side, precision=lax.Precision.HIGHEST)

def normed(tokens, gain_row, shift_row):
    centre = lax.optimization_barrier(jnp.mean(tokens, axis=-1, keepdims=True))
    spread = tokens - centre
    variance = lax.optimization_barrier(jnp.mean(spread * spread, axis=-1, keepdims=True))
    return spread * lax.rsqrt(variance + eps_norm) * gain_row + shift_row

def block(matrix, block_index):
    return matrix[block_index * D:(block_index + 1) * D]

def heads_of(matrix):
    return matrix.reshape(matrix.shape[0], HEADS, HEAD_DIM).transpose(1, 0, 2)

def attend(queries, keys_all, values_all, allowed):

    def one_head(pieces):
        head_q, head_k, head_v = pieces
        scores = low_back(product(head_q, head_k.T) * HEAD_DIM ** (-0.5))
        scores = jnp.where(allowed, scores, neg_large)
        probability = low(jax.nn.softmax(scores, axis=-1))
        return low_back(low(product(probability, head_v)))
    head_outs = lax.map(jax.checkpoint(one_head), (heads_of(queries), heads_of(keys_all), heads_of(values_all)))
    return head_outs.transpose(1, 0, 2).reshape(queries.shape[0], HEADS * HEAD_DIM)

def encoder(tokens, allowed, params, view_index):
    attn_w, out_w, mlp_full, cross_w, cross_o, gains, vectors, ffn_rows = params
    offset = 6 * view_index
    normal_a = low(normed(tokens, gains[2 * view_index], vectors[offset]))
    queries = low_back(low(product(normal_a, block(attn_w, 3 * view_index)) + vectors[offset + 1]))
    key_part = low_back(low(product(normal_a, block(attn_w, 3 * view_index + 1))))
    value_part = low_back(low(product(normal_a, block(attn_w, 3 * view_index + 2)) + vectors[offset + 2]))
    attended = attend(queries, key_part, value_part, allowed)
    hidden = tokens + low_back(product(attended, block(out_w, view_index)) + vectors[offset + 3])
    normal_c = low(normed(hidden, gains[2 * view_index + 1], vectors[offset + 4]))
    inner_sum = low_back(product(normal_c, block(mlp_full, 2 * view_index)) + ffn_rows[view_index])
    activated = low(jax.nn.gelu(inner_sum, approximate=False))
    return hidden + low_back(product(activated, block(mlp_full, 2 * view_index + 1).T) + vectors[offset + 5])

def cross(query_rows, key_rows, allowed, params, pair_index):
    attn_w, out_w, mlp_full, cross_w, cross_o, gains, vectors, ffn_rows = params
    offset = 18 + 5 * pair_index
    normal_q = low(normed(query_rows, gains[6 + 2 * pair_index], vectors[offset]))
    normal_k = low(normed(key_rows, gains[7 + 2 * pair_index], vectors[offset + 1]))
    queries = low_back(low(product(normal_q, block(cross_w, 3 * pair_index)) + vectors[offset + 2]))
    key_part = low_back(low(product(normal_k, block(cross_w, 3 * pair_index + 1))))
    value_part = low_back(low(product(normal_k, block(cross_w, 3 * pair_index + 2)) + vectors[offset + 3]))
    attended = attend(queries, key_part, value_part, allowed)
    return query_rows + low_back(product(attended, block(cross_o, pair_index)) + vectors[offset + 4])

def layer(inputs, params, row_ids):
    factors = (4, 2, 1)
    view_ids = [jnp.repeat(row_ids, factor) for factor in factors]
    encoded = [encoder(inputs[view_index], view_ids[view_index][:, None] == view_ids[view_index][None, :], params, view_index) for view_index in range(3)]
    mixed_mid = cross(encoded[1], encoded[0], view_ids[1][:, None] == view_ids[0][None, :], params, 0)
    mixed_coarse = cross(encoded[2], encoded[1], view_ids[2][:, None] == view_ids[1][None, :], params, 1)
    return (encoded[0], mixed_mid, mixed_coarse)

def reference(view_fine, view_mid, view_coarse, grad_fine, grad_mid, grad_coarse, clip_ids, attn_in, attn_out, mlp_w, cross_in, cross_out, norm_gains, biases, ffn_bias):
    params = tuple((weight.astype(jnp.float32) for weight in (attn_in, attn_out, mlp_w, cross_in, cross_out, norm_gains, biases, ffn_bias)))
    inputs = tuple((tokens.astype(jnp.float32) for tokens in (view_fine, view_mid, view_coarse)))
    cotangents = tuple((tokens.astype(jnp.float32) for tokens in (grad_fine, grad_mid, grad_coarse)))

    def per_row(totals, row_data):
        row_inputs, row_cotangents, row_ids = row_data
        outputs, pullback = jax.vjp(lambda values_in, weights_in: layer(values_in, weights_in, row_ids), row_inputs, params)
        input_grads, weight_grads = pullback(row_cotangents)
        return (jax.tree.map(jnp.add, totals, weight_grads), (outputs, input_grads))
    zero_sums = tuple((jnp.zeros_like(weight) for weight in params))
    totals, (outputs, input_grads) = lax.scan(per_row, zero_sums, (inputs, cotangents, clip_ids))
    return (outputs[0].astype(jnp.bfloat16), outputs[1].astype(jnp.bfloat16), outputs[2].astype(jnp.bfloat16), input_grads[0], input_grads[1], input_grads[2], totals[0], totals[1], totals[2], totals[3], totals[4], totals[5], totals[6], totals[7])
```

```python
import math

import jax
import jax.numpy as jnp
from jax import lax
from jax.experimental import pallas as pl
from jax.experimental.pallas import tpu as pltpu
from jax.sharding import Mesh, PartitionSpec as P

D = 768
HEADS = 12
HD = 64
VIEWS = 3
EPS = 1e-06
NEG = -1e30
SCALE = HD**-0.5
BF = jnp.bfloat16
F32 = jnp.float32


def mm(a, b):
    return lax.dot_general(a, b, (((1,), (0,)), ((), ())), preferred_element_type=F32)


def mm_nt(a, b):
    return lax.dot_general(a, b, (((1,), (1,)), ((), ())), preferred_element_type=F32)


def mm_tn(a, b):
    return lax.dot_general(a, b, (((0,), (0,)), ((), ())), preferred_element_type=F32)


def unit_rows(u):
    centre = jnp.mean(u, axis=-1, keepdims=True)
    spread = u - centre
    rs = lax.rsqrt(jnp.mean(spread * spread, axis=-1, keepdims=True) + EPS)
    return spread * rs, rs


def unit_back(z, rs, dz):
    return rs * (
        dz - jnp.mean(dz, axis=-1, keepdims=True) - z * jnp.mean(dz * z, axis=-1, keepdims=True)
    )


def gelu_parts(u):
    phi = 0.5 * lax.erfc(u * (-(0.5**0.5)))
    return phi


def gelu_slope(u):
    return gelu_parts(u) + u * jnp.exp(-0.5 * u * u) * (1.0 / math.sqrt(2.0 * math.pi))


def rounds_of(moves):
    rounds = []
    for move in moves:
        for group in rounds:
            if all(move[0] != other[0] and move[1] != other[1] for other in group):
                group.append(move)
                break
        else:
            rounds.append([move])
    return rounds


def attend_kernel(heads, parts, idq_ref, idk_ref, q_ref, *rest):
    kv_refs, (o_ref, lse_ref) = rest[: 2 * parts], rest[2 * parts :]
    tq = q_ref.shape[0] * q_ref.shape[2]
    wide = q_ref.shape[3]
    q = q_ref[...].reshape(tq, wide)
    ks = [r[...].reshape(-1, wide) for r in kv_refs[:parts]]
    vs = [r[...].reshape(-1, wide) for r in kv_refs[parts:]]
    k = jnp.concatenate(ks, axis=0)
    v = jnp.concatenate(vs, axis=0)
    allowed = idk_ref[0] == idq_ref[0]
    outs = []
    for n in range(heads):
        cols = slice(n * HD, (n + 1) * HD)
        s = jnp.where(allowed, mm_nt(k[:, cols], q[:, cols]) * SCALE, NEG)
        top = jnp.max(s, axis=0, keepdims=True)
        p = jnp.exp(s - top)
        total = jnp.sum(p, axis=0, keepdims=True)
        lse_ref[0, n : n + 1, :] = top + jnp.log(total)
        pb = (p * (1.0 / total)).astype(BF)
        outs.append(mm(v[:, cols].T, pb).T)
    o_ref[...] = jnp.concatenate(outs, axis=1).astype(BF).reshape(o_ref.shape)


def back_kernel(heads, parts, fused, idq_ref, idk_ref, q_ref, do_ref, *rest):
    if fused:
        kv_refs, outs_refs = rest[: 2 * parts], rest[2 * parts :]
        o_ref, dq_ref = outs_refs[:2]
        dkv_refs = outs_refs[2:]
    else:
        lse_ref = rest[0]
        kv_refs, outs_refs = rest[1 : 1 + 2 * parts], rest[1 + 2 * parts :]
        dq_ref = outs_refs[0]
        dkv_refs = outs_refs[1:]
    tq = q_ref.shape[0] * q_ref.shape[2]
    wide = q_ref.shape[3]
    q = q_ref[...].reshape(tq, wide)
    do = do_ref[...].reshape(tq, wide)
    k = jnp.concatenate([r[...].reshape(-1, wide) for r in kv_refs[:parts]], axis=0)
    v = jnp.concatenate([r[...].reshape(-1, wide) for r in kv_refs[parts:]], axis=0)
    tk = k.shape[0] // parts
    allowed = idk_ref[0] == idq_ref[0]
    os, dqs, dks, dvs = [], [], [], []
    for n in range(heads):
        cols = slice(n * HD, (n + 1) * HD)
        qn, kn, vn, gn = q[:, cols], k[:, cols], v[:, cols], do[:, cols]
        s = jnp.where(allowed, mm_nt(kn, qn) * SCALE, NEG)
        if fused:
            top = jnp.max(s, axis=0, keepdims=True)
            e = jnp.exp(s - top)
            p = e * (1.0 / jnp.sum(e, axis=0, keepdims=True))
        else:
            p = jnp.exp(s - lse_ref[0, n : n + 1, :])
        pb = p.astype(BF)
        if fused:
            os.append(mm(vn.T, pb).T)
        dp = mm_nt(vn, gn)
        delta = jnp.sum(p * dp, axis=0, keepdims=True)
        ds = (p * (dp - delta)).astype(BF)
        dqs.append(mm(kn.T, ds).T * SCALE)
        dks.append(mm(ds, qn) * SCALE)
        dvs.append(mm(pb, gn))
    if fused:
        o_ref[...] = jnp.concatenate(os, axis=1).astype(BF).reshape(o_ref.shape)
    dq_ref[...] = jnp.concatenate(dqs, axis=1).astype(BF).reshape(dq_ref.shape)
    dk = jnp.concatenate(dks, axis=1).astype(BF)
    dv = jnp.concatenate(dvs, axis=1).astype(BF)
    for n in range(parts):
        dkv_refs[n][...] = dk[n * tk : (n + 1) * tk].reshape(dkv_refs[n].shape)
        dkv_refs[parts + n][...] = dv[n * tk : (n + 1) * tk].reshape(dkv_refs[parts + n].shape)


def half_spec(a):
    return pl.BlockSpec((a.shape[0], 1) + a.shape[2:], lambda h: (0, h, 0, 0))


def id_spec(a):
    return pl.BlockSpec((1,) + a.shape[1:], lambda h: (h, 0, 0))


def sds(a, dtype=None):
    return jax.ShapeDtypeStruct(a.shape, dtype or a.dtype)


def attention(name, kernel, ins, specs, outs, out_specs, flops, trans):
    nbytes = sum(a.size * a.dtype.itemsize for a in ins)
    return pl.pallas_call(
        kernel,
        grid=(2,),
        in_specs=specs,
        out_specs=out_specs,
        out_shape=outs,
        name=name,
        compiler_params=pltpu.CompilerParams(vmem_limit_bytes=48 * 1024 * 1024),
        cost_estimate=pl.CostEstimate(
            flops=flops, bytes_accessed=2 * nbytes, transcendentals=trans
        ),
    )(*ins)


def attend(heads, idq, idk, q, ks, vs):
    parts = len(ks)
    kernel = lambda *refs: attend_kernel(heads, parts, *refs)
    ins = [idq, idk, q, *ks, *vs]
    specs = [id_spec(idq), id_spec(idk)] + [half_spec(a) for a in ins[2:]]
    lse = jax.ShapeDtypeStruct((2, 8, idq.shape[2]), F32)
    pairs = 2 * heads * idq.shape[2] * idk.shape[1]
    return attention(
        "attend", kernel, ins, specs, [sds(q), lse], [half_spec(q), id_spec(lse)],
        4 * pairs * HD, pairs,
    )


def attend_back(heads, idq, idk, q, do, lse, ks, vs):
    parts = len(ks)
    kernel = lambda *refs: back_kernel(heads, parts, False, *refs)
    ins = [idq, idk, q, do, lse, *ks, *vs]
    specs = [id_spec(idq), id_spec(idk), half_spec(q), half_spec(do), id_spec(lse)]
    specs += [half_spec(a) for a in ins[5:]]
    outs = [sds(q)] + [sds(a) for a in ks] + [sds(a) for a in vs]
    pairs = 2 * heads * idq.shape[2] * idk.shape[1]
    res = attention(
        "attend_back", kernel, ins, specs, outs, [half_spec(a) for a in outs],
        10 * pairs * HD, pairs,
    )
    return res[0], res[1 : 1 + parts], res[1 + parts :]


def attend_both(heads, idq, idk, q, do, ks, vs):
    parts = len(ks)
    kernel = lambda *refs: back_kernel(heads, parts, True, *refs)
    ins = [idq, idk, q, do, *ks, *vs]
    specs = [id_spec(idq), id_spec(idk)] + [half_spec(a) for a in ins[2:]]
    outs = [sds(q), sds(q)] + [sds(a) for a in ks] + [sds(a) for a in vs]
    pairs = 2 * heads * idq.shape[2] * idk.shape[1]
    res = attention(
        "attend_both", kernel, ins, specs, outs, [half_spec(a) for a in outs],
        12 * pairs * HD, pairs,
    )
    return res[0], res[1], res[2 : 2 + parts], res[2 + parts :]


def solution(mesh):
    dp, seq = mesh.shape["dp"], mesh.shape["seq"]
    G = math.gcd(HEADS, seq)
    while G & (G - 1) or (seq // G) & (seq // G - 1):
        G //= 2
    J = seq // G
    heads = HEADS // G
    wide = heads * HD
    nf, nm = dp // 2, dp // 4
    mesh3 = Mesh(mesh.devices.reshape(dp, G, J), ("dp", "g", "j"))
    everyone = ("dp", "g", "j")

    view_of = [0 if d < nf else (1 if d < nf + nm else 2) for d in range(dp)]
    owner = [
        [r // 2 for r in range(dp)],
        [nf + r // 4 for r in range(dp)],
        [nf + nm + r // 4 for r in range(dp)],
    ]
    slot = [[r % 2 for r in range(dp)], [r % 4 for r in range(dp)], [r % 4 for r in range(dp)]]

    def xor(axis, n, size, x):
        return lax.ppermute(x, axis, [(i, i ^ n) for i in range(size)])

    def per_device(
        view_fine, view_mid, view_coarse, grad_fine, grad_mid, grad_coarse, clip_ids,
        attn_in, attn_out, mlp_w, cross_in, cross_out, norm_gains, biases, ffn_bias,
    ):
        tf, tm, tc = view_fine.shape[1], view_mid.shape[1], view_coarse.shape[1]
        U = 2 * tf
        ff = mlp_w.shape[1]
        cells = clip_ids.shape[1]
        d, g, j = lax.axis_index("dp"), lax.axis_index("g"), lax.axis_index("j")
        v = jnp.where(d < nf, 0, jnp.where(d < nf + nm, 1, 2))
        p = jnp.where(d < nf, 0, 1)

        def table(values, index=d):
            out = jnp.int32(values[-1])
            for i in range(len(values) - 1):
                out = jnp.where(index == i, jnp.int32(values[i]), out)
            return out

        def pick(tag, options, dtype=None):
            out = jnp.zeros_like(options[0])
            for k, option in enumerate(options):
                out = jnp.where(tag == k, option, out)
            return out

        def rows_at(x, start, size):
            return lax.dynamic_slice_in_dim(x, start, size, axis=0)

        sizes = (tf, tm, tc)
        moves = [
            (r, owner[w][r], (w, r))
            for w in range(VIEWS)
            for r in range(dp)
            if r != owner[w][r]
        ]
        view_rounds = rounds_of(moves)

        def grow(x, rows):
            if x.shape[0] == rows:
                return x
            return jnp.concatenate([x, jnp.zeros((rows - x.shape[0], x.shape[1]), x.dtype)], axis=0)

        def to_views(fine, mid, coarse):
            mid_p, coarse_p = grow(mid, tf), grow(coarse, tf)
            got = []
            for group in view_rounds:
                n = max(sizes[w] for _, _, (w, _) in group)
                kind = [3] * dp
                for src, _, (w, _) in group:
                    kind[src] = w
                load = pick(table(kind), [fine[:n], mid_p[:n], coarse_p[:n]])
                got.append(grow(lax.ppermute(load, "dp", [(s, t) for s, t, _ in group]), tf))
            local = pick(v, [fine, mid_p, coarse_p])
            rows = []
            for k in range(4):
                tag = [len(got) + 1] * dp
                for i, group in enumerate(view_rounds):
                    for _, dst, (w, r) in group:
                        if slot[w][r] == k:
                            tag[dst] = i + 1
                for r in range(dp):
                    if owner[view_of[r]][r] == r and slot[view_of[r]][r] == k:
                        tag[r] = 0
                rows.append(pick(table(tag), [local] + got))
            as_fine = jnp.concatenate(rows[:2], axis=0)
            as_mid = jnp.concatenate([x[:tm] for x in rows], axis=0)
            pad = jnp.zeros((tf - 2 * tc, fine.shape[1]), fine.dtype)
            as_coarse = jnp.concatenate(
                [rows[0][:tc], rows[1][:tc], pad, rows[2][:tc], rows[3][:tc], pad], axis=0
            )
            return pick(v, [as_fine, as_mid, as_coarse])

        def place(w, k):
            return (tf * k, tm * k, tf * (k // 2) + tc * (k % 2))[w]

        def from_views(x):
            padded = grow(x, U + tf)
            got = []
            for group in view_rounds:
                n = max(sizes[w] for _, _, (w, _) in group)
                start = [0] * dp
                for _, src, (w, r) in group:
                    start[src] = place(w, slot[w][r])
                load = rows_at(padded, table(start), n)
                got.append(grow(lax.ppermute(load, "dp", [(t, s) for s, t, _ in group]), tf))
            local_start = [0] * dp
            for r in range(dp):
                w = view_of[r]
                if owner[w][r] == r:
                    local_start[r] = place(w, slot[w][r])
            local = rows_at(padded, table(local_start), tf)
            outs = []
            for w in range(VIEWS):
                tag = [0] * dp
                for i, group in enumerate(view_rounds):
                    for _, dst, (w2, r) in group:
                        if w2 == w:
                            tag[r] = i + 1
                outs.append(pick(table(tag), [local] + got)[: sizes[w]])
            return outs

        def half_moves(src_of):
            return [(src, dst, h) for dst, (src, h) in src_of.items()]

        q_src = {}
        k_src = {}
        for dst in range(dp):
            if dst < nf:
                q_src[dst] = (nf + (2 * dst) // 4, dst % 2)
            else:
                i = dst - nf
                q_src[dst] = (nf + nm + (2 * i) // 4, i % 2)
                k_src[dst] = (nf + (2 * i) // 4, i % 2)

        def to_cross(x, src_of):
            groups = rounds_of([m for m in half_moves(src_of) if m[0] != m[1]])
            got = []
            for group in groups:
                start = [0] * dp
                for src, _, h in group:
                    start[src] = h * tf
                got.append(
                    lax.ppermute(
                        rows_at(x, table(start), tf), "dp", [(s, t) for s, t, _ in group]
                    )
                )
            start = [0] * dp
            tag = [len(got) + 1] * dp
            for dst, (src, h) in src_of.items():
                if src == dst:
                    start[dst], tag[dst] = h * tf, 0
            for i, group in enumerate(groups):
                for _, dst, _ in group:
                    tag[dst] = i + 1
            return pick(table(tag), [rows_at(x, table(start), tf)] + got)

        def from_cross(x, src_of):
            groups = rounds_of([m for m in half_moves(src_of) if m[0] != m[1]])
            got = [
                lax.ppermute(x, "dp", [(t, s) for s, t, _ in group]) for group in groups
            ]
            halves = []
            for half in range(2):
                tag = [len(got) + 1] * dp
                for dst, (src, h) in src_of.items():
                    if h == half:
                        if src == dst:
                            tag[src] = 0
                        else:
                            for i, group in enumerate(groups):
                                if any(m[1] == dst for m in group):
                                    tag[src] = i + 1
                halves.append(pick(table(tag), [x] + got))
            return jnp.concatenate(halves, axis=0)

        def zeros(rows, like):
            return jnp.zeros((rows, like.shape[1]), like.dtype)

        def q_spread(x):
            z = zeros(tm - tc, x)
            return jnp.where(
                p == 0, x, jnp.concatenate([x[:tc], z, x[tc : 2 * tc], z], axis=0)
            )

        def q_gather(x):
            z = zeros(tf - 2 * tc, x)
            return jnp.where(
                p == 0, x, jnp.concatenate([x[:tc], x[tm : tm + tc], z], axis=0)
            )

        def k_spread(x):
            z = zeros(tf - tm, x)
            return jnp.concatenate([x[:tm], z, x[tm : 2 * tm], z], axis=0)

        def k_gather(x):
            return jnp.concatenate([x[:tm], x[tf : tf + tm]], axis=0)

        def spread_g(x):
            return [x] + [xor("g", m, G, x) for m in range(1, G)]

        def sum_g(pieces):
            out = pieces[0].astype(F32)
            got = [xor("g", m, G, pieces[m].astype(BF)) for m in range(1, G)]
            for x in got:
                out = out + x.astype(F32)
            return out

        def spread_j(x):
            return [x] + [xor("j", n, J, x) for n in range(1, J)]

        n_dev = dp * seq
        vec = jnp.concatenate(
            [
                norm_gains.reshape(-1), biases.reshape(-1), ffn_bias.reshape(-1),
                clip_ids.astype(BF).reshape(-1),
            ]
        )
        vec = jnp.broadcast_to(vec[None], (n_dev, vec.shape[0]))
        vecs = lax.all_to_all(vec, everyone, 0, 0, tiled=True)
        gw, bw, fw = norm_gains.shape[1], biases.shape[1], ffn_bias.shape[1]

        def unpack(start, rows, width):
            part = vecs[:, start : start + rows * width].astype(F32)
            return part.reshape(n_dev, rows, width).transpose(1, 0, 2).reshape(rows, n_dev * width)

        gains = unpack(0, 10, gw)
        vectors = unpack(10 * gw, 28, bw)
        ffn_rows = unpack(10 * gw + 28 * bw, 3, fw)
        ids_at = 10 * gw + 28 * bw + 3 * fw
        ids_all = vecs.reshape(dp, seq, -1)[:, 0, ids_at : ids_at + cells].astype(F32)

        enc_gain = pick(v, [gains[2 * i : 2 * i + 2] for i in range(3)])
        enc_bias = pick(v, [vectors[6 * i : 6 * i + 6] for i in range(3)])
        g1, g2 = enc_gain[0], enc_gain[1]
        n1, bq, bv, bo, n2, bm = [enc_bias[i] for i in range(6)]
        bf_row = pick(v, [ffn_rows[i] for i in range(3)])
        gq = pick(v, [gains[6], gains[6], gains[8]])
        gk = pick(v, [gains[7], gains[9], gains[9]])
        nq = pick(v, [vectors[18], vectors[18], vectors[23]])
        nk = pick(v, [vectors[19], vectors[24], vectors[24]])
        cq, cv, co = [jnp.where(p == 0, vectors[20 + i], vectors[25 + i]) for i in range(3)]

        def cols(x, width):
            return lax.dynamic_slice_in_dim(x, g * width, width, axis=-1)

        before = jnp.stack(
            [jnp.sum((ids_all < c).astype(F32), axis=1) for c in (1, 2, 3)], axis=1
        ).astype(jnp.int32)
        before = jnp.concatenate([before, jnp.zeros((4, 3), jnp.int32)], axis=0)
        s_grid = (
            (g ^ jnp.arange(G, dtype=jnp.int32))[None, :, None] * J
            + (j ^ jnp.arange(J, dtype=jnp.int32))[:, None, None]
        )

        def id_of(cell, starts):
            return sum((cell >= starts[..., c]).astype(jnp.int32) for c in range(3))

        u = jnp.arange(tf, dtype=jnp.int32)[None, None, :]
        base = table([2 * x if x < nf else 4 * ((x - nf) % nm) for x in range(dp)])
        view_starts = rows_at(before, base, 4)

        def view_ids(h):
            is_fine, is_mid = v == 0, v == 1
            unit = jnp.where(is_fine, tf, jnp.where(is_mid, tm, tc))
            second = (u >= unit) & ~is_fine
            first_row = jnp.where(is_fine, h, 2 * h)
            a = rows_at(view_starts, first_row, 1)[0]
            b = rows_at(view_starts, 2 * h + 1, 1)[0]
            starts = jnp.where(second[..., None], b, a)
            pos = s_grid * unit + u - jnp.where(second, unit, 0)
            cell = pos // jnp.where(is_fine, 4, jnp.where(is_mid, 2, 1))
            ids = id_of(cell, starts) + jnp.where(second, 4, 0)
            return jnp.where((u >= 2 * unit) & ~is_fine, -1, ids)

        def cross_ids(h, unit0, unit1, div0, div1, length):
            w = u[..., :length]
            a = rows_at(before, 2 * jnp.where(p == 0, d, d - nf) + h, 1)[0]
            unit = jnp.where(p == 0, unit0, unit1)
            cell = (s_grid * unit + w) // jnp.where(p == 0, div0, div1)
            return jnp.where(w >= unit, -1, id_of(cell, a))

        def as_q(ids):
            return jnp.stack([x[0].reshape(1, -1) for x in ids])

        def as_k(ids):
            return jnp.stack([x.reshape(-1, 1) for x in ids])

        self_ids = [view_ids(h) for h in range(2)]
        idq, idk = as_q(self_ids), as_k(self_ids)
        cross_idq = as_q([cross_ids(h, tm, tc, 2, 1, tm) for h in range(2)])
        cross_idk = as_k([cross_ids(h, tf, tm, 4, 2, tf) for h in range(2)])

        near = dp == 4

        def both_sides(x):
            up = lax.ppermute(x, "dp", [(0, 1), (1, 2), (2, 3)])
            down = lax.ppermute(x, "dp", [(1, 0), (3, 2)])
            return up, down

        def chunks(x):
            if near:
                up, down = both_sides(x)
                enc = jnp.stack([jnp.where(d == 0, x, up), jnp.where(d == 0, down, x)])
                odd = d % 2 == 1
                cross = jnp.stack([jnp.where(odd, up, x), jnp.where(odd, x, down)])
                return enc, cross
            everything = lax.all_gather(x, "dp", axis=0)
            return everything, everything

        enc_lo = jnp.maximum(d - 1, 0) if near else jnp.int32(0)
        cross_lo = 2 * p if near else jnp.int32(0)

        def start_of(part, n_parts, low, total):
            return part * (total // n_parts) - low * (total // dp)

        def join_j(x):
            xs = spread_j(x)
            parts = []
            for a in range(J):
                out = xs[0]
                for n in range(1, J):
                    out = jnp.where((j ^ n) == a, xs[n], out)
                parts.append(out)
            full = jnp.stack(parts, axis=2)
            return full.reshape(-1, x.shape[-1])

        r_in, r_cross = attn_in.shape[0], cross_in.shape[0]
        qkv = lax.all_to_all(
            jnp.concatenate([attn_in, cross_in], axis=0), "g", 1, 0, tiled=True
        ).reshape(G, r_in + r_cross, wide)
        hid = ff // G
        mlp = lax.all_to_all(mlp_w, "g", 1, 0, tiled=True).reshape(G, mlp_w.shape[0], hid)

        enc_c, cross_c = chunks(qkv)
        w_in = rows_at(
            join_j(enc_c[:, :, :r_in]), start_of(v, 3, enc_lo, n_dev * r_in), 3 * D
        )
        c_in = rows_at(
            join_j(cross_c[:, :, r_in:]), start_of(p, 2, cross_lo, n_dev * r_cross), 3 * D
        )
        enc_c, _ = chunks(mlp)
        w_mlp = rows_at(
            join_j(enc_c), start_of(v, 3, enc_lo, n_dev * mlp_w.shape[0]), 2 * D
        )
        r_out, r_co = attn_out.shape[0], cross_out.shape[0]
        enc_c, cross_c = chunks(jnp.concatenate([attn_out, cross_out], axis=0))
        planes = enc_c.shape[0]
        outs = jnp.concatenate([enc_c[:, :r_out], cross_c[:, r_out:]], axis=1)
        outs = lax.all_gather(outs.reshape(-1, D), ("g", "j"), axis=0)
        outs = outs.reshape(seq, planes, r_out + r_co, D).transpose(1, 0, 2, 3)
        w_out = rows_at(
            outs[:, :, :r_out].reshape(-1, D), start_of(v, 3, enc_lo, n_dev * r_out), D
        )
        c_out = rows_at(
            outs[:, :, r_out:].reshape(-1, D), start_of(p, 2, cross_lo, n_dev * r_co), D
        )

        def by_head_group(w):
            return jnp.concatenate([rows_at(w, (g ^ m) * wide, wide) for m in range(G)], axis=0)

        w_out, c_out = by_head_group(w_out), by_head_group(c_out)
        wq, wk, wv = w_in[:D], w_in[D : 2 * D], w_in[2 * D :]
        ccq, cck, ccv = c_in[:D], c_in[D : 2 * D], c_in[2 * D :]
        w1, w2 = w_mlp[:D], w_mlp[D:]

        x_own = to_views(view_fine[0], view_mid[0], view_coarse[0])
        grad_own = to_views(grad_fine[0], grad_mid[0], grad_coarse[0])
        x = jnp.concatenate(spread_g(x_own), axis=0).astype(F32)
        a = (unit_rows(x)[0] * g1 + n1).astype(BF)
        q = (mm(a, wq) + cols(bq, wide)).astype(BF)
        k = mm(a, wk).astype(BF)
        w = (mm(a, wv) + cols(bv, wide)).astype(BF)

        def halves(t, width=None):
            return t.reshape(G, 2, -1, t.shape[-1])

        kv = spread_j(jnp.concatenate([k, w], axis=1))
        ks = [halves(t[:, :wide]) for t in kv]
        vs = [halves(t[:, wide:]) for t in kv]
        o, lse = attend(heads, idq, idk, halves(q), ks, vs)

        def all_heads(t):
            t = t.reshape(G, -1, wide)
            got = [t]
            for m in range(1, G):
                r = xor("g", m, G, t)
                got.append(jnp.stack([r[i ^ m] for i in range(G)]))
            return jnp.concatenate(got, axis=2).reshape(-1, G * wide)

        o_all = all_heads(o)
        h = x + (mm(o_all, w_out) + bo)
        zh, _ = unit_rows(h)
        c = (zh * g2 + n2).astype(BF)
        up = mm(c, w1) + cols(bf_row, hid)
        e = (up * gelu_parts(up)).astype(BF)
        y_part = mm_nt(e, w2).reshape(G, U, D)
        h_own = h[:U]
        y = sum_g([y_part[m] for m in range(G)]) + h_own + bm

        zy, rs_y = unit_rows(y)
        kn_v = (zy * gk + nk).astype(BF)
        qn_v = (zy * gq + nq).astype(BF)
        kn_own = jnp.where(p == 0, kn_v, k_spread(to_cross(kn_v, k_src)))
        qn_own = q_spread(to_cross(qn_v, q_src))
        gq_own = q_spread(to_cross(grad_own, q_src))
        kn = jnp.concatenate(spread_g(kn_own), axis=0)
        qn = jnp.concatenate(spread_g(qn_own), axis=0)
        gc = jnp.concatenate(spread_g(gq_own), axis=0)
        cross_q = (mm(qn, ccq) + cols(cq, wide)).astype(BF)
        cross_k = mm(kn, cck).astype(BF)
        cross_v = (mm(kn, ccv) + cols(cv, wide)).astype(BF)
        d_att = mm_nt(gc, c_out[:wide]).astype(BF)
        kv = spread_j(jnp.concatenate([cross_k, cross_v], axis=1))
        cks = [halves(t[:, :wide]) for t in kv]
        cvs = [halves(t[:, wide:]) for t in kv]
        co_att, dq_c, dks, dvs = attend_both(
            heads, cross_idq, cross_idk, halves(cross_q), halves(d_att), cks, cvs
        )

        def home_j(ts):
            out = ts[0].astype(F32)
            for n in range(1, J):
                out = out + xor("j", n, J, ts[n]).astype(F32)
            return out

        def home_kv(dks, dvs):
            both = home_j([jnp.concatenate([a, b], axis=3) for a, b in zip(dks, dvs)])
            both = both.astype(BF).reshape(-1, 2 * wide)
            return both[:, :wide], both[:, wide:]

        dk_c, dv_c = home_kv(dks, dvs)
        dq_c = dq_c.reshape(-1, wide)
        cross_o = all_heads(co_att)
        Uq = 2 * tm
        mix = mm(cross_o[:Uq], c_out) + co
        mix_v = from_cross(q_gather(mix.astype(BF)), q_src).astype(F32)

        dqn_part = mm_nt(dq_c, ccq).reshape(G, Uq, D)
        dqn = sum_g([dqn_part[m] for m in range(G)]).astype(BF)
        dkn_part = (mm_nt(dk_c, cck) + mm_nt(dv_c, ccv)).reshape(G, U, D)
        dkn = sum_g([dkn_part[m] for m in range(G)]).astype(BF)
        dqn_v = from_cross(q_gather(dqn), q_src).astype(F32)
        dkn_v = jnp.where(v == 0, dkn, from_cross(k_gather(dkn), k_src)).astype(F32)
        dqn_v = jnp.where(v == 0, 0.0, dqn_v)
        mix_v = jnp.where(v == 0, 0.0, mix_v)
        dkn_v = jnp.where(v == 2, 0.0, dkn_v)
        dy = grad_own.astype(F32) + unit_back(zy, rs_y, dqn_v * gq + dkn_v * gk)

        dm_own = dy.astype(BF)
        dm = jnp.concatenate(spread_g(dm_own), axis=0)
        de = mm(dm, w2)
        du = (de * gelu_slope(up)).astype(BF)
        dc_part = mm_nt(du, w1).reshape(G, U, D)
        dn2 = sum_g([dc_part[m] for m in range(G)])
        zh_own, rs_h = unit_rows(h_own)
        dh = dy + unit_back(zh_own, rs_h, dn2 * g2)
        dh_own = dh.astype(BF)
        dh_all = jnp.concatenate(spread_g(dh_own), axis=0)
        d_o = mm_nt(dh_all, w_out[:wide]).astype(BF)
        dq, dks, dvs = attend_back(heads, idq, idk, halves(q), halves(d_o), lse, ks, vs)
        dk, dv = home_kv(dks, dvs)
        dq = dq.reshape(-1, wide)
        da_part = (mm_nt(dq, wq) + mm_nt(dk, wk) + mm_nt(dv, wv)).reshape(G, U, D)
        da = sum_g([da_part[m] for m in range(G)])
        zx, rs_x = unit_rows(x_own.astype(F32))
        dx = dh + unit_back(zx, rs_x, da * g1)

        out_f, out_m, out_c = from_views((y + mix_v).astype(BF))
        dx_f, dx_m, dx_c = from_views(dx.astype(BF))

        def my_rows(x):
            return lax.dynamic_index_in_dim(x, j, axis=2, keepdims=False)

        def send_home(grad, total, enc):
            width = grad.shape[1]
            r = total // n_dev
            if near:
                frame_rows, n_planes = total // 2, 2
                low = enc_lo if enc else cross_lo
            else:
                frame_rows, n_planes, low = total, dp, jnp.int32(0)
            if grad.shape[0] != frame_rows:
                part, n_parts = (v, 3) if enc else (p, 2)
                grad = lax.dynamic_update_slice_in_dim(
                    jnp.zeros((frame_rows, width), BF), grad.astype(BF),
                    start_of(part, n_parts, low, total), axis=0,
                )
            x = grad.astype(BF).reshape(n_planes, G, J, r, width)
            acc = lax.dynamic_index_in_dim(x, j, axis=2, keepdims=False).astype(F32)
            for n in range(1, J):
                part = lax.dynamic_index_in_dim(x, j ^ n, axis=2, keepdims=False)
                acc = acc + xor("j", n, J, part).astype(F32)
            if not near:
                acc = lax.psum_scatter(acc, "dp", scatter_dimension=0, tiled=False)
            elif enc:
                own = jnp.where(d == 0, acc[0], acc[1])
                other = jnp.where(d == 0, acc[1], acc[0]).astype(BF)
                down = lax.ppermute(other, "dp", [(1, 0), (2, 1), (3, 2)])
                upward = lax.ppermute(other, "dp", [(0, 1)])
                acc = own + down.astype(F32) + upward.astype(F32)
            else:
                odd = d % 2 == 1
                own = jnp.where(odd, acc[1], acc[0])
                other = jnp.where(odd, acc[0], acc[1]).astype(BF)
                acc = own + xor("dp", 1, dp, other).astype(F32)
            acc = acc.astype(BF).reshape(G * r, width)
            return lax.all_to_all(acc, "g", 0, 1, tiled=True).astype(F32)

        def in_order(w):
            return jnp.concatenate(
                [rows_at(w, (g ^ a) * wide, wide) for a in range(G)], axis=0
            )

        g_cin = jnp.concatenate([mm_tn(qn, dq_c), mm_tn(kn, dk_c), mm_tn(kn, dv_c)], axis=0)
        g_cout = in_order(mm_tn(cross_o, cols(gc, wide)))
        g_mlp = jnp.concatenate([mm_tn(c, du), mm_tn(dm, e)], axis=0)
        g_out = in_order(mm_tn(o_all, cols(dh_all, wide)))
        g_in = jnp.concatenate([mm_tn(a, dq), mm_tn(a, dk), mm_tn(a, dv)], axis=0)
        grad_cin = send_home(g_cin, n_dev * r_cross, False)
        grad_cout = send_home(g_cout, n_dev * r_co, False)
        grad_mlp = send_home(g_mlp, n_dev * mlp_w.shape[0], True)
        grad_out = send_home(g_out, n_dev * r_out, True)
        grad_in = send_home(g_in, n_dev * r_in, True)

        def total(x):
            return jnp.sum(x.astype(F32), axis=0)

        def at_cols(x):
            hot = (jnp.arange(G) == g).astype(F32)
            return (hot[:, None] * x[None]).reshape(-1)

        def at_row(x, index, n):
            hot = (jnp.arange(n) == index).astype(F32)
            return hot.reshape((n,) + (1,) * x.ndim) * x[None]

        enc_g = jnp.stack([total(da * zx), total(dn2 * zh_own)])
        enc_b = jnp.stack(
            [
                total(da), at_cols(total(dq)), at_cols(total(dv)), total(dh_own), total(dn2),
                total(dm_own),
            ]
        )
        q_role = at_row(jnp.stack([total(dqn_v * zy), total(dqn_v), total(grad_own)]), v - 1, 2)
        k_role = at_row(jnp.stack([total(dkn_v * zy), total(dkn_v)]), v, 2)
        pair = at_row(jnp.stack([at_cols(total(dq_c)), at_cols(total(dv_c))]), p, 2)
        gains_g = jnp.concatenate(
            [
                at_row(enc_g, v, 3).reshape(6, D),
                jnp.stack([q_role[:, 0], k_role[:, 0]], axis=1).reshape(4, D),
            ]
        )
        cross_b = jnp.stack(
            [q_role[:, 1], k_role[:, 1], pair[:, 0], pair[:, 1], q_role[:, 2]], axis=1
        )
        bias_g = jnp.concatenate([at_row(enc_b, v, 3).reshape(18, D), cross_b.reshape(10, D)])
        ffn_g = at_row(at_cols(total(du)), v, 3)

        def split(x):
            n = x.shape[0]
            return x.reshape(n, n_dev, -1).transpose(1, 0, 2).reshape(n_dev, -1)

        small = jnp.concatenate([split(gains_g), split(bias_g), split(ffn_g)], axis=1)
        small = jnp.sum(lax.all_to_all(small, everyone, 0, 0, tiled=True), axis=0)
        n_g, n_b = 10 * gw, 28 * bw
        return (
            out_f[None], out_m[None], out_c[None],
            dx_f.astype(F32)[None], dx_m.astype(F32)[None], dx_c.astype(F32)[None],
            grad_in, grad_out, grad_mlp, grad_cin, grad_cout,
            small[:n_g].reshape(10, gw),
            small[n_g : n_g + n_b].reshape(28, bw),
            small[n_g + n_b :].reshape(3, fw),
        )

    tokens = P("dp", ("g", "j"), None)
    rows = P(everyone, None)
    columns = P(None, everyone)
    return jax.shard_map(
        per_device,
        mesh=mesh3,
        in_specs=(tokens,) * 6 + (P("dp", None),) + (rows,) * 5 + (columns,) * 3,
        out_specs=(tokens,) * 6 + (rows,) * 5 + (columns,) * 3,
        check_vma=False,
    )
```

```python
import math

import jax
import jax.numpy as jnp
from jax import lax
from jax.experimental import pallas as pl
from jax.experimental.pallas import tpu as pltpu
from jax.sharding import Mesh, PartitionSpec as P

D = 768
HEADS = 12
HD = 64
VIEWS = 3
EPS = 1e-06
NEG = -1e30
SCALE = HD**-0.5
BF = jnp.bfloat16
F32 = jnp.float32


def mm(a, b):
    return lax.dot_general(a, b, (((1,), (0,)), ((), ())), preferred_element_type=F32)


def mm_nt(a, b):
    return lax.dot_general(a, b, (((1,), (1,)), ((), ())), preferred_element_type=F32)


def mm_tn(a, b):
    return lax.dot_general(a, b, (((0,), (0,)), ((), ())), preferred_element_type=F32)


def unit_rows(u):
    centre = jnp.mean(u, axis=-1, keepdims=True)
    spread = u - centre
    rs = lax.rsqrt(jnp.mean(spread * spread, axis=-1, keepdims=True) + EPS)
    return spread * rs, rs


def unit_back(z, rs, dz):
    return rs * (
        dz - jnp.mean(dz, axis=-1, keepdims=True) - z * jnp.mean(dz * z, axis=-1, keepdims=True)
    )


def gelu_parts(u):
    phi = 0.5 * lax.erfc(u * (-(0.5**0.5)))
    return phi


def gelu_slope(u):
    return gelu_parts(u) + u * jnp.exp(-0.5 * u * u) * (1.0 / math.sqrt(2.0 * math.pi))


def rounds_of(moves):
    rounds = []
    for move in moves:
        for group in rounds:
            if all(move[0] != other[0] and move[1] != other[1] for other in group):
                group.append(move)
                break
        else:
            rounds.append([move])
    return rounds


def attend_kernel(heads, parts, idq_ref, idk_ref, q_ref, *rest):
    kv_refs, (o_ref, lse_ref) = rest[: 2 * parts], rest[2 * parts :]
    tq = q_ref.shape[0] * q_ref.shape[2]
    wide = q_ref.shape[3]
    q = q_ref[...].reshape(tq, wide)
    ks = [r[...].reshape(-1, wide) for r in kv_refs[:parts]]
    vs = [r[...].reshape(-1, wide) for r in kv_refs[parts:]]
    k = jnp.concatenate(ks, axis=0)
    v = jnp.concatenate(vs, axis=0)
    allowed = idk_ref[0] == idq_ref[0]
    outs = []
    for n in range(heads):
        cols = slice(n * HD, (n + 1) * HD)
        s = jnp.where(allowed, mm_nt(k[:, cols], q[:, cols]) * SCALE, NEG)
        top = jnp.max(s, axis=0, keepdims=True)
        p = jnp.exp(s - top)
        total = jnp.sum(p, axis=0, keepdims=True)
        lse_ref[0, n : n + 1, :] = top + jnp.log(total)
        pb = (p * (1.0 / total)).astype(BF)
        outs.append(mm(v[:, cols].T, pb).T)
    o_ref[...] = jnp.concatenate(outs, axis=1).astype(BF).reshape(o_ref.shape)


def back_kernel(heads, parts, fused, idq_ref, idk_ref, q_ref, do_ref, *rest):
    if fused:
        kv_refs, outs_refs = rest[: 2 * parts], rest[2 * parts :]
        o_ref, dq_ref = outs_refs[:2]
        dkv_refs = outs_refs[2:]
    else:
        lse_ref = rest[0]
        kv_refs, outs_refs = rest[1 : 1 + 2 * parts], rest[1 + 2 * parts :]
        dq_ref = outs_refs[0]
        dkv_refs = outs_refs[1:]
    tq = q_ref.shape[0] * q_ref.shape[2]
    wide = q_ref.shape[3]
    q = q_ref[...].reshape(tq, wide)
    do = do_ref[...].reshape(tq, wide)
    k = jnp.concatenate([r[...].reshape(-1, wide) for r in kv_refs[:parts]], axis=0)
    v = jnp.concatenate([r[...].reshape(-1, wide) for r in kv_refs[parts:]], axis=0)
    tk = k.shape[0] // parts
    allowed = idk_ref[0] == idq_ref[0]
    os, dqs, dks, dvs = [], [], [], []
    for n in range(heads):
        cols = slice(n * HD, (n + 1) * HD)
        qn, kn, vn, gn = q[:, cols], k[:, cols], v[:, cols], do[:, cols]
        s = jnp.where(allowed, mm_nt(kn, qn) * SCALE, NEG)
        if fused:
            top = jnp.max(s, axis=0, keepdims=True)
            e = jnp.exp(s - top)
            p = e * (1.0 / jnp.sum(e, axis=0, keepdims=True))
        else:
            p = jnp.exp(s - lse_ref[0, n : n + 1, :])
        pb = p.astype(BF)
        if fused:
            os.append(mm(vn.T, pb).T)
        dp = mm_nt(vn, gn)
        delta = jnp.sum(p * dp, axis=0, keepdims=True)
        ds = (p * (dp - delta)).astype(BF)
        dqs.append(mm(kn.T, ds).T * SCALE)
        dks.append(mm(ds, qn) * SCALE)
        dvs.append(mm(pb, gn))
    if fused:
        o_ref[...] = jnp.concatenate(os, axis=1).astype(BF).reshape(o_ref.shape)
    dq_ref[...] = jnp.concatenate(dqs, axis=1).astype(BF).reshape(dq_ref.shape)
    dk = jnp.concatenate(dks, axis=1).astype(BF)
    dv = jnp.concatenate(dvs, axis=1).astype(BF)
    for n in range(parts):
        dkv_refs[n][...] = dk[n * tk : (n + 1) * tk].reshape(dkv_refs[n].shape)
        dkv_refs[parts + n][...] = dv[n * tk : (n + 1) * tk].reshape(dkv_refs[parts + n].shape)


def half_spec(a):
    return pl.BlockSpec((a.shape[0], 1) + a.shape[2:], lambda h: (0, h, 0, 0))


def id_spec(a):
    return pl.BlockSpec((1,) + a.shape[1:], lambda h: (h, 0, 0))


def sds(a, dtype=None):
    return jax.ShapeDtypeStruct(a.shape, dtype or a.dtype)


def attention(name, kernel, ins, specs, outs, out_specs, flops, trans):
    nbytes = sum(a.size * a.dtype.itemsize for a in ins)
    return pl.pallas_call(
        kernel,
        grid=(2,),
        in_specs=specs,
        out_specs=out_specs,
        out_shape=outs,
        name=name,
        compiler_params=pltpu.CompilerParams(vmem_limit_bytes=48 * 1024 * 1024),
        cost_estimate=pl.CostEstimate(
            flops=flops, bytes_accessed=2 * nbytes, transcendentals=trans
        ),
    )(*ins)


def attend(heads, idq, idk, q, ks, vs):
    parts = len(ks)
    kernel = lambda *refs: attend_kernel(heads, parts, *refs)
    ins = [idq, idk, q, *ks, *vs]
    specs = [id_spec(idq), id_spec(idk)] + [half_spec(a) for a in ins[2:]]
    lse = jax.ShapeDtypeStruct((2, 8, idq.shape[2]), F32)
    pairs = 2 * heads * idq.shape[2] * idk.shape[1]
    return attention(
        "attend", kernel, ins, specs, [sds(q), lse], [half_spec(q), id_spec(lse)],
        4 * pairs * HD, pairs,
    )


def attend_back(heads, idq, idk, q, do, lse, ks, vs):
    parts = len(ks)
    kernel = lambda *refs: back_kernel(heads, parts, False, *refs)
    ins = [idq, idk, q, do, lse, *ks, *vs]
    specs = [id_spec(idq), id_spec(idk), half_spec(q), half_spec(do), id_spec(lse)]
    specs += [half_spec(a) for a in ins[5:]]
    outs = [sds(q)] + [sds(a) for a in ks] + [sds(a) for a in vs]
    pairs = 2 * heads * idq.shape[2] * idk.shape[1]
    res = attention(
        "attend_back", kernel, ins, specs, outs, [half_spec(a) for a in outs],
        10 * pairs * HD, pairs,
    )
    return res[0], res[1 : 1 + parts], res[1 + parts :]


def attend_both(heads, idq, idk, q, do, ks, vs):
    parts = len(ks)
    kernel = lambda *refs: back_kernel(heads, parts, True, *refs)
    ins = [idq, idk, q, do, *ks, *vs]
    specs = [id_spec(idq), id_spec(idk)] + [half_spec(a) for a in ins[2:]]
    outs = [sds(q), sds(q)] + [sds(a) for a in ks] + [sds(a) for a in vs]
    pairs = 2 * heads * idq.shape[2] * idk.shape[1]
    res = attention(
        "attend_both", kernel, ins, specs, outs, [half_spec(a) for a in outs],
        12 * pairs * HD, pairs,
    )
    return res[0], res[1], res[2 : 2 + parts], res[2 + parts :]


def vmem_call(name, kernel, ins, outs, scratch=(), flops=0):
    nbytes = sum(a.size * a.dtype.itemsize for a in list(ins) + list(outs))
    spec = pl.BlockSpec(memory_space=pltpu.VMEM)
    return pl.pallas_call(
        kernel,
        in_specs=[spec] * len(ins),
        out_specs=[spec] * len(outs),
        out_shape=list(outs),
        scratch_shapes=list(scratch),
        name=name,
        compiler_params=pltpu.CompilerParams(vmem_limit_bytes=56 * 1024 * 1024),
        cost_estimate=pl.CostEstimate(flops=flops, bytes_accessed=nbytes, transcendentals=0),
    )(*ins)


def shape(dims, dtype):
    return jax.ShapeDtypeStruct(tuple(dims), dtype)


def aligned(x, n=8):
    return pl.multiple_of(x, n)


def solution(mesh):
    dp, seq = mesh.shape["dp"], mesh.shape["seq"]
    G = math.gcd(HEADS, seq)
    while G & (G - 1) or (seq // G) & (seq // G - 1):
        G //= 2
    J = seq // G
    heads = HEADS // G
    wide = heads * HD
    nf, nm = dp // 2, dp // 4
    mesh3 = Mesh(mesh.devices.reshape(dp, G, J), ("dp", "g", "j"))
    everyone = ("dp", "g", "j")

    view_of = [0 if d < nf else (1 if d < nf + nm else 2) for d in range(dp)]
    owner = [
        [r // 2 for r in range(dp)],
        [nf + r // 4 for r in range(dp)],
        [nf + nm + r // 4 for r in range(dp)],
    ]
    slot = [[r % 2 for r in range(dp)], [r % 4 for r in range(dp)], [r % 4 for r in range(dp)]]

    def xor(axis, n, size, x):
        return lax.ppermute(x, axis, [(i, i ^ n) for i in range(size)])

    def per_device(
        view_fine, view_mid, view_coarse, grad_fine, grad_mid, grad_coarse, clip_ids,
        attn_in, attn_out, mlp_w, cross_in, cross_out, norm_gains, biases, ffn_bias,
    ):
        tf, tm, tc = view_fine.shape[1], view_mid.shape[1], view_coarse.shape[1]
        U = 2 * tf
        ff = mlp_w.shape[1]
        cells = clip_ids.shape[1]
        d, g, j = lax.axis_index("dp"), lax.axis_index("g"), lax.axis_index("j")
        v = jnp.where(d < nf, 0, jnp.where(d < nf + nm, 1, 2))
        p = jnp.where(d < nf, 0, 1)

        def table(values, index=d):
            out = jnp.int32(values[-1])
            for i in range(len(values) - 1):
                out = jnp.where(index == i, jnp.int32(values[i]), out)
            return out

        def pick(tag, options, dtype=None):
            out = jnp.zeros_like(options[0])
            for k, option in enumerate(options):
                out = jnp.where(tag == k, option, out)
            return out

        def rows_at(x, start, size):
            return lax.dynamic_slice_in_dim(x, start, size, axis=0)

        sizes = (tf, tm, tc)
        moves = [
            (r, owner[w][r], (w, r))
            for w in range(VIEWS)
            for r in range(dp)
            if r != owner[w][r]
        ]
        view_rounds = rounds_of(moves)

        def grow(x, rows):
            if x.shape[0] == rows:
                return x
            return jnp.concatenate([x, jnp.zeros((rows - x.shape[0], x.shape[1]), x.dtype)], axis=0)

        def to_views(fine, mid, coarse):
            mid_p, coarse_p = grow(mid, tf), grow(coarse, tf)
            got = []
            for group in view_rounds:
                n = max(sizes[w] for _, _, (w, _) in group)
                kind = [3] * dp
                for src, _, (w, _) in group:
                    kind[src] = w
                load = pick(table(kind), [fine[:n], mid_p[:n], coarse_p[:n]])
                got.append(grow(lax.ppermute(load, "dp", [(s, t) for s, t, _ in group]), tf))
            local = pick(v, [fine, mid_p, coarse_p])
            rows = []
            for k in range(4):
                tag = [len(got) + 1] * dp
                for i, group in enumerate(view_rounds):
                    for _, dst, (w, r) in group:
                        if slot[w][r] == k:
                            tag[dst] = i + 1
                for r in range(dp):
                    if owner[view_of[r]][r] == r and slot[view_of[r]][r] == k:
                        tag[r] = 0
                rows.append(pick(table(tag), [local] + got))
            as_fine = jnp.concatenate(rows[:2], axis=0)
            as_mid = jnp.concatenate([x[:tm] for x in rows], axis=0)
            pad = jnp.zeros((tf - 2 * tc, fine.shape[1]), fine.dtype)
            as_coarse = jnp.concatenate(
                [rows[0][:tc], rows[1][:tc], pad, rows[2][:tc], rows[3][:tc], pad], axis=0
            )
            return pick(v, [as_fine, as_mid, as_coarse])

        def place(w, k):
            return (tf * k, tm * k, tf * (k // 2) + tc * (k % 2))[w]

        def from_views(x):
            padded = grow(x, U + tf)
            got = []
            for group in view_rounds:
                n = max(sizes[w] for _, _, (w, _) in group)
                start = [0] * dp
                for _, src, (w, r) in group:
                    start[src] = place(w, slot[w][r])
                load = rows_at(padded, table(start), n)
                got.append(grow(lax.ppermute(load, "dp", [(t, s) for s, t, _ in group]), tf))
            local_start = [0] * dp
            for r in range(dp):
                w = view_of[r]
                if owner[w][r] == r:
                    local_start[r] = place(w, slot[w][r])
            local = rows_at(padded, table(local_start), tf)
            outs = []
            for w in range(VIEWS):
                tag = [0] * dp
                for i, group in enumerate(view_rounds):
                    for _, dst, (w2, r) in group:
                        if w2 == w:
                            tag[r] = i + 1
                outs.append(pick(table(tag), [local] + got)[: sizes[w]])
            return outs

        def half_moves(src_of):
            return [(src, dst, h) for dst, (src, h) in src_of.items()]

        q_src = {}
        k_src = {}
        for dst in range(dp):
            if dst < nf:
                q_src[dst] = (nf + (2 * dst) // 4, dst % 2)
            else:
                i = dst - nf
                q_src[dst] = (nf + nm + (2 * i) // 4, i % 2)
                k_src[dst] = (nf + (2 * i) // 4, i % 2)

        def to_cross(x, src_of):
            groups = rounds_of([m for m in half_moves(src_of) if m[0] != m[1]])
            got = []
            for group in groups:
                start = [0] * dp
                for src, _, h in group:
                    start[src] = h * tf
                got.append(
                    lax.ppermute(
                        rows_at(x, table(start), tf), "dp", [(s, t) for s, t, _ in group]
                    )
                )
            start = [0] * dp
            tag = [len(got) + 1] * dp
            for dst, (src, h) in src_of.items():
                if src == dst:
                    start[dst], tag[dst] = h * tf, 0
            for i, group in enumerate(groups):
                for _, dst, _ in group:
                    tag[dst] = i + 1
            return pick(table(tag), [rows_at(x, table(start), tf)] + got)

        def from_cross(x, src_of):
            groups = rounds_of([m for m in half_moves(src_of) if m[0] != m[1]])
            got = [
                lax.ppermute(x, "dp", [(t, s) for s, t, _ in group]) for group in groups
            ]
            halves = []
            for half in range(2):
                tag = [len(got) + 1] * dp
                for dst, (src, h) in src_of.items():
                    if h == half:
                        if src == dst:
                            tag[src] = 0
                        else:
                            for i, group in enumerate(groups):
                                if any(m[1] == dst for m in group):
                                    tag[src] = i + 1
                halves.append(pick(table(tag), [x] + got))
            return jnp.concatenate(halves, axis=0)

        def zeros(rows, like):
            return jnp.zeros((rows, like.shape[1]), like.dtype)

        def q_spread(x):
            z = zeros(tm - tc, x)
            return jnp.where(
                p == 0, x, jnp.concatenate([x[:tc], z, x[tc : 2 * tc], z], axis=0)
            )

        def q_gather(x):
            z = zeros(tf - 2 * tc, x)
            return jnp.where(
                p == 0, x, jnp.concatenate([x[:tc], x[tm : tm + tc], z], axis=0)
            )

        def k_spread(x):
            z = zeros(tf - tm, x)
            return jnp.concatenate([x[:tm], z, x[tm : 2 * tm], z], axis=0)

        def k_gather(x):
            return jnp.concatenate([x[:tm], x[tf : tf + tm]], axis=0)

        def spread_g(x):
            return [x] + [xor("g", m, G, x) for m in range(1, G)]

        def sum_g(pieces):
            out = pieces[0].astype(F32)
            got = [xor("g", m, G, pieces[m].astype(BF)) for m in range(1, G)]
            for x in got:
                out = out + x.astype(F32)
            return out

        def spread_j(x):
            return [x] + [xor("j", n, J, x) for n in range(1, J)]

        n_dev = dp * seq
        gw, fw = norm_gains.shape[1], ffn_bias.shape[1]
        fq = fw // gw
        hid = ff // G
        id_rows = cells // gw
        n_vec = 38 + 3 * fq + id_rows
        vec = jnp.concatenate(
            [
                norm_gains, biases, ffn_bias.reshape(3 * fq, gw),
                clip_ids.astype(BF).reshape(id_rows, gw),
            ],
            axis=0,
        )
        vec = jnp.broadcast_to(vec[None], (n_dev, n_vec, gw))
        vecs = lax.all_to_all(vec, everyone, 0, 0, tiled=True)

        def role():
            kd, kg, kj = lax.axis_index("dp"), lax.axis_index("g"), lax.axis_index("j")
            kv = jnp.where(kd < nf, 0, jnp.where(kd < nf + nm, 1, 2))
            return kd, kg, kj, kv, jnp.where(kd < nf, 0, 1)

        def setup(vec_ref, prm_ref, idq_ref, idk_ref, cidq_ref, cidk_ref, full, ffn):
            kd, kg, kj, kv, kp = role()
            for i in range(n_dev):
                full[:, i * gw : (i + 1) * gw] = vec_ref[i, :38].astype(F32)
                for r in range(3):
                    for t in range(fq):
                        at = i * fw + t * gw
                        ffn[r : r + 1, at : at + gw] = vec_ref[
                            i, 38 + r * fq + t : 39 + r * fq + t
                        ].astype(F32)

            def row(r):
                return full[r : r + 1, :]

            def by_view(rows):
                return jnp.where(kv == 0, rows[0], jnp.where(kv == 1, rows[1], rows[2]))

            def part(x, width):
                out = x[:, :width]
                for i in range(1, G):
                    out = jnp.where(kg == i, x[:, i * width : (i + 1) * width], out)
                return out

            prm_ref[...] = jnp.zeros_like(prm_ref)
            for i in range(2):
                prm_ref[i : i + 1, :] = by_view([row(2 * k + i) for k in range(3)])
            for i in range(6):
                x = by_view([row(10 + 6 * k + i) for k in range(3)])
                if i in (1, 2):
                    prm_ref[2 + i : 3 + i, :wide] = part(x, wide)
                else:
                    prm_ref[2 + i : 3 + i, :] = x
            prm_ref[8:9, :hid] = part(by_view([ffn[k : k + 1, :] for k in range(3)]), hid)
            prm_ref[9:10, :] = by_view([row(6), row(6), row(8)])
            prm_ref[10:11, :] = by_view([row(7), row(9), row(9)])
            prm_ref[11:12, :] = by_view([row(28), row(28), row(33)])
            prm_ref[12:13, :] = by_view([row(29), row(34), row(34)])
            for i in range(3):
                x = jnp.where(kp == 0, row(30 + i), row(35 + i))
                if i < 2:
                    prm_ref[13 + i : 14 + i, :wide] = part(x, wide)
                else:
                    prm_ref[13 + i : 14 + i, :] = x

            starts = []
            for r in range(dp):
                x = vec_ref[r * seq, 38 + 3 * fq :].astype(F32)
                starts.append(
                    [jnp.sum((x < c).astype(F32), keepdims=True) for c in (0.5, 1.5, 2.5)]
                )

            def start_at(index):
                out = starts[0]
                for r in range(1, dp):
                    out = [jnp.where(index == r, b, a) for a, b in zip(out, starts[r])]
                return out

            def ids(first, second, unit, per_cell, cap, u, k, n):
                s = (kg ^ k) * J + (kj ^ n)
                late = u >= unit
                pos = (s * unit + u - jnp.where(late, unit, 0)).astype(F32)
                out = jnp.zeros(u.shape, F32)
                for a, b in zip(first, second):
                    edge = jnp.where(late, b, a) * per_cell.astype(F32)
                    out = out + (pos >= edge).astype(F32)
                out = out + jnp.where(late, 4.0, 0.0)
                return jnp.where(u >= cap, -1.0, out)

            unit = jnp.where(kv == 0, tf, jnp.where(kv == 1, tm, tc))
            per_cell = jnp.where(kv == 0, 4, jnp.where(kv == 1, 2, 1))
            base = jnp.where(kv == 0, 2 * kd, 4 * ((kd - nf) % nm))
            pair_base = 2 * jnp.where(kp == 0, kd, kd - nf)
            k_unit, k_cell = jnp.where(kp == 0, tf, tm), jnp.where(kp == 0, 4, 2)
            q_unit, q_cell = jnp.where(kp == 0, tm, tc), jnp.where(kp == 0, 2, 1)
            for h in range(2):
                first = start_at(base + jnp.where(kv == 0, h, 2 * h))
                second = start_at(base + 2 * h + 1)
                mine = start_at(pair_base + h)
                for k in range(G):
                    lane = lax.broadcasted_iota(jnp.int32, (1, tf), 1)
                    idq_ref[h, :, k * tf : (k + 1) * tf] = ids(
                        first, second, unit, per_cell, 2 * unit, lane, k, 0
                    )
                    lane = lax.broadcasted_iota(jnp.int32, (1, tm), 1)
                    cidq_ref[h, :, k * tm : (k + 1) * tm] = ids(
                        mine, mine, q_unit, q_cell, q_unit, lane, k, 0
                    )
                    for n in range(J):
                        deep = lax.broadcasted_iota(jnp.int32, (tf, 1), 0)
                        at = (n * G + k) * tf
                        idk_ref[h, at : at + tf, :] = ids(
                            first, second, unit, per_cell, 2 * unit, deep, k, n
                        )
                        cidk_ref[h, at : at + tf, :] = ids(
                            mine, mine, k_unit, k_cell, k_unit, deep, k, n
                        )

        prm, idq, idk, cross_idq, cross_idk = vmem_call(
            "setup",
            setup,
            [vecs],
            [
                shape((16, D), F32),
                shape((2, 1, G * tf), F32), shape((2, seq * tf, 1), F32),
                shape((2, 1, G * tm), F32), shape((2, seq * tf, 1), F32),
            ],
            [pltpu.VMEM((38, D), F32), pltpu.VMEM((3, ff), F32)],
        )

        def prow(i, width=D):
            return prm[i : i + 1, :width]

        g1, g2, n1, bq, bv, bo, n2, bm = [
            prow(i, wide if i in (3, 4) else D) for i in range(8)
        ]
        bf_g = prow(8, hid)
        gq, gk, nq, nk = [prow(i) for i in range(9, 13)]
        cq, cv, co = prow(13, wide), prow(14, wide), prow(15)

        def cols(x, width):
            return lax.dynamic_slice_in_dim(x, g * width, width, axis=-1)

        near = dp == 4

        def both_sides(x):
            up = lax.ppermute(x, "dp", [(0, 1), (1, 2), (2, 3)])
            down = lax.ppermute(x, "dp", [(1, 0), (3, 2)])
            return up, down

        def chunks(x):
            if near:
                up, down = both_sides(x)
                enc = jnp.stack([jnp.where(d == 0, x, up), jnp.where(d == 0, down, x)])
                odd = d % 2 == 1
                cross = jnp.stack([jnp.where(odd, up, x), jnp.where(odd, x, down)])
                return enc, cross
            everything = lax.all_gather(x, "dp", axis=0)
            return everything, everything

        enc_lo = jnp.maximum(d - 1, 0) if near else jnp.int32(0)
        cross_lo = 2 * p if near else jnp.int32(0)

        def start_of(part, n_parts, low, total):
            return part * (total // n_parts) - low * (total // dp)

        def join_j(x):
            xs = spread_j(x)
            parts = []
            for a in range(J):
                out = xs[0]
                for n in range(1, J):
                    out = jnp.where((j ^ n) == a, xs[n], out)
                parts.append(out)
            full = jnp.stack(parts, axis=2)
            return full.reshape(-1, x.shape[-1])

        r_in, r_cross = attn_in.shape[0], cross_in.shape[0]
        r_mlp, r_out, r_co = mlp_w.shape[0], attn_out.shape[0], cross_out.shape[0]

        def split_cols(in_ref, cross_ref, mlp_ref, qkv_ref, mlp_out):
            for i in range(G):
                at = slice(i * wide, (i + 1) * wide)
                qkv_ref[i, :r_in, :] = in_ref[:, at]
                qkv_ref[i, r_in:, :] = cross_ref[:, at]
                mlp_out[i] = mlp_ref[:, i * hid : (i + 1) * hid]

        qkv, mlp = vmem_call(
            "split_cols", split_cols, [attn_in, cross_in, mlp_w],
            [shape((G, r_in + r_cross, wide), BF), shape((G, r_mlp, hid), BF)],
        )
        qkv = lax.all_to_all(qkv, "g", 0, 0, tiled=True)
        mlp = lax.all_to_all(mlp, "g", 0, 0, tiled=True)

        def offset(kind, total, kd, kv, kp):
            low = jnp.maximum(kd - 1, 0)
            return kv * (total // 3) - low * (total // 4) if kind == "enc" else kp * 0

        def assemble(name, x, parts):
            up, down = both_sides(x)
            srcs = [*spread_j(x), *spread_j(up), *spread_j(down)]
            width = x.shape[2]
            outs, scratch = [], []
            for kind, _, r in parts:
                outs.append(shape((n_dev * r // (3 if kind == "enc" else 2), width), BF))
                scratch.append(pltpu.VMEM((n_dev * r // 2, width), F32))

            def kernel(*refs):
                kd, kg, kj, kv, kp = role()
                own, up_r, down_r = refs[:J], refs[J : 2 * J], refs[2 * J : 3 * J]
                out_refs = refs[3 * J : 3 * J + len(parts)]
                frames = refs[3 * J + len(parts) :]

                for (kind, first, r), frame in zip(parts, frames):

                    def put(t, group, first=first, r=r, frame=frame):
                        for n, ref in enumerate(group):
                            for i in range(G):
                                at = aligned(((t * G + i) * J + (kj ^ n)) * r)
                                frame[pl.ds(at, r), :] = ref[i, first : first + r].astype(F32)

                    low = kd == 0 if kind == "enc" else kd % 2 == 0

                    @pl.when(low)
                    def _(put=put):
                        put(0, own)
                        put(1, down_r)

                    @pl.when(jnp.logical_not(low))
                    def _(put=put):
                        put(0, up_r)
                        put(1, own)

                for (kind, _, r), frame, out in zip(parts, frames, out_refs):
                    at = aligned(offset(kind, n_dev * r, kd, kv, kp))
                    out[...] = frame[pl.ds(at, out.shape[0]), :].astype(BF)

            return vmem_call(name, kernel, srcs, outs, scratch)

        if near:
            w_in, c_in = assemble(
                "assemble_in", qkv, [("enc", 0, r_in), ("cross", r_in, r_cross)]
            )
            (w_mlp,) = assemble("assemble_mlp", mlp, [("enc", 0, r_mlp)])
        else:
            enc_c, cross_c = chunks(qkv)
            w_in = rows_at(
                join_j(enc_c[:, :, :r_in]), start_of(v, 3, enc_lo, n_dev * r_in), 3 * D
            )
            c_in = rows_at(
                join_j(cross_c[:, :, r_in:]), start_of(p, 2, cross_lo, n_dev * r_cross), 3 * D
            )
            enc_c, _ = chunks(mlp)
            w_mlp = rows_at(join_j(enc_c), start_of(v, 3, enc_lo, n_dev * r_mlp), 2 * D)
        enc_c, cross_c = chunks(jnp.concatenate([attn_out, cross_out], axis=0))
        planes = enc_c.shape[0]
        outs = jnp.concatenate([enc_c[:, :r_out], cross_c[:, r_out:]], axis=1)
        outs = lax.all_gather(outs.reshape(-1, D), ("g", "j"), axis=0)
        outs = outs.reshape(seq, planes, r_out + r_co, D)

        def arrange(x_ref, w_ref, c_ref, frame, cross_frame):
            kd, kg, kj, kv, kp = role()
            for t in range(planes):
                for i in range(seq):
                    at = (t * seq + i) * r_out
                    frame[at : at + r_out, :] = x_ref[i, t, :r_out].astype(F32)
                    at = (t * seq + i) * r_co
                    cross_frame[at : at + r_co, :] = x_ref[i, t, r_out:].astype(F32)
            low = jnp.maximum(kd - 1, 0) if near else 0
            first = kv * (n_dev * r_out // 3) - low * (n_dev * r_out // dp)
            cross_first = 0 if near else kp * (n_dev * r_co // 2)
            for m in range(G):
                to = slice(m * wide, (m + 1) * wide)
                at = aligned(first + (kg ^ m) * wide)
                w_ref[to, :] = frame[pl.ds(at, wide), :].astype(BF)
                at = aligned(cross_first + (kg ^ m) * wide)
                c_ref[to, :] = cross_frame[pl.ds(at, wide), :].astype(BF)

        w_out, c_out = vmem_call(
            "arrange_out", arrange, [outs], [shape((D, D), BF), shape((D, D), BF)],
            [
                pltpu.VMEM((planes * seq * r_out, D), F32),
                pltpu.VMEM((planes * seq * r_co, D), F32),
            ],
        )
        wq, wk, wv = w_in[:D], w_in[D : 2 * D], w_in[2 * D :]
        ccq, cck, ccv = c_in[:D], c_in[D : 2 * D], c_in[2 * D :]
        w1, w2 = w_mlp[:D], w_mlp[D:]

        x_own = to_views(view_fine[0], view_mid[0], view_coarse[0])
        grad_own = to_views(grad_fine[0], grad_mid[0], grad_coarse[0])
        x = jnp.concatenate(spread_g(x_own), axis=0).astype(F32)
        a = (unit_rows(x)[0] * g1 + n1).astype(BF)
        q = (mm(a, wq) + bq).astype(BF)
        k = mm(a, wk).astype(BF)
        w = (mm(a, wv) + bv).astype(BF)

        def halves(t, width=None):
            return t.reshape(G, 2, -1, t.shape[-1])

        kv = spread_j(jnp.concatenate([k, w], axis=1))
        ks = [halves(t[:, :wide]) for t in kv]
        vs = [halves(t[:, wide:]) for t in kv]
        o, lse = attend(heads, idq, idk, halves(q), ks, vs)

        def all_heads(t):
            t = t.reshape(G, -1, wide)
            got = [t]
            for m in range(1, G):
                r = xor("g", m, G, t)
                got.append(jnp.stack([r[i ^ m] for i in range(G)]))
            return jnp.concatenate(got, axis=2).reshape(-1, G * wide)

        o_all = all_heads(o)
        h = x + (mm(o_all, w_out) + bo)
        zh, _ = unit_rows(h)
        c = (zh * g2 + n2).astype(BF)
        up = mm(c, w1) + bf_g
        e = (up * gelu_parts(up)).astype(BF)
        y_part = mm_nt(e, w2).reshape(G, U, D)
        h_own = h[:U]
        y = sum_g([y_part[m] for m in range(G)]) + h_own + bm

        zy, rs_y = unit_rows(y)
        kn_v = (zy * gk + nk).astype(BF)
        qn_v = (zy * gq + nq).astype(BF)
        kn_own = jnp.where(p == 0, kn_v, k_spread(to_cross(kn_v, k_src)))
        qn_own = q_spread(to_cross(qn_v, q_src))
        gq_own = q_spread(to_cross(grad_own, q_src))
        kn = jnp.concatenate(spread_g(kn_own), axis=0)
        qn = jnp.concatenate(spread_g(qn_own), axis=0)
        gc = jnp.concatenate(spread_g(gq_own), axis=0)
        cross_q = (mm(qn, ccq) + cq).astype(BF)
        cross_k = mm(kn, cck).astype(BF)
        cross_v = (mm(kn, ccv) + cv).astype(BF)
        d_att = mm_nt(gc, c_out[:wide]).astype(BF)
        kv = spread_j(jnp.concatenate([cross_k, cross_v], axis=1))
        cks = [halves(t[:, :wide]) for t in kv]
        cvs = [halves(t[:, wide:]) for t in kv]
        co_att, dq_c, dks, dvs = attend_both(
            heads, cross_idq, cross_idk, halves(cross_q), halves(d_att), cks, cvs
        )

        def home_j(ts):
            out = ts[0].astype(F32)
            for n in range(1, J):
                out = out + xor("j", n, J, ts[n]).astype(F32)
            return out

        def home_kv(dks, dvs):
            both = home_j([jnp.concatenate([a, b], axis=3) for a, b in zip(dks, dvs)])
            both = both.astype(BF).reshape(-1, 2 * wide)
            return both[:, :wide], both[:, wide:]

        dk_c, dv_c = home_kv(dks, dvs)
        dq_c = dq_c.reshape(-1, wide)
        cross_o = all_heads(co_att)
        Uq = 2 * tm
        mix = mm(cross_o[:Uq], c_out) + co
        mix_v = from_cross(q_gather(mix.astype(BF)), q_src).astype(F32)

        dqn_part = mm_nt(dq_c, ccq).reshape(G, Uq, D)
        dqn = sum_g([dqn_part[m] for m in range(G)]).astype(BF)
        dkn_part = (mm_nt(dk_c, cck) + mm_nt(dv_c, ccv)).reshape(G, U, D)
        dkn = sum_g([dkn_part[m] for m in range(G)]).astype(BF)
        dqn_v = from_cross(q_gather(dqn), q_src).astype(F32)
        dkn_v = jnp.where(v == 0, dkn, from_cross(k_gather(dkn), k_src)).astype(F32)
        dqn_v = jnp.where(v == 0, 0.0, dqn_v)
        mix_v = jnp.where(v == 0, 0.0, mix_v)
        dkn_v = jnp.where(v == 2, 0.0, dkn_v)
        dy = grad_own.astype(F32) + unit_back(zy, rs_y, dqn_v * gq + dkn_v * gk)

        dm_own = dy.astype(BF)
        dm = jnp.concatenate(spread_g(dm_own), axis=0)
        de = mm(dm, w2)
        du = (de * gelu_slope(up)).astype(BF)
        dc_part = mm_nt(du, w1).reshape(G, U, D)
        dn2 = sum_g([dc_part[m] for m in range(G)])
        zh_own, rs_h = unit_rows(h_own)
        dh = dy + unit_back(zh_own, rs_h, dn2 * g2)
        dh_own = dh.astype(BF)
        dh_all = jnp.concatenate(spread_g(dh_own), axis=0)
        d_o = mm_nt(dh_all, w_out[:wide]).astype(BF)
        dq, dks, dvs = attend_back(heads, idq, idk, halves(q), halves(d_o), lse, ks, vs)
        dk, dv = home_kv(dks, dvs)
        dq = dq.reshape(-1, wide)
        da_part = (mm_nt(dq, wq) + mm_nt(dk, wk) + mm_nt(dv, wv)).reshape(G, U, D)
        da = sum_g([da_part[m] for m in range(G)])
        zx, rs_x = unit_rows(x_own.astype(F32))
        dx = dh + unit_back(zx, rs_x, da * g1)

        out_f, out_m, out_c = from_views((y + mix_v).astype(BF))
        dx_f, dx_m, dx_c = from_views(dx.astype(BF))

        def my_rows(x):
            return lax.dynamic_index_in_dim(x, j, axis=2, keepdims=False)

        def send_home(grad, total, enc):
            width = grad.shape[1]
            r = total // n_dev
            if near:
                frame_rows, n_planes = total // 2, 2
                low = enc_lo if enc else cross_lo
            else:
                frame_rows, n_planes, low = total, dp, jnp.int32(0)
            if grad.shape[0] != frame_rows:
                part, n_parts = (v, 3) if enc else (p, 2)
                grad = lax.dynamic_update_slice_in_dim(
                    jnp.zeros((frame_rows, width), BF), grad.astype(BF),
                    start_of(part, n_parts, low, total), axis=0,
                )
            x = grad.astype(BF).reshape(n_planes, G, J, r, width)
            acc = lax.dynamic_index_in_dim(x, j, axis=2, keepdims=False).astype(F32)
            for n in range(1, J):
                part = lax.dynamic_index_in_dim(x, j ^ n, axis=2, keepdims=False)
                acc = acc + xor("j", n, J, part).astype(F32)
            if not near:
                acc = lax.psum_scatter(acc, "dp", scatter_dimension=0, tiled=False)
            elif enc:
                own = jnp.where(d == 0, acc[0], acc[1])
                other = jnp.where(d == 0, acc[1], acc[0]).astype(BF)
                down = lax.ppermute(other, "dp", [(1, 0), (2, 1), (3, 2)])
                upward = lax.ppermute(other, "dp", [(0, 1)])
                acc = own + down.astype(F32) + upward.astype(F32)
            else:
                odd = d % 2 == 1
                own = jnp.where(odd, acc[1], acc[0])
                other = jnp.where(odd, acc[0], acc[1]).astype(BF)
                acc = own + xor("dp", 1, dp, other).astype(F32)
            acc = acc.astype(BF).reshape(G * r, width)
            return lax.all_to_all(acc, "g", 0, 1, tiled=True).astype(F32)

        def in_order(w):
            return jnp.concatenate(
                [rows_at(w, (g ^ a) * wide, wide) for a in range(G)], axis=0
            )

        def home(name, arrays, parts):
            ins = list(arrays)
            width = ins[parts[0][2][0][1]].shape[1]
            n_rows = sum(r for _, r, _ in parts)
            outs = [shape((2, G, n_rows, width), BF) for _ in range(J)]
            scratch = [pltpu.VMEM((n_dev * r // 2, width), F32) for _, r, _ in parts]

            def kernel(*refs):
                kd, kg, kj, kv, kp = role()
                in_refs = refs[: len(ins)]
                out_refs = refs[len(ins) : len(ins) + J]
                frames = refs[len(ins) + J :]
                first = 0
                for (kind, r, mats), frame in zip(parts, frames):
                    n = n_dev * r // (3 if kind == "enc" else 2)
                    if kind == "enc":
                        frame[...] = jnp.zeros_like(frame)
                    base = offset(kind, n_dev * r, kd, kv, kp)
                    for i, (left, right, grouped) in enumerate(mats):
                        b = in_refs[right][...]
                        if grouped:
                            x = b[:, :wide]
                            for k in range(1, G):
                                x = jnp.where(kg == k, b[:, k * wide : (k + 1) * wide], x)
                            res = mm_tn(in_refs[left][...], x)
                            for m in range(G):
                                at = aligned(base + i * D + (kg ^ m) * wide)
                                frame[pl.ds(at, wide), :] = res[m * wide : (m + 1) * wide]
                        else:
                            at = aligned(base + i * D)
                            frame[pl.ds(at, D), :] = mm_tn(in_refs[left][...], b)
                    own = jnp.where(kd == 0, 0, 1) if kind == "enc" else kd % 2
                    for n in range(J):
                        for side in range(2):
                            t = own if side == 0 else 1 - own
                            for k in range(G):
                                at = aligned(((t * G + k) * J + (kj ^ n)) * r)
                                out_refs[n][side, k, first : first + r, :] = frame[
                                    pl.ds(at, r), :
                                ].astype(BF)
                    first += r

            flops = 2 * D * D * width * sum(len(m) for _, _, m in parts)
            mine, *others = vmem_call(name, kernel, ins, outs, scratch, flops)
            acc = mine.astype(F32)
            for n in range(1, J):
                acc = acc + xor("j", n, J, others[n - 1]).astype(F32)
            own, other = acc[0], acc[1].astype(BF)
            if parts[0][0] == "enc":
                down = lax.ppermute(other, "dp", [(1, 0), (2, 1), (3, 2)])
                upward = lax.ppermute(other, "dp", [(0, 1)])
                own = own + down.astype(F32) + upward.astype(F32)
            else:
                own = own + xor("dp", 1, dp, other).astype(F32)
            return lax.all_to_all(own.astype(BF), "g", 0, 0, tiled=True)

        if near:
            x_cross = home(
                "home_cross", [qn, kn, dq_c, dk_c, dv_c, cross_o, gc],
                [
                    ("cross", r_cross, [(0, 2, False), (1, 3, False), (1, 4, False)]),
                    ("cross", r_co, [(5, 6, True)]),
                ],
            )
            x_mlp = home(
                "home_mlp", [c, du, dm, e],
                [("enc", r_mlp, [(0, 1, False), (2, 3, False)])],
            )
            x_enc = home(
                "home_enc", [a, dq, dk, dv, o_all, dh_all],
                [
                    ("enc", r_in, [(0, 1, False), (0, 2, False), (0, 3, False)]),
                    ("enc", r_out, [(4, 5, True)]),
                ],
            )

            def landed(cross_ref, mlp_ref, enc_ref, gi_ref, go_ref, gm_ref, gci_ref, gco_ref):
                for i in range(G):
                    at = slice(i * wide, (i + 1) * wide)
                    gi_ref[:, at] = enc_ref[i, :r_in].astype(F32)
                    go_ref[:, at] = enc_ref[i, r_in:].astype(F32)
                    gci_ref[:, at] = cross_ref[i, :r_cross].astype(F32)
                    gco_ref[:, at] = cross_ref[i, r_cross:].astype(F32)
                    gm_ref[:, i * hid : (i + 1) * hid] = mlp_ref[i].astype(F32)

            grad_in, grad_out, grad_mlp, grad_cin, grad_cout = vmem_call(
                "landed", landed, [x_cross, x_mlp, x_enc],
                [
                    shape(attn_in.shape, F32), shape(attn_out.shape, F32),
                    shape(mlp_w.shape, F32), shape(cross_in.shape, F32),
                    shape(cross_out.shape, F32),
                ],
            )
        else:
            g_cin = jnp.concatenate(
                [mm_tn(qn, dq_c), mm_tn(kn, dk_c), mm_tn(kn, dv_c)], axis=0
            )
            g_cout = in_order(mm_tn(cross_o, cols(gc, wide)))
            g_mlp = jnp.concatenate([mm_tn(c, du), mm_tn(dm, e)], axis=0)
            g_out = in_order(mm_tn(o_all, cols(dh_all, wide)))
            g_in = jnp.concatenate([mm_tn(a, dq), mm_tn(a, dk), mm_tn(a, dv)], axis=0)
            grad_cin = send_home(g_cin, n_dev * r_cross, False)
            grad_cout = send_home(g_cout, n_dev * r_co, False)
            grad_mlp = send_home(g_mlp, n_dev * r_mlp, True)
            grad_out = send_home(g_out, n_dev * r_out, True)
            grad_in = send_home(g_in, n_dev * r_in, True)

        def total(x):
            return jnp.sum(x.astype(F32), axis=0)

        def at_cols(x):
            hot = (jnp.arange(G) == g).astype(F32)
            return (hot[:, None] * x[None]).reshape(-1)

        def at_row(x, index, n):
            hot = (jnp.arange(n) == index).astype(F32)
            return hot.reshape((n,) + (1,) * x.ndim) * x[None]

        enc_g = jnp.stack([total(da * zx), total(dn2 * zh_own)])
        enc_b = jnp.stack(
            [
                total(da), at_cols(total(dq)), at_cols(total(dv)), total(dh_own), total(dn2),
                total(dm_own),
            ]
        )
        q_role = at_row(jnp.stack([total(dqn_v * zy), total(dqn_v), total(grad_own)]), v - 1, 2)
        k_role = at_row(jnp.stack([total(dkn_v * zy), total(dkn_v)]), v, 2)
        pair = at_row(jnp.stack([at_cols(total(dq_c)), at_cols(total(dv_c))]), p, 2)
        gains_g = jnp.concatenate(
            [
                at_row(enc_g, v, 3).reshape(6, D),
                jnp.stack([q_role[:, 0], k_role[:, 0]], axis=1).reshape(4, D),
            ]
        )
        cross_b = jnp.stack(
            [q_role[:, 1], k_role[:, 1], pair[:, 0], pair[:, 1], q_role[:, 2]], axis=1
        )
        bias_g = jnp.concatenate([at_row(enc_b, v, 3).reshape(18, D), cross_b.reshape(10, D)])
        ffn_g = at_row(at_cols(total(du)), v, 3)

        def deal(g_ref, b_ref, f_ref, out_ref):
            for i in range(n_dev):
                at = slice(i * gw, (i + 1) * gw)
                out_ref[i, :10, :] = g_ref[:, at]
                out_ref[i, 10:38, :] = b_ref[:, at]
                for r in range(3):
                    for t in range(fq):
                        to = 38 + r * fq + t
                        out_ref[i, to : to + 1, :] = f_ref[
                            r : r + 1, i * fw + t * gw : i * fw + (t + 1) * gw
                        ]

        (small,) = vmem_call(
            "deal", deal, [gains_g, bias_g, ffn_g], [shape((n_dev, 38 + 3 * fq, gw), F32)]
        )
        small = lax.all_to_all(small, everyone, 0, 0, tiled=True)

        def collect(x_ref, g_ref, b_ref, f_ref):
            x = jnp.sum(x_ref[...], axis=0)
            g_ref[...] = x[:10]
            b_ref[...] = x[10:38]
            for r in range(3):
                for t in range(fq):
                    at = 38 + r * fq + t
                    f_ref[r : r + 1, t * gw : (t + 1) * gw] = x[at : at + 1]

        grad_gains, grad_bias, grad_ffn = vmem_call(
            "collect", collect, [small],
            [shape(norm_gains.shape, F32), shape(biases.shape, F32), shape(ffn_bias.shape, F32)],
        )
        return (
            out_f[None], out_m[None], out_c[None],
            dx_f.astype(F32)[None], dx_m.astype(F32)[None], dx_c.astype(F32)[None],
            grad_in, grad_out, grad_mlp, grad_cin, grad_cout,
            grad_gains, grad_bias, grad_ffn,
        )

    tokens = P("dp", ("g", "j"), None)
    rows = P(everyone, None)
    columns = P(None, everyone)
    return jax.shard_map(
        per_device,
        mesh=mesh3,
        in_specs=(tokens,) * 6 + (P("dp", None),) + (rows,) * 5 + (columns,) * 3,
        out_specs=(tokens,) * 6 + (rows,) * 5 + (columns,) * 3,
        check_vma=False,
    )
```

```python
import math

import jax
import jax.numpy as jnp
from jax import lax
from jax.experimental import pallas as pl
from jax.experimental.pallas import tpu as pltpu
from jax.sharding import Mesh, PartitionSpec as P

D = 768
HEADS = 12
HD = 64
VIEWS = 3
EPS = 1e-06
NEG = -1e30
SCALE = HD**-0.5
BF = jnp.bfloat16
F32 = jnp.float32


def mm(a, b):
    return lax.dot_general(a, b, (((1,), (0,)), ((), ())), preferred_element_type=F32)


def mm_nt(a, b):
    return lax.dot_general(a, b, (((1,), (1,)), ((), ())), preferred_element_type=F32)


def mm_tn(a, b):
    return lax.dot_general(a, b, (((0,), (0,)), ((), ())), preferred_element_type=F32)


def unit_rows(u):
    centre = jnp.mean(u, axis=-1, keepdims=True)
    spread = u - centre
    rs = lax.rsqrt(jnp.mean(spread * spread, axis=-1, keepdims=True) + EPS)
    return spread * rs, rs


def unit_back(z, rs, dz):
    return rs * (
        dz - jnp.mean(dz, axis=-1, keepdims=True) - z * jnp.mean(dz * z, axis=-1, keepdims=True)
    )


def gelu_parts(u):
    phi = 0.5 * lax.erfc(u * (-(0.5**0.5)))
    return phi


def gelu_slope(u):
    return gelu_parts(u) + u * jnp.exp(-0.5 * u * u) * (1.0 / math.sqrt(2.0 * math.pi))


def rounds_of(moves):
    rounds = []
    for move in moves:
        for group in rounds:
            if all(move[0] != other[0] and move[1] != other[1] for other in group):
                group.append(move)
                break
        else:
            rounds.append([move])
    return rounds


def attend_kernel(heads, parts, idq_ref, idk_ref, q_ref, *rest):
    kv_refs, (o_ref, lse_ref) = rest[:parts], rest[parts:]
    wide = heads * HD
    q = q_ref[...].reshape(-1, wide)
    kv = jnp.concatenate([r[...].reshape(-1, 2 * wide) for r in kv_refs], axis=0)
    allowed = idk_ref[0] == idq_ref[0]
    outs = []
    for n in range(heads):
        cols = slice(n * HD, (n + 1) * HD)
        v_cols = slice(wide + n * HD, wide + (n + 1) * HD)
        s = jnp.where(allowed, mm_nt(kv[:, cols], q[:, cols]) * SCALE, NEG)
        top = jnp.max(s, axis=0, keepdims=True)
        p = jnp.exp(s - top)
        total = jnp.sum(p, axis=0, keepdims=True)
        lse_ref[0, n : n + 1, :] = top + jnp.log(total)
        pb = (p * (1.0 / total)).astype(BF)
        outs.append(mm(kv[:, v_cols].T, pb).T)
    o_ref[...] = jnp.concatenate(outs, axis=1).astype(BF).reshape(o_ref.shape)


def attend_grads(heads, idq, idk, q, do, kv, lse):
    wide = heads * HD
    allowed = idk == idq
    os, dqs, dks, dvs = [], [], [], []
    for n in range(heads):
        cols = slice(n * HD, (n + 1) * HD)
        qn, kn, gn = q[:, cols], kv[:, cols], do[:, cols]
        vn = kv[:, wide + n * HD : wide + (n + 1) * HD]
        s = jnp.where(allowed, mm_nt(kn, qn) * SCALE, NEG)
        if lse is None:
            e = jnp.exp(s - jnp.max(s, axis=0, keepdims=True))
            p = e * (1.0 / jnp.sum(e, axis=0, keepdims=True))
        else:
            p = jnp.exp(s - lse[n : n + 1, :])
        pb = p.astype(BF)
        if lse is None:
            os.append(mm(vn.T, pb).T)
        dp = mm_nt(vn, gn)
        delta = jnp.sum(p * dp, axis=0, keepdims=True)
        ds = (p * (dp - delta)).astype(BF)
        dqs.append(mm(kn.T, ds).T * SCALE)
        dks.append(mm(ds, qn) * SCALE)
        dvs.append(mm(pb, gn))
    join = lambda xs: jnp.concatenate(xs, axis=1).astype(BF)
    return (join(os) if os else None), join(dqs), join(dks + dvs)


def put_parts(refs, x):
    rows = x.shape[0] // len(refs)
    for n, ref in enumerate(refs):
        ref[...] = x[n * rows : (n + 1) * rows].reshape(ref.shape)


def both_kernel(heads, parts, idq_ref, idk_ref, q_ref, do_ref, *rest):
    kv_refs, (o_ref, dq_ref, *dkv_refs) = rest[:parts], rest[parts:]
    wide = heads * HD
    q, do = q_ref[...].reshape(-1, wide), do_ref[...].reshape(-1, wide)
    kv = jnp.concatenate([r[...].reshape(-1, 2 * wide) for r in kv_refs], axis=0)
    o, dq, dkv = attend_grads(heads, idq_ref[0], idk_ref[0], q, do, kv, None)
    o_ref[...] = o.reshape(o_ref.shape)
    dq_ref[...] = dq.reshape(dq_ref.shape)
    put_parts(dkv_refs, dkv)


def back_kernel(heads, parts, pieces, idq_ref, idk_ref, q_ref, lse_ref, w_ref, *rest):
    dh_refs, rest = rest[:pieces], rest[pieces:]
    kv_refs, (dq_ref, *dkv_refs) = rest[:parts], rest[parts:]
    wide = heads * HD
    q = q_ref[...].reshape(-1, wide)
    dh = jnp.concatenate([r[0] for r in dh_refs], axis=0)
    do = mm_nt(dh, w_ref[...]).astype(BF)
    kv = jnp.concatenate([r[...].reshape(-1, 2 * wide) for r in kv_refs], axis=0)
    _, dq, dkv = attend_grads(heads, idq_ref[0], idk_ref[0], q, do, kv, lse_ref[0])
    dq_ref[...] = dq.reshape(dq_ref.shape)
    put_parts(dkv_refs, dkv)


def half_spec(a):
    return pl.BlockSpec((a.shape[0], 1) + a.shape[2:], lambda h: (0, h, 0, 0))


def id_spec(a):
    return pl.BlockSpec((1,) + a.shape[1:], lambda h: (h, 0, 0))


def sds(a, dtype=None):
    return jax.ShapeDtypeStruct(a.shape, dtype or a.dtype)


def attention(name, kernel, ins, specs, outs, out_specs, flops, trans):
    nbytes = sum(a.size * a.dtype.itemsize for a in ins)
    return pl.pallas_call(
        kernel,
        grid=(2,),
        in_specs=specs,
        out_specs=out_specs,
        out_shape=outs,
        name=name,
        compiler_params=pltpu.CompilerParams(vmem_limit_bytes=48 * 1024 * 1024),
        cost_estimate=pl.CostEstimate(
            flops=flops, bytes_accessed=2 * nbytes, transcendentals=trans
        ),
    )(*ins)


def attend(heads, idq, idk, q, kvs):
    kernel = lambda *refs: attend_kernel(heads, len(kvs), *refs)
    ins = [idq, idk, q, *kvs]
    specs = [id_spec(idq), id_spec(idk)] + [half_spec(a) for a in ins[2:]]
    lse = jax.ShapeDtypeStruct((2, 8, idq.shape[2]), F32)
    pairs = 2 * heads * idq.shape[2] * idk.shape[1]
    return attention(
        "attend", kernel, ins, specs, [sds(q), lse], [half_spec(q), id_spec(lse)],
        4 * pairs * HD, pairs,
    )


def attend_back(heads, idq, idk, q, lse, w_out, dhs, kvs):
    kernel = lambda *refs: back_kernel(heads, len(kvs), len(dhs), *refs)
    dhs = [x.reshape(2, -1, D) for x in dhs]
    ins = [idq, idk, q, lse, w_out, *dhs, *kvs]
    specs = [id_spec(idq), id_spec(idk), half_spec(q), id_spec(lse)]
    specs += [pl.BlockSpec((heads * HD, D), lambda h: (0, 0))]
    specs += [id_spec(x) for x in dhs] + [half_spec(a) for a in kvs]
    outs = [sds(q)] + [sds(a) for a in kvs]
    pairs = 2 * heads * idq.shape[2] * idk.shape[1]
    res = attention(
        "attend_back", kernel, ins, specs, outs, [half_spec(a) for a in outs],
        10 * pairs * HD, pairs,
    )
    return res[0], res[1:]


def attend_both(heads, idq, idk, q, do, kvs):
    kernel = lambda *refs: both_kernel(heads, len(kvs), *refs)
    ins = [idq, idk, q, do, *kvs]
    specs = [id_spec(idq), id_spec(idk)] + [half_spec(a) for a in ins[2:]]
    outs = [sds(q), sds(q)] + [sds(a) for a in kvs]
    pairs = 2 * heads * idq.shape[2] * idk.shape[1]
    res = attention(
        "attend_both", kernel, ins, specs, outs, [half_spec(a) for a in outs],
        12 * pairs * HD, pairs,
    )
    return res[0], res[1], res[2:]


def vmem_call(name, kernel, ins, outs, scratch=(), flops=0):
    nbytes = sum(a.size * a.dtype.itemsize for a in list(ins) + list(outs))
    spec = pl.BlockSpec(memory_space=pltpu.VMEM)
    return pl.pallas_call(
        kernel,
        in_specs=[spec] * len(ins),
        out_specs=[spec] * len(outs),
        out_shape=list(outs),
        scratch_shapes=list(scratch),
        name=name,
        compiler_params=pltpu.CompilerParams(vmem_limit_bytes=56 * 1024 * 1024),
        cost_estimate=pl.CostEstimate(flops=flops, bytes_accessed=nbytes, transcendentals=0),
    )(*ins)


def shape(dims, dtype):
    return jax.ShapeDtypeStruct(tuple(dims), dtype)


def aligned(x, n=8):
    return pl.multiple_of(x, n)


def solution(mesh):
    dp, seq = mesh.shape["dp"], mesh.shape["seq"]
    G = math.gcd(HEADS, seq)
    while G & (G - 1) or (seq // G) & (seq // G - 1):
        G //= 2
    J = seq // G
    heads = HEADS // G
    wide = heads * HD
    nf, nm = dp // 2, dp // 4
    mesh3 = Mesh(mesh.devices.reshape(dp, G, J), ("dp", "g", "j"))
    everyone = ("dp", "g", "j")

    view_of = [0 if d < nf else (1 if d < nf + nm else 2) for d in range(dp)]
    owner = [
        [r // 2 for r in range(dp)],
        [nf + r // 4 for r in range(dp)],
        [nf + nm + r // 4 for r in range(dp)],
    ]
    slot = [[r % 2 for r in range(dp)], [r % 4 for r in range(dp)], [r % 4 for r in range(dp)]]

    def xor(axis, n, size, x):
        return lax.ppermute(x, axis, [(i, i ^ n) for i in range(size)])

    def per_device(
        view_fine, view_mid, view_coarse, grad_fine, grad_mid, grad_coarse, clip_ids,
        attn_in, attn_out, mlp_w, cross_in, cross_out, norm_gains, biases, ffn_bias,
    ):
        tf, tm, tc = view_fine.shape[1], view_mid.shape[1], view_coarse.shape[1]
        U = 2 * tf
        ff = mlp_w.shape[1]
        cells = clip_ids.shape[1]
        d, g, j = lax.axis_index("dp"), lax.axis_index("g"), lax.axis_index("j")
        v = jnp.where(d < nf, 0, jnp.where(d < nf + nm, 1, 2))
        p = jnp.where(d < nf, 0, 1)

        def table(values, index=d):
            out = jnp.int32(values[-1])
            for i in range(len(values) - 1):
                out = jnp.where(index == i, jnp.int32(values[i]), out)
            return out

        def pick(tag, options, dtype=None):
            out = jnp.zeros_like(options[0])
            for k, option in enumerate(options):
                out = jnp.where(tag == k, option, out)
            return out

        def rows_at(x, start, size):
            return lax.dynamic_slice_in_dim(x, start, size, axis=0)

        sizes = (tf, tm, tc)
        moves = [
            (r, owner[w][r], (w, r))
            for w in range(VIEWS)
            for r in range(dp)
            if r != owner[w][r]
        ]
        view_rounds = rounds_of(moves)

        def grow(x, rows):
            if x.shape[0] == rows:
                return x
            return jnp.concatenate([x, jnp.zeros((rows - x.shape[0], x.shape[1]), x.dtype)], axis=0)

        def to_views(fine, mid, coarse):
            mid_p, coarse_p = grow(mid, tf), grow(coarse, tf)
            got = []
            for group in view_rounds:
                n = max(sizes[w] for _, _, (w, _) in group)
                kind = [3] * dp
                for src, _, (w, _) in group:
                    kind[src] = w
                load = pick(table(kind), [fine[:n], mid_p[:n], coarse_p[:n]])
                got.append(grow(lax.ppermute(load, "dp", [(s, t) for s, t, _ in group]), tf))
            local = pick(v, [fine, mid_p, coarse_p])
            rows = []
            for k in range(4):
                tag = [len(got) + 1] * dp
                for i, group in enumerate(view_rounds):
                    for _, dst, (w, r) in group:
                        if slot[w][r] == k:
                            tag[dst] = i + 1
                for r in range(dp):
                    if owner[view_of[r]][r] == r and slot[view_of[r]][r] == k:
                        tag[r] = 0
                rows.append(pick(table(tag), [local] + got))
            as_fine = jnp.concatenate(rows[:2], axis=0)
            as_mid = jnp.concatenate([x[:tm] for x in rows], axis=0)
            pad = jnp.zeros((tf - 2 * tc, fine.shape[1]), fine.dtype)
            as_coarse = jnp.concatenate(
                [rows[0][:tc], rows[1][:tc], pad, rows[2][:tc], rows[3][:tc], pad], axis=0
            )
            return pick(v, [as_fine, as_mid, as_coarse])

        def place(w, k):
            return (tf * k, tm * k, tf * (k // 2) + tc * (k % 2))[w]

        def from_views(x):
            padded = grow(x, U + tf)
            got = []
            for group in view_rounds:
                n = max(sizes[w] for _, _, (w, _) in group)
                start = [0] * dp
                for _, src, (w, r) in group:
                    start[src] = place(w, slot[w][r])
                load = rows_at(padded, table(start), n)
                got.append(grow(lax.ppermute(load, "dp", [(t, s) for s, t, _ in group]), tf))
            local_start = [0] * dp
            for r in range(dp):
                w = view_of[r]
                if owner[w][r] == r:
                    local_start[r] = place(w, slot[w][r])
            local = rows_at(padded, table(local_start), tf)
            outs = []
            for w in range(VIEWS):
                tag = [0] * dp
                for i, group in enumerate(view_rounds):
                    for _, dst, (w2, r) in group:
                        if w2 == w:
                            tag[r] = i + 1
                outs.append(pick(table(tag), [local] + got)[: sizes[w]])
            return outs

        def half_moves(src_of):
            return [(src, dst, h) for dst, (src, h) in src_of.items()]

        q_src = {}
        k_src = {}
        for dst in range(dp):
            if dst < nf:
                q_src[dst] = (nf + (2 * dst) // 4, dst % 2)
            else:
                i = dst - nf
                q_src[dst] = (nf + nm + (2 * i) // 4, i % 2)
                k_src[dst] = (nf + (2 * i) // 4, i % 2)

        def to_cross(x, src_of):
            groups = rounds_of([m for m in half_moves(src_of) if m[0] != m[1]])
            got = []
            for group in groups:
                start = [0] * dp
                for src, _, h in group:
                    start[src] = h * tf
                got.append(
                    lax.ppermute(
                        rows_at(x, table(start), tf), "dp", [(s, t) for s, t, _ in group]
                    )
                )
            start = [0] * dp
            tag = [len(got) + 1] * dp
            for dst, (src, h) in src_of.items():
                if src == dst:
                    start[dst], tag[dst] = h * tf, 0
            for i, group in enumerate(groups):
                for _, dst, _ in group:
                    tag[dst] = i + 1
            return pick(table(tag), [rows_at(x, table(start), tf)] + got)

        def from_cross(x, src_of):
            groups = rounds_of([m for m in half_moves(src_of) if m[0] != m[1]])
            got = [
                lax.ppermute(x, "dp", [(t, s) for s, t, _ in group]) for group in groups
            ]
            halves = []
            for half in range(2):
                tag = [len(got) + 1] * dp
                for dst, (src, h) in src_of.items():
                    if h == half:
                        if src == dst:
                            tag[src] = 0
                        else:
                            for i, group in enumerate(groups):
                                if any(m[1] == dst for m in group):
                                    tag[src] = i + 1
                halves.append(pick(table(tag), [x] + got))
            return jnp.concatenate(halves, axis=0)

        def zeros(rows, like):
            return jnp.zeros((rows, like.shape[1]), like.dtype)

        def q_spread(x):
            z = zeros(tm - tc, x)
            return jnp.where(
                p == 0, x, jnp.concatenate([x[:tc], z, x[tc : 2 * tc], z], axis=0)
            )

        def q_gather(x):
            z = zeros(tf - 2 * tc, x)
            return jnp.where(
                p == 0, x, jnp.concatenate([x[:tc], x[tm : tm + tc], z], axis=0)
            )

        def k_spread(x):
            z = zeros(tf - tm, x)
            return jnp.concatenate([x[:tm], z, x[tm : 2 * tm], z], axis=0)

        def k_gather(x):
            return jnp.concatenate([x[:tm], x[tf : tf + tm]], axis=0)

        def spread_g(x):
            return [x] + [xor("g", m, G, x) for m in range(1, G)]

        def sum_g(pieces):
            out = pieces[0].astype(F32)
            got = [xor("g", m, G, pieces[m].astype(BF)) for m in range(1, G)]
            for x in got:
                out = out + x.astype(F32)
            return out

        def spread_j(x):
            return [x] + [xor("j", n, J, x) for n in range(1, J)]

        n_dev = dp * seq
        gw, fw = norm_gains.shape[1], ffn_bias.shape[1]
        fq = fw // gw
        hid = ff // G
        id_rows = cells // gw
        n_vec = 38 + 3 * fq + id_rows
        vec = jnp.concatenate(
            [
                norm_gains, biases, ffn_bias.reshape(3 * fq, gw),
                clip_ids.astype(BF).reshape(id_rows, gw),
            ],
            axis=0,
        )
        vec = jnp.broadcast_to(vec[None], (n_dev, n_vec, gw))
        vecs = lax.all_to_all(vec, everyone, 0, 0, tiled=True)

        def role():
            kd, kg, kj = lax.axis_index("dp"), lax.axis_index("g"), lax.axis_index("j")
            kv = jnp.where(kd < nf, 0, jnp.where(kd < nf + nm, 1, 2))
            return kd, kg, kj, kv, jnp.where(kd < nf, 0, 1)

        def setup(vec_ref, prm_ref, idq_ref, idk_ref, cidq_ref, cidk_ref, full, ffn):
            kd, kg, kj, kv, kp = role()
            for i in range(n_dev):
                full[:, i * gw : (i + 1) * gw] = vec_ref[i, :38].astype(F32)
                for r in range(3):
                    for t in range(fq):
                        at = i * fw + t * gw
                        ffn[r : r + 1, at : at + gw] = vec_ref[
                            i, 38 + r * fq + t : 39 + r * fq + t
                        ].astype(F32)

            def row(r):
                return full[r : r + 1, :]

            def by_view(rows):
                return jnp.where(kv == 0, rows[0], jnp.where(kv == 1, rows[1], rows[2]))

            def part(x, width):
                out = x[:, :width]
                for i in range(1, G):
                    out = jnp.where(kg == i, x[:, i * width : (i + 1) * width], out)
                return out

            prm_ref[...] = jnp.zeros_like(prm_ref)
            for i in range(2):
                prm_ref[i : i + 1, :] = by_view([row(2 * k + i) for k in range(3)])
            for i in range(6):
                x = by_view([row(10 + 6 * k + i) for k in range(3)])
                if i in (1, 2):
                    prm_ref[2 + i : 3 + i, :wide] = part(x, wide)
                else:
                    prm_ref[2 + i : 3 + i, :] = x
            prm_ref[8:9, :hid] = part(by_view([ffn[k : k + 1, :] for k in range(3)]), hid)
            prm_ref[9:10, :] = by_view([row(6), row(6), row(8)])
            prm_ref[10:11, :] = by_view([row(7), row(9), row(9)])
            prm_ref[11:12, :] = by_view([row(28), row(28), row(33)])
            prm_ref[12:13, :] = by_view([row(29), row(34), row(34)])
            for i in range(3):
                x = jnp.where(kp == 0, row(30 + i), row(35 + i))
                if i < 2:
                    prm_ref[13 + i : 14 + i, :wide] = part(x, wide)
                else:
                    prm_ref[13 + i : 14 + i, :] = x

            starts = []
            for r in range(dp):
                x = vec_ref[r * seq, 38 + 3 * fq :].astype(F32)
                starts.append(
                    [jnp.sum((x < c).astype(F32), keepdims=True) for c in (0.5, 1.5, 2.5)]
                )

            def start_at(index):
                out = starts[0]
                for r in range(1, dp):
                    out = [jnp.where(index == r, b, a) for a, b in zip(out, starts[r])]
                return out

            def ids(first, second, unit, per_cell, cap, u, k, n):
                s = (kg ^ k) * J + (kj ^ n)
                late = u >= unit
                pos = (s * unit + u - jnp.where(late, unit, 0)).astype(F32)
                out = jnp.zeros(u.shape, F32)
                for a, b in zip(first, second):
                    edge = jnp.where(late, b, a) * per_cell.astype(F32)
                    out = out + (pos >= edge).astype(F32)
                out = out + jnp.where(late, 4.0, 0.0)
                return jnp.where(u >= cap, -1.0, out)

            unit = jnp.where(kv == 0, tf, jnp.where(kv == 1, tm, tc))
            per_cell = jnp.where(kv == 0, 4, jnp.where(kv == 1, 2, 1))
            base = jnp.where(kv == 0, 2 * kd, 4 * ((kd - nf) % nm))
            pair_base = 2 * jnp.where(kp == 0, kd, kd - nf)
            k_unit, k_cell = jnp.where(kp == 0, tf, tm), jnp.where(kp == 0, 4, 2)
            q_unit, q_cell = jnp.where(kp == 0, tm, tc), jnp.where(kp == 0, 2, 1)
            for h in range(2):
                first = start_at(base + jnp.where(kv == 0, h, 2 * h))
                second = start_at(base + 2 * h + 1)
                mine = start_at(pair_base + h)
                for k in range(G):
                    lane = lax.broadcasted_iota(jnp.int32, (1, tf), 1)
                    idq_ref[h, :, k * tf : (k + 1) * tf] = ids(
                        first, second, unit, per_cell, 2 * unit, lane, k, 0
                    )
                    lane = lax.broadcasted_iota(jnp.int32, (1, tm), 1)
                    cidq_ref[h, :, k * tm : (k + 1) * tm] = ids(
                        mine, mine, q_unit, q_cell, q_unit, lane, k, 0
                    )
                    for n in range(J):
                        deep = lax.broadcasted_iota(jnp.int32, (tf, 1), 0)
                        at = (n * G + k) * tf
                        idk_ref[h, at : at + tf, :] = ids(
                            first, second, unit, per_cell, 2 * unit, deep, k, n
                        )
                        cidk_ref[h, at : at + tf, :] = ids(
                            mine, mine, k_unit, k_cell, k_unit, deep, k, n
                        )

        prm, idq, idk, cross_idq, cross_idk = vmem_call(
            "setup",
            setup,
            [vecs],
            [
                shape((16, D), F32),
                shape((2, 1, G * tf), F32), shape((2, seq * tf, 1), F32),
                shape((2, 1, G * tm), F32), shape((2, seq * tf, 1), F32),
            ],
            [pltpu.VMEM((38, D), F32), pltpu.VMEM((3, ff), F32)],
        )

        def cols(x, width):
            return lax.dynamic_slice_in_dim(x, g * width, width, axis=-1)

        near = dp == 4

        def both_sides(x):
            up = lax.ppermute(x, "dp", [(0, 1), (1, 2), (2, 3)])
            down = lax.ppermute(x, "dp", [(1, 0), (3, 2)])
            return up, down

        def chunks(x):
            if near:
                up, down = both_sides(x)
                enc = jnp.stack([jnp.where(d == 0, x, up), jnp.where(d == 0, down, x)])
                odd = d % 2 == 1
                cross = jnp.stack([jnp.where(odd, up, x), jnp.where(odd, x, down)])
                return enc, cross
            everything = lax.all_gather(x, "dp", axis=0)
            return everything, everything

        enc_lo = jnp.maximum(d - 1, 0) if near else jnp.int32(0)
        cross_lo = 2 * p if near else jnp.int32(0)

        def start_of(part, n_parts, low, total):
            return part * (total // n_parts) - low * (total // dp)

        def join_j(x):
            xs = spread_j(x)
            parts = []
            for a in range(J):
                out = xs[0]
                for n in range(1, J):
                    out = jnp.where((j ^ n) == a, xs[n], out)
                parts.append(out)
            full = jnp.stack(parts, axis=2)
            return full.reshape(-1, x.shape[-1])

        r_in, r_cross = attn_in.shape[0], cross_in.shape[0]
        r_mlp, r_out, r_co = mlp_w.shape[0], attn_out.shape[0], cross_out.shape[0]

        def half_of(r):
            return (r + 15) // 16 * 8

        h_in, h_cross = half_of(r_in), half_of(r_cross)
        lanes = 2 * wide

        def pack(dst, i, at, r, x):
            half = half_of(r)
            dst[i, at : at + half, :wide] = x[:half]
            dst[i, at : at + r - half, wide:] = x[half:]

        def split_qkv(in_ref, cross_ref, qkv_ref):
            for i in range(G):
                at = slice(i * wide, (i + 1) * wide)
                pack(qkv_ref, i, 0, r_in, in_ref[:, at])
                pack(qkv_ref, i, h_in, r_cross, cross_ref[:, at])

        def split_mlp(mlp_ref, mlp_out):
            for i in range(G):
                mlp_out[i] = mlp_ref[:, i * hid : (i + 1) * hid]

        if near:
            (qkv,) = vmem_call(
                "split_qkv", split_qkv, [attn_in, cross_in],
                [shape((G, h_in + h_cross, lanes), BF)],
            )
            qkv = lax.all_to_all(qkv, "g", 0, 0, tiled=True)
            (mlp,) = vmem_call("split_mlp", split_mlp, [mlp_w], [shape((G, r_mlp, hid), BF)])
            mlp = lax.all_to_all(mlp, "g", 0, 0, tiled=True)
        else:
            qkv = lax.all_to_all(
                jnp.concatenate([attn_in, cross_in], axis=0), "g", 1, 0, tiled=True
            ).reshape(G, r_in + r_cross, wide)
            mlp = lax.all_to_all(mlp_w, "g", 1, 0, tiled=True).reshape(G, r_mlp, hid)

        def offset(kind, total, kd, kv, kp):
            low = jnp.maximum(kd - 1, 0)
            return kv * (total // 3) - low * (total // 4) if kind == "enc" else kp * 0

        def assemble(name, x, parts, width):
            up, down = both_sides(x)
            srcs = [*spread_j(x), *spread_j(up), *spread_j(down)]
            packed = width != x.shape[2]
            outs, scratch = [], []
            for kind, _, r in parts:
                outs.append(shape((n_dev * r // (3 if kind == "enc" else 2), width), BF))
                scratch.append(pltpu.VMEM((n_dev * r // 2, width), F32))

            def kernel(*refs):
                kd, kg, kj, kv, kp = role()
                own, up_r, down_r = refs[:J], refs[J : 2 * J], refs[2 * J : 3 * J]
                out_refs = refs[3 * J : 3 * J + len(parts)]
                frames = refs[3 * J + len(parts) :]

                for (kind, first, r), frame in zip(parts, frames):

                    def put(t, group, first=first, r=r, frame=frame):
                        for n, ref in enumerate(group):
                            for i in range(G):
                                at = ((t * G + i) * J + (kj ^ n)) * r
                                size = half_of(r) if packed else r
                                frame[pl.ds(aligned(at), size), :] = ref[
                                    i, first : first + size, :width
                                ].astype(F32)
                                if packed:
                                    frame[pl.ds(aligned(at + size), r - size), :] = ref[
                                        i, first : first + r - size, width:
                                    ].astype(F32)

                    low = kd == 0 if kind == "enc" else kd % 2 == 0

                    @pl.when(low)
                    def _(put=put):
                        put(0, own)
                        put(1, down_r)

                    @pl.when(jnp.logical_not(low))
                    def _(put=put):
                        put(0, up_r)
                        put(1, own)

                for (kind, _, r), frame, out in zip(parts, frames, out_refs):
                    at = aligned(offset(kind, n_dev * r, kd, kv, kp))
                    out[...] = frame[pl.ds(at, out.shape[0]), :].astype(BF)

            return vmem_call(name, kernel, srcs, outs, scratch)

        if near:
            w_in, c_in = assemble(
                "assemble_in", qkv, [("enc", 0, r_in), ("cross", h_in, r_cross)], wide
            )
            (w_mlp,) = assemble("assemble_mlp", mlp, [("enc", 0, r_mlp)], hid)
        else:
            enc_c, cross_c = chunks(qkv)
            w_in = rows_at(
                join_j(enc_c[:, :, :r_in]), start_of(v, 3, enc_lo, n_dev * r_in), 3 * D
            )
            c_in = rows_at(
                join_j(cross_c[:, :, r_in:]), start_of(p, 2, cross_lo, n_dev * r_cross), 3 * D
            )
            enc_c, _ = chunks(mlp)
            w_mlp = rows_at(join_j(enc_c), start_of(v, 3, enc_lo, n_dev * r_mlp), 2 * D)
        enc_c, cross_c = chunks(jnp.concatenate([attn_out, cross_out], axis=0))
        planes = enc_c.shape[0]
        outs = jnp.concatenate([enc_c[:, :r_out], cross_c[:, r_out:]], axis=1)
        outs = lax.all_gather(outs.reshape(-1, D), ("g", "j"), axis=0)
        outs = outs.reshape(seq, planes, r_out + r_co, D)

        def arrange(x_ref, w_ref, c_ref, frame, cross_frame):
            kd, kg, kj, kv, kp = role()
            for t in range(planes):
                for i in range(seq):
                    at = (t * seq + i) * r_out
                    frame[at : at + r_out, :] = x_ref[i, t, :r_out].astype(F32)
                    at = (t * seq + i) * r_co
                    cross_frame[at : at + r_co, :] = x_ref[i, t, r_out:].astype(F32)
            low = jnp.maximum(kd - 1, 0) if near else 0
            first = kv * (n_dev * r_out // 3) - low * (n_dev * r_out // dp)
            cross_first = 0 if near else kp * (n_dev * r_co // 2)
            for m in range(G):
                to = slice(m * wide, (m + 1) * wide)
                at = aligned(first + (kg ^ m) * wide)
                w_ref[to, :] = frame[pl.ds(at, wide), :].astype(BF)
                at = aligned(cross_first + (kg ^ m) * wide)
                c_ref[to, :] = cross_frame[pl.ds(at, wide), :].astype(BF)

        w_out, c_out = vmem_call(
            "arrange_out", arrange, [outs], [shape((D, D), BF), shape((D, D), BF)],
            [
                pltpu.VMEM((planes * seq * r_out, D), F32),
                pltpu.VMEM((planes * seq * r_co, D), F32),
            ],
        )
        Uq = 2 * tm
        dot = 2 * D * D

        def piece(rows, dtype=BF, width=D):
            return shape((rows, width), dtype)

        def stack(rows, width, dtype=BF):
            return shape((G, rows, width), dtype)

        def loop(body):
            lax.fori_loop(0, G, lambda k, c: (body(k), c)[1], 0)

        def stage(refs, dst):
            for i, ref in enumerate(refs):
                dst[i] = ref[...]

        def deliver(src, own_ref, other_refs):
            own_ref[...] = src[0]
            for m, ref in enumerate(other_refs):
                ref[...] = src[m + 1].astype(BF)

        def send(pieces):
            return [xor("g", m + 1, G, x) for m, x in enumerate(pieces)]

        x_own = to_views(view_fine[0], view_mid[0], view_coarse[0])
        xs = spread_g(x_own)

        def k_qkv(*refs):
            x_refs, (w, prm_r, x_ref, a_ref, q_ref, kv_ref) = refs[:G], refs[G:]
            stage(x_refs, x_ref)

            def body(k):
                z, _ = unit_rows(x_ref[k].astype(F32))
                a = (z * prm_r[0:1] + prm_r[2:3]).astype(BF)
                a_ref[k] = a
                q_ref[k] = (mm(a, w[:D]) + prm_r[3:4, :wide]).astype(BF)
                kv_ref[k, :, :wide] = mm(a, w[D : 2 * D]).astype(BF)
                kv_ref[k, :, wide:] = (mm(a, w[2 * D :]) + prm_r[4:5, :wide]).astype(BF)

            loop(body)

        x_all, a, q, kv = vmem_call(
            "qkv", k_qkv, [*xs, w_in, prm],
            [stack(U, D), stack(U, D), stack(U, wide), stack(U, 2 * wide)],
            flops=dot * U * G * 3 // 4 // D,
        )

        def halves(t):
            return t.reshape(G, 2, -1, t.shape[-1])

        q4 = halves(q)
        kvs = [halves(t) for t in spread_j(kv)]
        o, lse = attend(heads, idq, idk, q4, kvs)
        os = spread_g(o.reshape(G, U, wide))

        def gelu_of(u):
            cdf = 0.5 * (1.0 + lax.erf(u * (0.5**0.5)))
            return u * cdf, cdf + u * jnp.exp(-0.5 * u * u) * (1.0 / math.sqrt(2.0 * math.pi))

        def k_mlp(*refs):
            o_refs, (x_ref, wo, wm, prm_r, *rest) = refs[:G], refs[G:]
            oa_ref, c_ref, slope_ref, e_ref, h_ref, y_ref = rest[:6]
            others, parts = rest[6:-1], rest[-1]

            def body(k):
                o_k = jnp.concatenate([r[k ^ m] for m, r in enumerate(o_refs)], axis=1)
                oa_ref[k] = o_k
                h = x_ref[k].astype(F32) + (mm(o_k, wo[...]) + prm_r[5:6])

                @pl.when(k == 0)
                def _():
                    h_ref[...] = h

                z, _ = unit_rows(h)
                c = (z * prm_r[1:2] + prm_r[6:7]).astype(BF)
                c_ref[k] = c
                e, slope = gelu_of(mm(c, wm[:D]) + prm_r[8:9, :hid])
                e = e.astype(BF)
                e_ref[k] = e
                slope_ref[k] = slope.astype(BF)
                parts[k] = mm_nt(e, wm[D:])

            loop(body)
            y_ref[...] = parts[0] + h_ref[...] + prm_r[7:8]
            for m, ref in enumerate(others):
                ref[...] = parts[m + 1].astype(BF)

        o_all, c, slope, e, h_own, y_own, *y_out = vmem_call(
            "mlp", k_mlp, [*os, x_all, w_out, w_mlp, prm],
            [stack(U, D), stack(U, D), stack(U, hid), stack(U, hid), piece(U, F32), piece(U, F32)]
            + [piece(U)] * (G - 1),
            [pltpu.VMEM((G, U, D), F32)],
            flops=3 * dot * U * G // D,
        )
        y_in = send(y_out)

        def total_of(own_ref, refs):
            out = own_ref[...]
            for ref in refs:
                out = out + ref[...].astype(F32)
            return out

        def k_norm(*refs):
            own, got, (prm_r, y_ref, zy_ref, rs_ref, kn_ref, qn_ref) = refs[0], refs[1:G], refs[G:]
            y = total_of(own, got)
            y_ref[...] = y
            z, rs = unit_rows(y)
            zy_ref[...] = z
            rs_ref[...] = rs
            kn_ref[...] = (z * prm_r[10:11] + prm_r[12:13]).astype(BF)
            qn_ref[...] = (z * prm_r[9:10] + prm_r[11:12]).astype(BF)

        y, zy, rs_y, kn_v, qn_v = vmem_call(
            "norm_y", k_norm, [y_own, *y_in, prm],
            [piece(U, F32), piece(U, F32), piece(U, F32, 1), piece(U), piece(U)],
        )
        grad_own = to_views(grad_fine[0], grad_mid[0], grad_coarse[0])
        gc_own = q_spread(to_cross(grad_own, q_src))
        gcs = spread_g(gc_own)
        qn_own = q_spread(to_cross(qn_v, q_src))
        kn_own = jnp.where(p == 0, kn_v, k_spread(to_cross(kn_v, k_src)))
        qns, kns = spread_g(qn_own), spread_g(kn_own)

        def k_given(*refs):
            g_refs, (w, g_ref, do_ref) = refs[:G], refs[G:]
            stage(g_refs, g_ref)
            for k in range(G):
                do_ref[k] = mm_nt(g_ref[k], w[:wide]).astype(BF)

        gc, d_att = vmem_call(
            "given", k_given, [*gcs, c_out], [stack(Uq, D), stack(Uq, wide)],
            flops=dot * Uq * G // 4 // D,
        )

        def k_cross(*refs):
            q_refs, k_refs, (w, prm_r, qn_ref, kn_ref, q_ref, kv_ref) = (
                refs[:G], refs[G : 2 * G], refs[2 * G :],
            )
            stage(q_refs, qn_ref)
            stage(k_refs, kn_ref)

            def body(k):
                q_ref[k] = (mm(qn_ref[k], w[:D]) + prm_r[13:14, :wide]).astype(BF)
                x = kn_ref[k]
                kv_ref[k, :, :wide] = mm(x, w[D : 2 * D]).astype(BF)
                kv_ref[k, :, wide:] = (mm(x, w[2 * D :]) + prm_r[14:15, :wide]).astype(BF)

            loop(body)

        qn, kn, cross_q, cross_kv = vmem_call(
            "cross", k_cross, [*qns, *kns, c_in, prm],
            [stack(Uq, D), stack(U, D), stack(Uq, wide), stack(U, 2 * wide)],
            flops=dot * U * G * 5 // 8 // D,
        )
        ckvs = [halves(t) for t in spread_j(cross_kv)]
        c_att, dq_c, dkvs = attend_both(
            heads, cross_idq, cross_idk, halves(cross_q), halves(d_att), ckvs
        )
        dkv_c_in = [dkvs[0]] + [xor("j", n, J, dkvs[n]) for n in range(1, J)]
        dkv_c_in = [t.reshape(G, U, 2 * wide) for t in dkv_c_in]
        dq_c = dq_c.reshape(G, Uq, wide)

        def k_dqn(dq_ref, w, sum_ref, own, *rest):
            others, parts = rest[:-1], rest[-1]
            sum_ref[...] = jnp.zeros_like(sum_ref)

            def body(k):
                x = dq_ref[k]
                parts[k] = mm_nt(x, w[:D])
                sum_ref[...] += jnp.sum(x.astype(F32), axis=0, keepdims=True)

            loop(body)
            deliver(parts, own, others)

        dcq, dqn_own, *dqn_out = vmem_call(
            "dqn", k_dqn, [dq_c, c_in],
            [piece(1, F32, wide), piece(Uq, F32)] + [piece(Uq)] * (G - 1),
            [pltpu.VMEM((G, Uq, D), F32)],
            flops=dot * Uq * G // 4 // D,
        )
        dqn_in = send(dqn_out)

        def k_dkn(*refs):
            in_refs, (w, dkv_ref, sum_ref, own, *rest) = refs[:J], refs[J:]
            others, parts = rest[:-1], rest[-1]
            sum_ref[...] = jnp.zeros_like(sum_ref)

            def body(k):
                x = in_refs[0][k].astype(F32)
                for r in in_refs[1:]:
                    x = x + r[k].astype(F32)
                x = x.astype(BF)
                dkv_ref[k] = x
                sum_ref[...] += jnp.sum(x.astype(F32), axis=0, keepdims=True)
                parts[k] = mm_nt(x[:, :wide], w[D : 2 * D]) + mm_nt(x[:, wide:], w[2 * D :])

            loop(body)
            deliver(parts, own, others)

        dkv_c, dckv, dkn_own, *dkn_out = vmem_call(
            "dkn", k_dkn, [*dkv_c_in, c_in],
            [stack(U, 2 * wide), piece(1, F32, 2 * wide), piece(U, F32)] + [piece(U)] * (G - 1),
            [pltpu.VMEM((G, U, D), F32)],
            flops=dot * U * G // 2 // D,
        )
        dkn_in = send(dkn_out)

        def gather_sum(own, got):
            out = own
            for x in got:
                out = out + x.astype(F32)
            return out.astype(BF)

        dqn = gather_sum(dqn_own, dqn_in)
        dqn_v = from_cross(q_gather(dqn), q_src)
        dkn = gather_sum(dkn_own, dkn_in)
        dkn_v = jnp.where(v == 0, dkn, from_cross(k_gather(dkn), k_src))

        def k_dy(grad_ref, zy_ref, rs_ref, dq_ref, dk_ref, prm_r, dy_ref, dm_ref, sum_ref):
            _, _, _, kv, _ = role()
            z = zy_ref[...]
            grad = grad_ref[...].astype(F32)
            dqv = jnp.where(kv == 0, 0.0, dq_ref[...].astype(F32))
            dkv = jnp.where(kv == 2, 0.0, dk_ref[...].astype(F32))
            dy = grad + unit_back(z, rs_ref[...], dqv * prm_r[9:10] + dkv * prm_r[10:11])
            dm = dy.astype(BF)
            dy_ref[...] = dy
            dm_ref[...] = dm
            for i, x in enumerate([dqv * z, dqv, dkv * z, dkv, grad, dm.astype(F32)]):
                sum_ref[i : i + 1, :] = jnp.sum(x, axis=0, keepdims=True)

        dy, dm_own, sums_y = vmem_call(
            "dy", k_dy, [grad_own, zy, rs_y, dqn_v, dkn_v, prm],
            [piece(U, F32), piece(U), piece(8, F32)],
        )

        dms = spread_g(dm_own)

        def k_mlp_back(*refs):
            m_refs, (slope_ref, wm, dm_ref, du_ref, sum_ref, own, *rest) = refs[:G], refs[G:]
            others, parts = rest[:-1], rest[-1]
            stage(m_refs, dm_ref)
            sum_ref[...] = jnp.zeros_like(sum_ref)

            def body(k):
                du = (mm(dm_ref[k], wm[D:]) * slope_ref[k].astype(F32)).astype(BF)
                du_ref[k] = du
                sum_ref[...] += jnp.sum(du.astype(F32), axis=0, keepdims=True)
                parts[k] = mm_nt(du, wm[:D])

            loop(body)
            deliver(parts, own, others)

        dm, du, dbf, dc_own, *dc_out = vmem_call(
            "mlp_back", k_mlp_back, [*dms, slope, w_mlp],
            [stack(U, D), stack(U, hid), piece(1, F32, hid), piece(U, F32)]
            + [piece(U)] * (G - 1),
            [pltpu.VMEM((G, U, D), F32)],
            flops=2 * dot * U * G // D,
        )
        dc_in = send(dc_out)

        def k_dh(*refs):
            own, got, (h_ref, dy_ref, prm_r, dh_ref, dhb_ref, sum_ref) = (
                refs[0], refs[1:G], refs[G:],
            )
            dn = total_of(own, got)
            z, rs = unit_rows(h_ref[...])
            dh = dy_ref[...] + unit_back(z, rs, dn * prm_r[1:2])
            dh_ref[...] = dh
            dhb = dh.astype(BF)
            dhb_ref[...] = dhb
            for i, x in enumerate([dn * z, dn, dhb.astype(F32)]):
                sum_ref[i : i + 1, :] = jnp.sum(x, axis=0, keepdims=True)

        dh, dh_own, sums_h = vmem_call(
            "dh", k_dh, [dc_own, *dc_in, h_own, dy, prm],
            [piece(U, F32), piece(U), piece(8, F32)],
        )
        dhs = spread_g(dh_own)
        dq, dkvs = attend_back(heads, idq, idk, q4, lse, w_out, dhs, kvs)
        dkv_in = [dkvs[0]] + [xor("j", n, J, dkvs[n]) for n in range(1, J)]
        dkv_in = [t.reshape(G, U, 2 * wide) for t in dkv_in]
        dq = dq.reshape(G, U, wide)

        def k_da(*refs):
            in_refs, (dq_ref, w, dkv_ref, sum_ref, own, *rest) = refs[:J], refs[J:]
            others, parts = rest[:-1], rest[-1]
            sum_ref[...] = jnp.zeros_like(sum_ref)

            def body(k):
                x = in_refs[0][k].astype(F32)
                for r in in_refs[1:]:
                    x = x + r[k].astype(F32)
                x = x.astype(BF)
                dkv_ref[k] = x
                dqk = dq_ref[k]
                sum_ref[0:1, :wide] += jnp.sum(dqk.astype(F32), axis=0, keepdims=True)
                sum_ref[1:2, :wide] += jnp.sum(
                    x[:, wide:].astype(F32), axis=0, keepdims=True
                )
                parts[k] = (
                    mm_nt(dqk, w[:D])
                    + mm_nt(x[:, :wide], w[D : 2 * D])
                    + mm_nt(x[:, wide:], w[2 * D :])
                )

            loop(body)
            deliver(parts, own, others)

        dkv, sums_q, da_own, *da_out = vmem_call(
            "da", k_da, [*dkv_in, dq, w_in],
            [stack(U, 2 * wide), piece(8, F32, wide), piece(U, F32)] + [piece(U)] * (G - 1),
            [pltpu.VMEM((G, U, D), F32)],
            flops=dot * U * G * 3 // 4 // D,
        )
        da_in = send(da_out)

        def k_dx(*refs):
            own, got, (x_ref, dh_ref, prm_r, dx_ref, sum_ref) = refs[0], refs[1:G], refs[G:]
            da = total_of(own, got)
            z, rs = unit_rows(x_ref[...].astype(F32))
            dx_ref[...] = (dh_ref[...] + unit_back(z, rs, da * prm_r[0:1])).astype(BF)
            for i, x in enumerate([da * z, da]):
                sum_ref[i : i + 1, :] = jnp.sum(x, axis=0, keepdims=True)

        dx, sums_x = vmem_call(
            "dx", k_dx, [da_own, *da_in, x_own, dh, prm], [piece(U), piece(8, F32)]
        )

        cos = spread_g(c_att.reshape(G, Uq, wide))

        def k_mix(*refs):
            o_refs, (w, prm_r, o_ref, mix_ref) = refs[:G], refs[G:]
            for k in range(G):
                o_ref[k] = jnp.concatenate([r[k ^ m] for m, r in enumerate(o_refs)], axis=1)
            mix_ref[...] = (mm(o_ref[0], w[...]) + prm_r[15:16]).astype(BF)

        cross_o, mix = vmem_call(
            "mix", k_mix, [*cos, c_out, prm], [stack(Uq, D), piece(Uq)],
            flops=dot * Uq // D,
        )
        mix_v = jnp.where(v == 0, 0.0, from_cross(q_gather(mix), q_src).astype(F32))
        out_f, out_m, out_c = from_views((y + mix_v).astype(BF))
        dx_f, dx_m, dx_c = from_views(dx)

        def my_rows(x):
            return lax.dynamic_index_in_dim(x, j, axis=2, keepdims=False)

        def send_home(grad, total, enc):
            width = grad.shape[1]
            r = total // n_dev
            if near:
                frame_rows, n_planes = total // 2, 2
                low = enc_lo if enc else cross_lo
            else:
                frame_rows, n_planes, low = total, dp, jnp.int32(0)
            if grad.shape[0] != frame_rows:
                part, n_parts = (v, 3) if enc else (p, 2)
                grad = lax.dynamic_update_slice_in_dim(
                    jnp.zeros((frame_rows, width), BF), grad.astype(BF),
                    start_of(part, n_parts, low, total), axis=0,
                )
            x = grad.astype(BF).reshape(n_planes, G, J, r, width)
            acc = lax.dynamic_index_in_dim(x, j, axis=2, keepdims=False).astype(F32)
            for n in range(1, J):
                part = lax.dynamic_index_in_dim(x, j ^ n, axis=2, keepdims=False)
                acc = acc + xor("j", n, J, part).astype(F32)
            if not near:
                acc = lax.psum_scatter(acc, "dp", scatter_dimension=0, tiled=False)
            elif enc:
                own = jnp.where(d == 0, acc[0], acc[1])
                other = jnp.where(d == 0, acc[1], acc[0]).astype(BF)
                down = lax.ppermute(other, "dp", [(1, 0), (2, 1), (3, 2)])
                upward = lax.ppermute(other, "dp", [(0, 1)])
                acc = own + down.astype(F32) + upward.astype(F32)
            else:
                odd = d % 2 == 1
                own = jnp.where(odd, acc[1], acc[0])
                other = jnp.where(odd, acc[0], acc[1]).astype(BF)
                acc = own + xor("dp", 1, dp, other).astype(F32)
            acc = acc.astype(BF).reshape(G * r, width)
            return lax.all_to_all(acc, "g", 0, 1, tiled=True).astype(F32)

        def in_order(w):
            return jnp.concatenate(
                [rows_at(w, (g ^ a) * wide, wide) for a in range(G)], axis=0
            )

        def home(name, arrays, parts, width):
            ins = list(arrays)
            n_rows = sum(r for _, r, _ in parts)
            outs = [shape((2, G, n_rows, width), BF) for _ in range(J)]
            scratch = [pltpu.VMEM((n_dev * r // 2, width), F32) for _, r, _ in parts]

            def kernel(*refs):
                kd, kg, kj, kv, kp = role()
                in_refs = refs[: len(ins)]
                out_refs = refs[len(ins) : len(ins) + J]
                frames = refs[len(ins) + J :]

                def value(key):
                    if isinstance(key, list):
                        return jnp.concatenate([in_refs[i][...] for i in key], axis=0)
                    index, at, size = key if isinstance(key, tuple) else (key, 0, None)
                    x = in_refs[index][...]
                    x = x.reshape(-1, x.shape[-1])
                    return x if size is None else x[:, at : at + size]

                first = 0
                for (kind, r, mats), frame in zip(parts, frames):
                    if kind == "enc":
                        frame[...] = jnp.zeros_like(frame)
                    base = offset(kind, n_dev * r, kd, kv, kp)
                    for i, (left, right, grouped) in enumerate(mats):
                        b = value(right)
                        if grouped:
                            x = b[:, :wide]
                            for k in range(1, G):
                                x = jnp.where(kg == k, b[:, k * wide : (k + 1) * wide], x)
                            res = mm_tn(value(left), x)
                            for m in range(G):
                                at = aligned(base + i * D + (kg ^ m) * wide)
                                frame[pl.ds(at, wide), :] = res[m * wide : (m + 1) * wide]
                        else:
                            at = aligned(base + i * D)
                            frame[pl.ds(at, D), :] = mm_tn(value(left), b)
                    own = jnp.where(kd == 0, 0, 1) if kind == "enc" else kd % 2
                    for n in range(J):
                        for side in range(2):
                            t = own if side == 0 else 1 - own
                            for k in range(G):
                                at = aligned(((t * G + k) * J + (kj ^ n)) * r)
                                out_refs[n][side, k, first : first + r, :] = frame[
                                    pl.ds(at, r), :
                                ].astype(BF)
                    first += r

            flops = 2 * D * D * width * sum(len(m) for _, _, m in parts)
            mine, *others = vmem_call(name, kernel, ins, outs, scratch, flops)
            acc = mine.astype(F32)
            for n in range(1, J):
                acc = acc + xor("j", n, J, others[n - 1]).astype(F32)
            own, other = acc[0], acc[1].astype(BF)
            if parts[0][0] == "enc":
                down = lax.ppermute(other, "dp", [(1, 0), (2, 1), (3, 2)])
                upward = lax.ppermute(other, "dp", [(0, 1)])
                own = own + down.astype(F32) + upward.astype(F32)
            else:
                own = own + xor("dp", 1, dp, other).astype(F32)
            return lax.all_to_all(own.astype(BF), "g", 0, 0, tiled=True)

        if near:
            pair_kv = [(3, i * wide, wide) for i in range(2)]
            x_cross = home(
                "home_cross", [qn, kn, dq_c, dkv_c, cross_o, gc],
                [
                    (
                        "cross", r_cross,
                        [(0, 2, False), (1, pair_kv[0], False), (1, pair_kv[1], False)],
                    ),
                    ("cross", r_co, [(4, 5, True)]),
                ],
                wide,
            )
            x_mlp = home(
                "home_mlp", [c, du, dm, e],
                [("enc", r_mlp, [(0, 1, False), (2, 3, False)])],
                hid,
            )
            own_kv = [(2, i * wide, wide) for i in range(2)]
            x_enc = home(
                "home_enc", [a, dq, dkv, o_all, *dhs],
                [
                    (
                        "enc", r_in,
                        [(0, 1, False), (0, own_kv[0], False), (0, own_kv[1], False)],
                    ),
                    ("enc", r_out, [(3, [4 + i for i in range(G)], True)]),
                ],
                wide,
            )

            def landed(cross_ref, mlp_ref, enc_ref, gi_ref, go_ref, gm_ref, gci_ref, gco_ref):
                for i in range(G):
                    at = slice(i * wide, (i + 1) * wide)
                    gi_ref[:, at] = enc_ref[i, :r_in].astype(F32)
                    go_ref[:, at] = enc_ref[i, r_in:].astype(F32)
                    gci_ref[:, at] = cross_ref[i, :r_cross].astype(F32)
                    gco_ref[:, at] = cross_ref[i, r_cross:].astype(F32)
                    gm_ref[:, i * hid : (i + 1) * hid] = mlp_ref[i].astype(F32)

            grad_in, grad_out, grad_mlp, grad_cin, grad_cout = vmem_call(
                "landed", landed, [x_cross, x_mlp, x_enc],
                [
                    shape(attn_in.shape, F32), shape(attn_out.shape, F32),
                    shape(mlp_w.shape, F32), shape(cross_in.shape, F32),
                    shape(cross_out.shape, F32),
                ],
            )
        else:
            flat = lambda t: t.reshape(-1, t.shape[-1])
            a_f, c_f, q_f, k_f = flat(a), flat(c), flat(qn), flat(kn)
            ckv, skv = flat(dkv_c), flat(dkv)
            dh_all = jnp.concatenate(dhs, axis=0)
            g_cin = jnp.concatenate(
                [mm_tn(q_f, flat(dq_c)), mm_tn(k_f, ckv[:, :wide]), mm_tn(k_f, ckv[:, wide:])],
                axis=0,
            )
            g_cout = in_order(mm_tn(flat(cross_o), cols(flat(gc), wide)))
            g_mlp = jnp.concatenate([mm_tn(c_f, flat(du)), mm_tn(flat(dm), flat(e))], axis=0)
            g_out = in_order(mm_tn(flat(o_all), cols(dh_all, wide)))
            g_in = jnp.concatenate(
                [mm_tn(a_f, flat(dq)), mm_tn(a_f, skv[:, :wide]), mm_tn(a_f, skv[:, wide:])],
                axis=0,
            )
            grad_cin = send_home(g_cin, n_dev * r_cross, False)
            grad_cout = send_home(g_cout, n_dev * r_co, False)
            grad_mlp = send_home(g_mlp, n_dev * r_mlp, True)
            grad_out = send_home(g_out, n_dev * r_out, True)
            grad_in = send_home(g_in, n_dev * r_in, True)

        def deal(sy, sh, sx, sq, cq_ref, ckv_ref, bf_ref, out_ref, full, ffn):
            kd, kg, kj, kv, kp = role()

            def if_view(k, x):
                return jnp.where(kv == k, x, 0.0)

            full[...] = jnp.zeros_like(full)
            ffn[...] = jnp.zeros_like(ffn)

            def at_cols(row, on, x):
                for k in range(G):
                    full[row : row + 1, k * wide : (k + 1) * wide] = jnp.where(
                        jnp.logical_and(on, kg == k), x, 0.0
                    )

            for k in range(3):
                full[2 * k : 2 * k + 1, :] = if_view(k, sx[0:1])
                full[2 * k + 1 : 2 * k + 2, :] = if_view(k, sh[0:1])
                at = 10 + 6 * k
                full[at : at + 1, :] = if_view(k, sx[1:2])
                at_cols(at + 1, kv == k, sq[0:1])
                at_cols(at + 2, kv == k, sq[1:2])
                full[at + 3 : at + 4, :] = if_view(k, sh[2:3])
                full[at + 4 : at + 5, :] = if_view(k, sh[1:2])
                full[at + 5 : at + 6, :] = if_view(k, sy[5:6])
                for i in range(G):
                    ffn[k : k + 1, i * hid : (i + 1) * hid] = jnp.where(
                        jnp.logical_and(kv == k, kg == i), bf_ref[...], 0.0
                    )
            for k in range(2):
                full[6 + 2 * k : 7 + 2 * k, :] = if_view(k + 1, sy[0:1])
                full[7 + 2 * k : 8 + 2 * k, :] = if_view(k, sy[2:3])
                at = 28 + 5 * k
                full[at : at + 1, :] = if_view(k + 1, sy[1:2])
                full[at + 1 : at + 2, :] = if_view(k, sy[3:4])
                at_cols(at + 2, kp == k, cq_ref[...])
                at_cols(at + 3, kp == k, ckv_ref[:, wide:])
                full[at + 4 : at + 5, :] = if_view(k + 1, sy[4:5])
            for i in range(n_dev):
                out_ref[i, :38, :] = full[:, i * gw : (i + 1) * gw]
                for r in range(3):
                    for t in range(fq):
                        to = 38 + r * fq + t
                        out_ref[i, to : to + 1, :] = ffn[
                            r : r + 1, i * fw + t * gw : i * fw + (t + 1) * gw
                        ]

        (small,) = vmem_call(
            "deal", deal, [sums_y, sums_h, sums_x, sums_q, dcq, dckv, dbf],
            [shape((n_dev, 38 + 3 * fq, gw), F32)],
            [pltpu.VMEM((38, D), F32), pltpu.VMEM((3, ff), F32)],
        )
        small = lax.all_to_all(small, everyone, 0, 0, tiled=True)

        def collect(x_ref, g_ref, b_ref, f_ref):
            x = jnp.sum(x_ref[...], axis=0)
            g_ref[...] = x[:10]
            b_ref[...] = x[10:38]
            for r in range(3):
                for t in range(fq):
                    at = 38 + r * fq + t
                    f_ref[r : r + 1, t * gw : (t + 1) * gw] = x[at : at + 1]

        grad_gains, grad_bias, grad_ffn = vmem_call(
            "collect", collect, [small],
            [shape(norm_gains.shape, F32), shape(biases.shape, F32), shape(ffn_bias.shape, F32)],
        )
        return (
            out_f[None], out_m[None], out_c[None],
            dx_f.astype(F32)[None], dx_m.astype(F32)[None], dx_c.astype(F32)[None],
            grad_in, grad_out, grad_mlp, grad_cin, grad_cout,
            grad_gains, grad_bias, grad_ffn,
        )

    tokens = P("dp", ("g", "j"), None)
    rows = P(everyone, None)
    columns = P(None, everyone)
    return jax.shard_map(
        per_device,
        mesh=mesh3,
        in_specs=(tokens,) * 6 + (P("dp", None),) + (rows,) * 5 + (columns,) * 3,
        out_specs=(tokens,) * 6 + (rows,) * 5 + (columns,) * 3,
        check_vma=False,
    )
```

```python
import math

import jax
import jax.numpy as jnp
from jax import lax
from jax.experimental import pallas as pl
from jax.experimental.pallas import tpu as pltpu
from jax.sharding import Mesh, PartitionSpec as P

D = 768
HEADS = 12
HD = 64
VIEWS = 3
EPS = 1e-06
NEG = -1e30
SCALE = HD**-0.5
BF = jnp.bfloat16
F32 = jnp.float32


def mm(a, b):
    return lax.dot_general(a, b, (((1,), (0,)), ((), ())), preferred_element_type=F32)


def mm_nt(a, b):
    return lax.dot_general(a, b, (((1,), (1,)), ((), ())), preferred_element_type=F32)


def mm_tn(a, b):
    return lax.dot_general(a, b, (((0,), (0,)), ((), ())), preferred_element_type=F32)


def unit_rows(u):
    centre = jnp.mean(u, axis=-1, keepdims=True)
    spread = u - centre
    rs = lax.rsqrt(jnp.mean(spread * spread, axis=-1, keepdims=True) + EPS)
    return spread * rs, rs


def unit_back(z, rs, dz):
    return rs * (
        dz - jnp.mean(dz, axis=-1, keepdims=True) - z * jnp.mean(dz * z, axis=-1, keepdims=True)
    )


def gelu_parts(u):
    phi = 0.5 * lax.erfc(u * (-(0.5**0.5)))
    return phi


def gelu_slope(u):
    return gelu_parts(u) + u * jnp.exp(-0.5 * u * u) * (1.0 / math.sqrt(2.0 * math.pi))


def rounds_of(moves):
    rounds = []
    for move in moves:
        for group in rounds:
            if all(move[0] != other[0] and move[1] != other[1] for other in group):
                group.append(move)
                break
        else:
            rounds.append([move])
    return rounds


def attend_kernel(heads, parts, idq_ref, idk_ref, q_ref, *rest):
    kv_refs, (o_ref, lse_ref) = rest[:parts], rest[parts:]
    wide = heads * HD
    q = q_ref[...].reshape(-1, wide)
    kv = jnp.concatenate([r[...].reshape(-1, 2 * wide) for r in kv_refs], axis=0)
    allowed = idk_ref[0] == idq_ref[0]
    outs = []
    for n in range(heads):
        cols = slice(n * HD, (n + 1) * HD)
        v_cols = slice(wide + n * HD, wide + (n + 1) * HD)
        s = jnp.where(allowed, mm_nt(kv[:, cols], q[:, cols]) * SCALE, NEG)
        top = jnp.max(s, axis=0, keepdims=True)
        p = jnp.exp(s - top)
        total = jnp.sum(p, axis=0, keepdims=True)
        lse_ref[0, n : n + 1, :] = top + jnp.log(total)
        pb = (p * (1.0 / total)).astype(BF)
        outs.append(mm(kv[:, v_cols].T, pb).T)
    put_half(o_ref, jnp.concatenate(outs, axis=1).astype(BF))


def put_half(o_ref, o):
    wide = o.shape[1]
    o = o.reshape(o_ref.shape[:2] + (wide,))

    @pl.when(pl.program_id(0) == 0)
    def _():
        o_ref[:, :, :wide] = o

    @pl.when(pl.program_id(0) == 1)
    def _():
        o_ref[:, :, wide:] = o


def attend_grads(heads, idq, idk, q, do, kv, lse):
    wide = heads * HD
    allowed = idk == idq
    os, dqs, dks, dvs = [], [], [], []
    for n in range(heads):
        cols = slice(n * HD, (n + 1) * HD)
        qn, kn, gn = q[:, cols], kv[:, cols], do[:, cols]
        vn = kv[:, wide + n * HD : wide + (n + 1) * HD]
        s = jnp.where(allowed, mm_nt(kn, qn) * SCALE, NEG)
        if lse is None:
            e = jnp.exp(s - jnp.max(s, axis=0, keepdims=True))
            p = e * (1.0 / jnp.sum(e, axis=0, keepdims=True))
        else:
            p = jnp.exp(s - lse[n : n + 1, :])
        pb = p.astype(BF)
        if lse is None:
            os.append(mm(vn.T, pb).T)
        dp = mm_nt(vn, gn)
        delta = jnp.sum(p * dp, axis=0, keepdims=True)
        ds = (p * (dp - delta)).astype(BF)
        dqs.append(mm(kn.T, ds).T * SCALE)
        dks.append(mm(ds, qn) * SCALE)
        dvs.append(mm(pb, gn))
    join = lambda xs: jnp.concatenate(xs, axis=1).astype(BF)
    return (join(os) if os else None), join(dqs), join(dks + dvs)


def put_parts(refs, x):
    rows = x.shape[0] // len(refs)
    for n, ref in enumerate(refs):
        ref[...] = x[n * rows : (n + 1) * rows].reshape(ref.shape)


def both_kernel(heads, parts, pieces, idq_ref, idk_ref, q_ref, *rest):
    do_refs, rest = rest[:pieces], rest[pieces:]
    kv_refs, (o_ref, dq_ref, *dkv_refs) = rest[:parts], rest[parts:]
    wide = heads * HD
    q = q_ref[...].reshape(-1, wide)
    do = jnp.concatenate([r[0][:, :wide] for r in do_refs], axis=0)
    kv = jnp.concatenate([r[...].reshape(-1, 2 * wide) for r in kv_refs], axis=0)
    o, dq, dkv = attend_grads(heads, idq_ref[0], idk_ref[0], q, do, kv, None)
    put_half(o_ref, o)
    dq_ref[...] = dq.reshape(dq_ref.shape)
    put_parts(dkv_refs, dkv)


def back_kernel(heads, parts, pieces, idq_ref, idk_ref, q_ref, lse_ref, w_ref, *rest):
    dh_refs, rest = rest[:pieces], rest[pieces:]
    kv_refs, (dq_ref, *dkv_refs) = rest[:parts], rest[parts:]
    wide = heads * HD
    q = q_ref[...].reshape(-1, wide)
    dh = jnp.concatenate([r[0] for r in dh_refs], axis=0)
    do = mm_nt(dh, w_ref[...]).astype(BF)
    kv = jnp.concatenate([r[...].reshape(-1, 2 * wide) for r in kv_refs], axis=0)
    _, dq, dkv = attend_grads(heads, idq_ref[0], idk_ref[0], q, do, kv, lse_ref[0])
    dq_ref[...] = dq.reshape(dq_ref.shape)
    put_parts(dkv_refs, dkv)


def half_spec(a):
    return pl.BlockSpec((a.shape[0], 1) + a.shape[2:], lambda h: (0, h, 0, 0))


def side_by_side(q):
    return jax.ShapeDtypeStruct((q.shape[0], q.shape[2], 2 * q.shape[3]), q.dtype)


def all_spec(q):
    return pl.BlockSpec(side_by_side(q).shape, lambda h: (0, 0, 0))


def id_spec(a):
    return pl.BlockSpec((1,) + a.shape[1:], lambda h: (h, 0, 0))


def sds(a, dtype=None):
    return jax.ShapeDtypeStruct(a.shape, dtype or a.dtype)


def attention(name, kernel, ins, specs, outs, out_specs, flops, trans):
    nbytes = sum(a.size * a.dtype.itemsize for a in ins)
    return pl.pallas_call(
        kernel,
        grid=(2,),
        in_specs=specs,
        out_specs=out_specs,
        out_shape=outs,
        name=name,
        compiler_params=pltpu.CompilerParams(vmem_limit_bytes=48 * 1024 * 1024),
        cost_estimate=pl.CostEstimate(
            flops=flops, bytes_accessed=2 * nbytes, transcendentals=trans
        ),
    )(*ins)


def attend(heads, idq, idk, q, kvs):
    kernel = lambda *refs: attend_kernel(heads, len(kvs), *refs)
    ins = [idq, idk, q, *kvs]
    specs = [id_spec(idq), id_spec(idk)] + [half_spec(a) for a in ins[2:]]
    lse = jax.ShapeDtypeStruct((2, 8, idq.shape[2]), F32)
    pairs = 2 * heads * idq.shape[2] * idk.shape[1]
    return attention(
        "attend", kernel, ins, specs, [side_by_side(q), lse], [all_spec(q), id_spec(lse)],
        4 * pairs * HD, pairs,
    )


def attend_back(heads, idq, idk, q, lse, w_out, dhs, kvs):
    kernel = lambda *refs: back_kernel(heads, len(kvs), len(dhs), *refs)
    dhs = [x.reshape(2, -1, D) for x in dhs]
    ins = [idq, idk, q, lse, w_out, *dhs, *kvs]
    specs = [id_spec(idq), id_spec(idk), half_spec(q), id_spec(lse)]
    specs += [pl.BlockSpec((heads * HD, D), lambda h: (0, 0))]
    specs += [id_spec(x) for x in dhs] + [half_spec(a) for a in kvs]
    outs = [sds(q)] + [sds(a) for a in kvs]
    pairs = 2 * heads * idq.shape[2] * idk.shape[1]
    res = attention(
        "attend_back", kernel, ins, specs, outs, [half_spec(a) for a in outs],
        10 * pairs * HD, pairs,
    )
    return res[0], res[1:]


def attend_both(heads, idq, idk, q, dos, kvs):
    kernel = lambda *refs: both_kernel(heads, len(kvs), len(dos), *refs)
    dos = [x.reshape(2, -1, x.shape[-1]) for x in dos]
    ins = [idq, idk, q, *dos, *kvs]
    specs = [id_spec(idq), id_spec(idk), half_spec(q)]
    specs += [id_spec(x) for x in dos] + [half_spec(a) for a in kvs]
    outs = [side_by_side(q), sds(q)] + [sds(a) for a in kvs]
    pairs = 2 * heads * idq.shape[2] * idk.shape[1]
    res = attention(
        "attend_both", kernel, ins, specs, outs, [all_spec(q)] + [half_spec(a) for a in outs[1:]],
        12 * pairs * HD, pairs,
    )
    return res[0], res[1], res[2:]


def after(x, *others):
    return lax.optimization_barrier((x,) + others)[0]


def vmem_call(name, kernel, ins, outs, scratch=(), flops=0):
    nbytes = sum(a.size * a.dtype.itemsize for a in list(ins) + list(outs))
    spec = pl.BlockSpec(memory_space=pltpu.VMEM)
    return pl.pallas_call(
        kernel,
        in_specs=[spec] * len(ins),
        out_specs=[spec] * len(outs),
        out_shape=list(outs),
        scratch_shapes=list(scratch),
        name=name,
        compiler_params=pltpu.CompilerParams(vmem_limit_bytes=56 * 1024 * 1024),
        cost_estimate=pl.CostEstimate(flops=flops, bytes_accessed=nbytes, transcendentals=0),
    )(*ins)


def shape(dims, dtype):
    return jax.ShapeDtypeStruct(tuple(dims), dtype)


def aligned(x, n=8):
    return pl.multiple_of(x, n)


def solution(mesh):
    dp, seq = mesh.shape["dp"], mesh.shape["seq"]
    G = math.gcd(HEADS, seq)
    while G & (G - 1) or (seq // G) & (seq // G - 1):
        G //= 2
    J = seq // G
    heads = HEADS // G
    wide = heads * HD
    nf, nm = dp // 2, dp // 4
    mesh3 = Mesh(mesh.devices.reshape(dp, G, J), ("dp", "g", "j"))
    everyone = ("dp", "g", "j")

    view_of = [0 if d < nf else (1 if d < nf + nm else 2) for d in range(dp)]
    owner = [
        [r // 2 for r in range(dp)],
        [nf + r // 4 for r in range(dp)],
        [nf + nm + r // 4 for r in range(dp)],
    ]
    slot = [[r % 2 for r in range(dp)], [r % 4 for r in range(dp)], [r % 4 for r in range(dp)]]

    def xor(axis, n, size, x):
        return lax.ppermute(x, axis, [(i, i ^ n) for i in range(size)])

    def per_device(
        view_fine, view_mid, view_coarse, grad_fine, grad_mid, grad_coarse, clip_ids,
        attn_in, attn_out, mlp_w, cross_in, cross_out, norm_gains, biases, ffn_bias,
    ):
        tf, tm, tc = view_fine.shape[1], view_mid.shape[1], view_coarse.shape[1]
        U = 2 * tf
        ff = mlp_w.shape[1]
        cells = clip_ids.shape[1]
        d, g, j = lax.axis_index("dp"), lax.axis_index("g"), lax.axis_index("j")
        v = jnp.where(d < nf, 0, jnp.where(d < nf + nm, 1, 2))
        p = jnp.where(d < nf, 0, 1)

        def table(values, index=d):
            out = jnp.int32(values[-1])
            for i in range(len(values) - 1):
                out = jnp.where(index == i, jnp.int32(values[i]), out)
            return out

        def pick(tag, options, dtype=None):
            out = jnp.zeros_like(options[0])
            for k, option in enumerate(options):
                out = jnp.where(tag == k, option, out)
            return out

        def rows_at(x, start, size):
            return lax.dynamic_slice_in_dim(x, start, size, axis=0)

        sizes = (tf, tm, tc)
        moves = [
            (r, owner[w][r], (w, r))
            for w in (0, 2, 1)
            for r in range(dp)
            if r != owner[w][r]
        ]
        view_rounds = rounds_of(moves)
        back_rounds = rounds_of([m for m in moves if m[2][0] == 0]) + rounds_of(
            [m for m in moves if m[2][0] != 0]
        )

        def grow(x, rows):
            n = x.shape[-2]
            if n == rows:
                return x
            pad = jnp.zeros(x.shape[:-2] + (rows - n, x.shape[-1]), x.dtype)
            return jnp.concatenate([x, pad], axis=-2)

        def to_views(fine, mid, coarse):
            mid_p, coarse_p = grow(mid, tf), grow(coarse, tf)
            got = []
            for group in view_rounds:
                n = max(sizes[w] for _, _, (w, _) in group)
                kind = [3] * dp
                for src, _, (w, _) in group:
                    kind[src] = w
                load = pick(table(kind), [t[:, :n] for t in (fine, mid_p, coarse_p)])
                got.append(grow(lax.ppermute(load, "dp", [(s, t) for s, t, _ in group]), tf))
            local = pick(v, [fine, mid_p, coarse_p])
            rows = []
            for k in range(4):
                tag = [len(got) + 1] * dp
                for i, group in enumerate(view_rounds):
                    for _, dst, (w, r) in group:
                        if slot[w][r] == k:
                            tag[dst] = i + 1
                for r in range(dp):
                    if owner[view_of[r]][r] == r and slot[view_of[r]][r] == k:
                        tag[r] = 0
                rows.append(pick(table(tag), [local] + got))
            join = lambda xs: jnp.concatenate(xs, axis=1)
            pad = jnp.zeros((fine.shape[0], tf - 2 * tc, fine.shape[2]), fine.dtype)
            as_coarse = [rows[0][:, :tc], rows[1][:, :tc], pad, rows[2][:, :tc], rows[3][:, :tc], pad]
            return pick(
                v, [join(rows[:2]), join([x[:, :tm] for x in rows]), join(as_coarse)]
            )

        def route(name, views, moves, local, rows, zero):
            rounds = rounds_of(moves)
            heights = [max(m[2][2] for m in group) for group in rounds]

            def load(*refs):
                kd = lax.axis_index("dp")
                for group, out in zip(rounds, refs[len(views) :]):
                    for src, _, (w, first, size, _) in group:

                        @pl.when(kd == src)
                        def _(w=w, first=first, size=size, out=out):
                            out[:size, :] = refs[w][first : first + size, :]

            loads = vmem_call(name + "_load", load, views, [shape((n, D), BF) for n in heights])
            got = [
                lax.ppermute(x, "dp", [(a, b) for a, b, _ in group])
                for x, group in zip(loads, rounds)
            ]

            def unload(*refs):
                got_refs, out = refs[len(views) : -1], refs[-1]
                kd = lax.axis_index("dp")
                for here in range(dp):

                    @pl.when(kd == here)
                    def _(here=here):
                        if here in zero:
                            out[...] = jnp.zeros_like(out)
                        for src, _, (w, first, size, at) in local:
                            if src == here:
                                out[at : at + size, :] = refs[w][first : first + size, :]
                        for ref, group in zip(got_refs, rounds):
                            for _, dst, (_, _, size, at) in group:
                                if dst == here:
                                    out[at : at + size, :] = ref[:size, :]

            (out,) = vmem_call(name + "_unload", unload, views + got, [shape((rows, D), BF)])
            return out

        def grads_to_views(fine, mid, coarse):
            all_moves = [
                (r, owner[w][r], (w, 0, sizes[w], place(w, slot[w][r])))
                for w in (0, 2, 1)
                for r in range(dp)
            ]
            zero = [x for x in range(dp) if view_of[x] == 2]
            return route(
                "grads", [fine[0], mid[0], coarse[0]],
                [m for m in all_moves if m[0] != m[1]], [m for m in all_moves if m[0] == m[1]],
                U, zero,
            )

        def grads_to_queries(mid, coarse):
            all_moves = [(r, r // 2, (0, 0, tm, r % 2 * tm)) for r in range(dp)]
            all_moves += [(r, nf + r // 4, (1, 0, tc, r % 4 * tc)) for r in range(dp)]
            zero = [x for x in range(dp) if view_of[x] == 2]
            return route(
                "query_grads", [mid[0], coarse[0]],
                [m for m in all_moves if m[0] != m[1]], [m for m in all_moves if m[0] == m[1]],
                2 * tm, zero,
            )

        def place(w, k):
            return (tf * k, tm * k, tf * (k // 2) + tc * (k % 2))[w]

        def from_views(x):
            padded = grow(x, U + tf)
            rows_of = lambda start, n: lax.dynamic_slice_in_dim(padded, start, n, axis=1)
            got = []
            for group in back_rounds:
                n = max(sizes[w] for _, _, (w, _) in group)
                start = [0] * dp
                for _, src, (w, r) in group:
                    start[src] = place(w, slot[w][r])
                load = rows_of(table(start), n)
                got.append(grow(lax.ppermute(load, "dp", [(t, s) for s, t, _ in group]), tf))
            local_start = [0] * dp
            for r in range(dp):
                w = view_of[r]
                if owner[w][r] == r:
                    local_start[r] = place(w, slot[w][r])
            local = rows_of(table(local_start), tf)
            outs = []
            for w in range(VIEWS):
                tag = [0] * dp
                for i, group in enumerate(back_rounds):
                    for _, dst, (w2, r) in group:
                        if w2 == w:
                            tag[r] = i + 1
                outs.append(pick(table(tag), [local] + got)[:, : sizes[w]])
            return outs

        q_moves = [(nf + (2 * t) // 4, t, t % 2) for t in range(nf)]
        q_moves += [(nf + nm + i, nf + i, 0) for i in range(nm)]
        q_rounds = rounds_of(q_moves)

        def to_queries(x):
            dense = jnp.concatenate([x[: 2 * tc], x[tf : tf + 2 * tc]], axis=0)
            got = []
            for group in q_rounds:
                start = [0] * dp
                for src, _, h in group:
                    start[src] = h * tf
                load = jnp.where(v == 2, dense, rows_at(x, table(start), tf))
                got.append(lax.ppermute(load, "dp", [(s, t) for s, t, _ in group]))
            tag = [len(got)] * dp
            for i, group in enumerate(q_rounds):
                for _, dst, _ in group:
                    tag[dst] = i
            return pick(table(tag), got)

        def from_queries(x):
            got = [lax.ppermute(x, "dp", [(t, s) for s, t, _ in group]) for group in q_rounds]
            parts = []
            for half in range(2):
                tag = [len(got)] * dp
                for i, group in enumerate(q_rounds):
                    for src, _, h in group:
                        if h == half:
                            tag[src] = i
                parts.append(pick(table(tag), got))
            pad = jnp.zeros((tf - 2 * tc, x.shape[1]), x.dtype)
            coarse = jnp.concatenate([parts[0][: 2 * tc], pad, parts[0][2 * tc :], pad], axis=0)
            return jnp.where(v == 2, coarse, jnp.concatenate(parts, axis=0))

        def spread_g(x):
            return [x] + [xor("g", m, G, x) for m in range(1, G)]

        def sum_g(pieces):
            out = pieces[0].astype(F32)
            got = [xor("g", m, G, pieces[m].astype(BF)) for m in range(1, G)]
            for x in got:
                out = out + x.astype(F32)
            return out

        def spread_j(x):
            return [x] + [xor("j", n, J, x) for n in range(1, J)]

        n_dev = dp * seq
        gw, fw = norm_gains.shape[1], ffn_bias.shape[1]
        fq = fw // gw
        hid = ff // G
        id_rows = cells // gw
        n_vec = 38 + 3 * fq + id_rows
        n_par = 38 + 3 * fq
        per = 128 // gw
        deep = (-(-n_vec // per) + 7) // 8 * 8
        blocks = -(-n_vec // deep)

        def pack_vec(g_ref, b_ref, f_ref, i_ref, out_ref, rows):
            rows[...] = jnp.zeros_like(rows)
            rows[:10, :] = g_ref[...].astype(F32)
            rows[10:38, :] = b_ref[...].astype(F32)
            for r in range(3):
                for t in range(fq):
                    at = 38 + r * fq + t
                    rows[at : at + 1, :] = f_ref[r : r + 1, t * gw : (t + 1) * gw].astype(F32)
            for t in range(id_rows):
                at = n_par + t
                rows[at : at + 1, :] = i_ref[0:1, t * gw : (t + 1) * gw].astype(F32)
            out = [rows[b * deep : (b + 1) * deep, :] for b in range(blocks)]
            out.append(jnp.zeros((deep, 128 - blocks * gw), F32))
            out = jnp.concatenate(out, axis=1).astype(BF)
            for i in range(n_dev):
                out_ref[i] = out

        def role():
            kd, kg, kj = lax.axis_index("dp"), lax.axis_index("g"), lax.axis_index("j")
            kv = jnp.where(kd < nf, 0, jnp.where(kd < nf + nm, 1, 2))
            return kd, kg, kj, kv, jnp.where(kd < nf, 0, 1)

        def setup(vec_ref, prm_ref, idq_ref, idk_ref, cidq_ref, full, ffn):
            kd, kg, kj, kv, kp = role()
            for i in range(n_dev):
                x = vec_ref[i].astype(F32)
                for b in range(blocks):
                    full[b * deep : (b + 1) * deep, i * gw : (i + 1) * gw] = x[
                        :, b * gw : (b + 1) * gw
                    ]
            for i in range(n_dev):
                for r in range(3):
                    for t in range(fq):
                        at = i * fw + t * gw
                        ffn[r : r + 1, at : at + gw] = full[
                            38 + r * fq + t : 39 + r * fq + t, i * gw : (i + 1) * gw
                        ]

            def row(r):
                return full[r : r + 1, :]

            def by_view(rows):
                return jnp.where(kv == 0, rows[0], jnp.where(kv == 1, rows[1], rows[2]))

            def part(x, width):
                out = x[:, :width]
                for i in range(1, G):
                    out = jnp.where(kg == i, x[:, i * width : (i + 1) * width], out)
                return out

            prm_ref[...] = jnp.zeros_like(prm_ref)
            for i in range(2):
                prm_ref[i : i + 1, :] = by_view([row(2 * k + i) for k in range(3)])
            for i in range(6):
                x = by_view([row(10 + 6 * k + i) for k in range(3)])
                if i in (1, 2):
                    prm_ref[2 + i : 3 + i, :wide] = part(x, wide)
                else:
                    prm_ref[2 + i : 3 + i, :] = x
            prm_ref[8:9, :hid] = part(by_view([ffn[k : k + 1, :] for k in range(3)]), hid)
            prm_ref[9:10, :] = by_view([row(6), row(6), row(8)])
            prm_ref[10:11, :] = by_view([row(7), row(9), row(9)])
            prm_ref[11:12, :] = by_view([row(28), row(28), row(33)])
            prm_ref[12:13, :] = by_view([row(29), row(34), row(34)])
            for i in range(3):
                x = jnp.where(kp == 0, row(30 + i), row(35 + i))
                if i < 2:
                    prm_ref[13 + i : 14 + i, :wide] = part(x, wide)
                else:
                    prm_ref[13 + i : 14 + i, :] = x

            starts = []
            for r in range(dp):
                x = full[n_par:n_vec, r * seq * gw : (r * seq + 1) * gw]
                starts.append(
                    [jnp.sum((x < c).astype(F32), keepdims=True) for c in (0.5, 1.5, 2.5)]
                )

            def start_at(index):
                out = starts[0]
                for r in range(1, dp):
                    out = [jnp.where(index == r, b, a) for a, b in zip(out, starts[r])]
                return out

            def ids(first, second, unit, per_cell, cap, u, k, n):
                s = (kg ^ k) * J + (kj ^ n)
                late = u >= unit
                pos = (s * unit + u - jnp.where(late, unit, 0)).astype(F32)
                out = jnp.zeros(u.shape, F32)
                for a, b in zip(first, second):
                    edge = jnp.where(late, b, a) * per_cell.astype(F32)
                    out = out + (pos >= edge).astype(F32)
                out = out + jnp.where(late, 4.0, 0.0)
                return jnp.where(u >= cap, -1.0, out)

            unit = jnp.where(kv == 0, tf, jnp.where(kv == 1, tm, tc))
            per_cell = jnp.where(kv == 0, 4, jnp.where(kv == 1, 2, 1))
            base = jnp.where(kv == 0, 2 * kd, 4 * ((kd - nf) % nm))
            q_unit, q_cell = jnp.where(kp == 0, tm, tc), jnp.where(kp == 0, 2, 1)
            for h in range(2):
                first = start_at(base + jnp.where(kv == 0, h, 2 * h))
                second = start_at(base + 2 * h + 1)
                for k in range(G):
                    lane = lax.broadcasted_iota(jnp.int32, (1, tf), 1)
                    idq_ref[h, :, k * tf : (k + 1) * tf] = ids(
                        first, second, unit, per_cell, 2 * unit, lane, k, 0
                    )
                    lane = lax.broadcasted_iota(jnp.int32, (1, tm), 1)
                    cidq_ref[h, :, k * tm : (k + 1) * tm] = ids(
                        first, second, q_unit, q_cell, tm, lane, k, 0
                    )
                    for n in range(J):
                        deep_u = lax.broadcasted_iota(jnp.int32, (tf, 1), 0)
                        at = (n * G + k) * tf
                        idk_ref[h, at : at + tf, :] = ids(
                            first, second, unit, per_cell, 2 * unit, deep_u, k, n
                        )

        def cols(x, width):
            return lax.dynamic_slice_in_dim(x, g * width, width, axis=-1)

        near = dp == 4

        def both_sides(x):
            return xor("dp", 1, dp, x), lax.ppermute(x, "dp", [(1, 2)])

        def chunks(x):
            if near:
                twin, below = both_sides(x)
                odd = d % 2 == 1
                lo = jnp.where(d == 2, below, jnp.where(odd, twin, x))
                enc = jnp.stack([lo, jnp.where(d == 0, twin, x)])
                cross = jnp.stack([jnp.where(odd, twin, x), jnp.where(odd, x, twin)])
                return enc, cross
            everything = lax.all_gather(x, "dp", axis=0)
            return everything, everything

        enc_lo = jnp.maximum(d - 1, 0) if near else jnp.int32(0)
        cross_lo = 2 * p if near else jnp.int32(0)

        def start_of(part, n_parts, low, total):
            return part * (total // n_parts) - low * (total // dp)

        def join_j(x):
            xs = spread_j(x)
            parts = []
            for a in range(J):
                out = xs[0]
                for n in range(1, J):
                    out = jnp.where((j ^ n) == a, xs[n], out)
                parts.append(out)
            full = jnp.stack(parts, axis=2)
            return full.reshape(-1, x.shape[-1])

        r_in, r_cross = attn_in.shape[0], cross_in.shape[0]
        r_mlp, r_out, r_co = mlp_w.shape[0], attn_out.shape[0], cross_out.shape[0]

        def half_of(r):
            return (r + 15) // 16 * 8

        h_in, h_cross = half_of(r_in), half_of(r_cross)
        lanes = 2 * wide

        def pack(dst, i, at, r, x):
            half = half_of(r)
            dst[i, at : at + half, :wide] = x[:half]
            dst[i, at : at + r - half, wide:] = x[half:]

        def split_qkv(in_ref, cross_ref, qkv_ref):
            for i in range(G):
                at = slice(i * wide, (i + 1) * wide)
                pack(qkv_ref, i, 0, r_in, in_ref[:, at])
                pack(qkv_ref, i, h_in, r_cross, cross_ref[:, at])

        def split_mlp(mlp_ref, mlp_out):
            for i in range(G):
                mlp_out[i] = mlp_ref[:, i * hid : (i + 1) * hid]

        outs = jnp.concatenate([attn_out, cross_out], axis=0)
        (vec,) = vmem_call(
            "pack_vec", pack_vec, [norm_gains, biases, ffn_bias, clip_ids],
            [shape((n_dev, deep, 128), BF)], [pltpu.VMEM((blocks * deep, gw), F32)],
        )
        if near:
            (qkv,) = vmem_call(
                "split_qkv", split_qkv, [attn_in, cross_in],
                [shape((G, h_in + h_cross, lanes), BF)],
            )
            vec = after(vec, qkv)
        vecs = lax.all_to_all(vec, everyone, 0, 0, tiled=True)
        if near:
            qkv = lax.all_to_all(after(qkv, vecs), "g", 0, 0, tiled=True)
            x_own = to_views(after(view_fine, qkv), view_mid, view_coarse)[0]
            (mlp,) = vmem_call(
                "split_mlp", split_mlp, [after(mlp_w, x_own)], [shape((G, r_mlp, hid), BF)]
            )
            mlp = lax.all_to_all(mlp, "g", 0, 0, tiled=True)
        else:
            x_own = to_views(view_fine, view_mid, view_coarse)[0]
            qkv = lax.all_to_all(
                jnp.concatenate([attn_in, cross_in], axis=0), "g", 1, 0, tiled=True
            ).reshape(G, r_in + r_cross, wide)
            mlp = lax.all_to_all(mlp_w, "g", 1, 0, tiled=True).reshape(G, r_mlp, hid)
        set_outs = [
            shape((16, D), F32),
            shape((2, 1, G * tf), F32), shape((2, seq * tf, 1), F32), shape((2, 1, G * tm), F32),
        ]
        prm, idq, idk, cross_idq = pl.pallas_call(
            setup,
            grid=(1,),
            in_specs=[pl.BlockSpec((n_dev, deep, 128), lambda i: (0, 0, 0))],
            out_specs=[
                pl.BlockSpec(t.shape, lambda i, n=len(t.shape): (0,) * n) for t in set_outs
            ],
            out_shape=set_outs,
            scratch_shapes=[pltpu.VMEM((blocks * deep, D), F32), pltpu.VMEM((3, ff), F32)],
            name="setup",
            compiler_params=pltpu.CompilerParams(vmem_limit_bytes=32 * 1024 * 1024),
        )(vecs)

        def offset(kind, total, kd, kv, kp):
            low = jnp.maximum(kd - 1, 0)
            return kv * (total // 3) - low * (total // 4) if kind == "enc" else kp * 0

        def assemble(name, x, parts, width, sides, wait=None):
            twin, below = sides
            if wait is not None:
                twin, below = after(twin, wait), after(below, wait)
            srcs = [*spread_j(x), *spread_j(twin), *spread_j(below)]
            packed = width != x.shape[2]
            outs, scratch = [], []
            for kind, _, r in parts:
                outs.append(shape((n_dev * r // (3 if kind == "enc" else 2), width), BF))
                scratch.append(pltpu.VMEM((n_dev * r // 2, width), F32))

            def kernel(*refs):
                kd, kg, kj, kv, kp = role()
                own, twin_r, below_r = refs[:J], refs[J : 2 * J], refs[2 * J : 3 * J]
                out_refs = refs[3 * J : 3 * J + len(parts)]
                frames = refs[3 * J + len(parts) :]

                for (kind, first, r), frame in zip(parts, frames):

                    def put(t, group, first=first, r=r, frame=frame):
                        for n, ref in enumerate(group):
                            for i in range(G):
                                at = ((t * G + i) * J + (kj ^ n)) * r
                                size = half_of(r) if packed else r
                                frame[pl.ds(aligned(at), size), :] = ref[
                                    i, first : first + size, :width
                                ].astype(F32)
                                if packed:
                                    frame[pl.ds(aligned(at + size), r - size), :] = ref[
                                        i, first : first + r - size, width:
                                    ].astype(F32)

                    own_first = kd == 0 if kind == "enc" else kd % 2 == 0
                    from_below = kd == 2 if kind == "enc" else kd < 0

                    @pl.when(own_first)
                    def _(put=put):
                        put(0, own)
                        put(1, twin_r)

                    @pl.when(from_below)
                    def _(put=put):
                        put(0, below_r)
                        put(1, own)

                    @pl.when(jnp.logical_not(jnp.logical_or(own_first, from_below)))
                    def _(put=put):
                        put(0, twin_r)
                        put(1, own)

                for (kind, _, r), frame, out in zip(parts, frames, out_refs):
                    at = aligned(offset(kind, n_dev * r, kd, kv, kp))
                    out[...] = frame[pl.ds(at, out.shape[0]), :].astype(BF)

            return vmem_call(name, kernel, srcs, outs, scratch)

        if near:
            w_in, c_in = assemble(
                "assemble_in", qkv, [("enc", 0, r_in), ("cross", h_in, r_cross)], wide,
                both_sides(qkv),
            )
            mlp_sides = both_sides(mlp)
        else:
            enc_c, cross_c = chunks(qkv)
            w_in = rows_at(
                join_j(enc_c[:, :, :r_in]), start_of(v, 3, enc_lo, n_dev * r_in), 3 * D
            )
            c_in = rows_at(
                join_j(cross_c[:, :, r_in:]), start_of(p, 2, cross_lo, n_dev * r_cross), 3 * D
            )

        def mlp_weights(wait):
            if near:
                return assemble(
                    "assemble_mlp", mlp, [("enc", 0, r_mlp)], hid, mlp_sides, wait
                )[0]
            enc_c, _ = chunks(mlp)
            return rows_at(join_j(enc_c), start_of(v, 3, enc_lo, n_dev * r_mlp), 2 * D)

        enc_c, cross_c = chunks(outs)
        planes = enc_c.shape[0]
        outs = jnp.concatenate([enc_c[:, :r_out], cross_c[:, r_out:]], axis=1)
        outs = lax.all_gather(outs.reshape(-1, D), ("g", "j"), axis=0)
        outs = outs.reshape(seq, planes, r_out + r_co, D)

        def arrange(x_ref, w_ref, c_ref, frame, cross_frame):
            kd, kg, kj, kv, kp = role()
            for t in range(planes):
                for i in range(seq):
                    at = (t * seq + i) * r_out
                    frame[at : at + r_out, :] = x_ref[i, t, :r_out].astype(F32)
                    at = (t * seq + i) * r_co
                    cross_frame[at : at + r_co, :] = x_ref[i, t, r_out:].astype(F32)
            low = jnp.maximum(kd - 1, 0) if near else 0
            first = kv * (n_dev * r_out // 3) - low * (n_dev * r_out // dp)
            cross_first = 0 if near else kp * (n_dev * r_co // 2)
            for m in range(G):
                to = slice(m * wide, (m + 1) * wide)
                at = aligned(first + (kg ^ m) * wide)
                w_ref[to, :] = frame[pl.ds(at, wide), :].astype(BF)
                at = aligned(cross_first + (kg ^ m) * wide)
                c_ref[to, :] = cross_frame[pl.ds(at, wide), :].astype(BF)

        def out_weights(wait):
            return vmem_call(
                "arrange_out", arrange, [after(outs, wait)],
                [shape((D, D), BF), shape((D, D), BF)],
                [
                    pltpu.VMEM((planes * seq * r_out, D), F32),
                    pltpu.VMEM((planes * seq * r_co, D), F32),
                ],
            )

        def home(name, arrays, parts):
            ins = list(arrays)
            places, row, lane = [], 0, 0
            for _, width, r, _ in parts:
                if width == D:
                    places.append((row, 0, r))
                    row += r
                else:
                    unit = n_unit(parts, width)
                    places.append((row, lane, unit))
                    lane += r // unit * width
                    if lane == D:
                        row, lane = row + unit, 0
            outs = [shape((2, G, row, D), BF) for _ in range(J)]
            scratch = [pltpu.VMEM((n_dev * r // 2, width), F32) for _, width, r, _ in parts]

            def kernel(*refs):
                kd, kg, kj, kv, kp = role()
                in_refs = refs[: len(ins)]
                out_refs = refs[len(ins) : len(ins) + J]
                frames = refs[len(ins) + J :]

                def value(key):
                    if isinstance(key, list):
                        return jnp.concatenate([value(k) for k in key], axis=0)
                    index, at, size = key if isinstance(key, tuple) else (key, 0, None)
                    x = in_refs[index][...]
                    x = x.reshape(-1, x.shape[-1])
                    return x if size is None else x[:, at : at + size]

                for (kind, width, r, mats), frame, place in zip(parts, frames, places):
                    if kind == "enc":
                        frame[...] = jnp.zeros_like(frame)
                    base = offset(kind, n_dev * r, kd, kv, kp)
                    for i, (left, right, grouped) in enumerate(mats):
                        b = value(right)
                        if b.shape[1] > width:
                            x = b[:, :wide]
                            for k in range(1, G):
                                x = jnp.where(kg == k, b[:, k * wide : (k + 1) * wide], x)
                            b = x
                        res = mm_tn(value(left), b)
                        if grouped:
                            for m in range(G):
                                at = aligned(base + i * D + (kg ^ m) * wide)
                                frame[pl.ds(at, wide), :] = res[m * wide : (m + 1) * wide]
                        else:
                            frame[pl.ds(aligned(base + i * D), D), :] = res
                    own = jnp.where(kd == 0, 0, 1) if kind == "enc" else kd % 2
                    first, lane0, unit = place
                    for n in range(J):
                        for side in range(2):
                            t = own if side == 0 else 1 - own
                            for k in range(G):
                                at = ((t * G + k) * J + (kj ^ n)) * r
                                for i in range(r // unit):
                                    to = lane0 + i * width
                                    out_refs[n][
                                        side, k, first : first + unit, to : to + width
                                    ] = frame[pl.ds(aligned(at + i * unit), unit), :].astype(BF)

            return vmem_call(name, kernel, ins, outs, scratch)

        def n_unit(parts, width):
            return min(r for _, w, r, _ in parts if w == width)

        def sum_j(blocks, ready, *wait):
            got = [xor("j", n, J, after(blocks[n], ready)) for n in range(1, J)]
            acc = after(blocks[0], *wait).astype(F32)
            for x in got:
                acc = acc + x.astype(F32)
            return acc[0].astype(BF), acc[1].astype(BF)

        def move_planes(other):
            return xor("dp", 1, dp, other), lax.ppermute(other, "dp", [(2, 1)])

        def sum_planes(own, moved, enc_rows):
            got, below = moved
            enc = lax.broadcasted_iota(jnp.int32, own.shape, 1) < enc_rows
            got = jnp.where(enc & (d == 3), 0.0, got.astype(F32))
            got = got + jnp.where(enc, below.astype(F32), 0.0)
            return (own.astype(F32) + got).astype(BF)

        Uq = 2 * tm
        dot = 2 * D * D

        def piece(rows, dtype=BF, width=D):
            return shape((rows, width), dtype)

        def stack(rows, width, dtype=BF):
            return shape((G, rows, width), dtype)

        def loop(body):
            lax.fori_loop(0, G, lambda k, c: (body(k), c)[1], 0)

        def stage(refs, dst):
            for i, ref in enumerate(refs):
                dst[i] = ref[...]

        def deliver(src, out_ref):
            for m in range(G):
                out_ref[lax.axis_index("g") ^ m] = src[m].astype(BF)

        def deliver_each(src, out_refs):
            for m, ref in enumerate(out_refs):
                ref[...] = src[m].astype(BF)

        def swap_g(pieces):
            return [pieces[0]] + [xor("g", m, G, pieces[m]) for m in range(1, G)]

        def collect_g(x):
            return lax.all_to_all(x, "g", 0, 0, tiled=True)

        def total_of(ref):
            out = ref[0].astype(F32)
            for m in range(1, G):
                out = out + ref[m].astype(F32)
            return out

        xs = spread_g(x_own)
        gc_own = grads_to_queries(after(grad_mid, x_own), grad_coarse)

        def k_qkv(*refs):
            x_refs, (w, prm_r, x_ref, a_ref, q_ref, kv_ref) = refs[:G], refs[G:]
            stage(x_refs, x_ref)

            def body(k):
                z, _ = unit_rows(x_ref[k].astype(F32))
                a = (z * prm_r[0:1] + prm_r[2:3]).astype(BF)
                a_ref[k] = a
                q_ref[k] = (mm(a, w[:D]) + prm_r[3:4, :wide]).astype(BF)
                kv_ref[k, :, :wide] = mm(a, w[D : 2 * D]).astype(BF)
                kv_ref[k, :, wide:] = (mm(a, w[2 * D :]) + prm_r[4:5, :wide]).astype(BF)

            loop(body)

        x_all, a, q, kv = vmem_call(
            "qkv", k_qkv, [*xs, after(w_in, gc_own), prm],
            [stack(U, D), stack(U, D), stack(U, wide), stack(U, 2 * wide)],
            flops=dot * U * G * 3 // 4 // D,
        )

        def halves(t):
            return t.reshape(G, 2, -1, t.shape[-1])

        q4 = halves(q)
        kvs = [halves(t) for t in spread_j(kv)]
        o, lse = attend(heads, idq, idk, q4, kvs)
        os = spread_g(o)

        def unfold(r, k):
            x = r[k]
            return jnp.concatenate([x[:, :wide], x[:, wide:]], axis=0)

        w_mlp = mlp_weights(kv)
        w_out, c_out = out_weights(o)

        def gelu_of(u):
            cdf = 0.5 * (1.0 + lax.erf(u * (0.5**0.5)))
            return u * cdf, cdf + u * jnp.exp(-0.5 * u * u) * (1.0 / math.sqrt(2.0 * math.pi))

        def k_mlp(*refs):
            o_refs, (x_ref, wo, wm, prm_r, *rest) = refs[:G], refs[G:]
            oa_ref, c_ref, slope_ref, e_ref, h_ref, y_ref, parts = rest

            def body(k):
                o_k = jnp.concatenate([unfold(r, k ^ m) for m, r in enumerate(o_refs)], axis=1)
                oa_ref[k] = o_k
                h = x_ref[k].astype(F32) + (mm(o_k, wo[...]) + prm_r[5:6])

                @pl.when(k == 0)
                def _():
                    h_ref[...] = h

                z, _ = unit_rows(h)
                c = (z * prm_r[1:2] + prm_r[6:7]).astype(BF)
                c_ref[k] = c
                e, slope = gelu_of(mm(c, wm[:D]) + prm_r[8:9, :hid])
                e = e.astype(BF)
                e_ref[k] = e
                slope_ref[k] = slope.astype(BF)
                parts[k] = mm_nt(e, wm[D:])

            loop(body)
            deliver(parts, y_ref)

        o_all, c, slope, e, h_own, y_out = vmem_call(
            "mlp", k_mlp, [*os, x_all, w_out, w_mlp, prm],
            [stack(U, D), stack(U, D), stack(U, hid), stack(U, hid), piece(U, F32), stack(U, D)],
            [pltpu.VMEM((G, U, D), F32)],
            flops=3 * dot * U * G // D,
        )
        y_in = collect_g(y_out)

        def k_given(g_ref, w, *out_refs):
            grad = g_ref[...]
            kg = lax.axis_index("g")
            for m, ref in enumerate(out_refs):
                ref[:, :wide] = mm_nt(grad, w[m * wide : (m + 1) * wide]).astype(BF)
                x = grad[:, :wide]
                for k in range(1, G):
                    x = jnp.where(kg ^ m == k, grad[:, k * wide : (k + 1) * wide], x)
                ref[:, wide:] = x

        given = vmem_call("given", k_given, [gc_own, c_out], [piece(Uq, BF, 2 * wide)] * G)
        given = [given[0]] + [xor("g", m, G, given[m]) for m in range(1, G)]
        h_own = after(h_own, *given)

        def k_norm(h_ref, got, prm_r, y_ref, zy_ref, rs_ref, kn_ref, qn_ref):
            y = total_of(got) + h_ref[...] + prm_r[7:8]
            y_ref[...] = y
            z, rs = unit_rows(y)
            zy_ref[...] = z
            rs_ref[...] = rs
            kn_ref[...] = (z * prm_r[10:11] + prm_r[12:13]).astype(BF)
            qn_ref[...] = (z * prm_r[9:10] + prm_r[11:12]).astype(BF)

        y, zy, rs_y, kn_v, qn_v = vmem_call(
            "norm_y", k_norm, [h_own, y_in, prm],
            [piece(U, F32), piece(U, F32), piece(U, F32, 1), piece(U), piece(U)],
        )
        qns, kns = None, spread_g(kn_v)
        qns = spread_g(to_queries(qn_v))

        grad_own = grads_to_views(after(grad_fine, kns[1]), grad_mid, grad_coarse)

        def k_cross(*refs):
            q_refs, k_refs, (w, prm_r, qn_ref, kn_ref, q_ref, kv_ref) = (
                refs[:G], refs[G : 2 * G], refs[2 * G :],
            )
            stage(q_refs, qn_ref)
            stage(k_refs, kn_ref)

            def body(k):
                q_ref[k] = (mm(qn_ref[k], w[:D]) + prm_r[13:14, :wide]).astype(BF)
                x = kn_ref[k]
                kv_ref[k, :, :wide] = mm(x, w[D : 2 * D]).astype(BF)
                kv_ref[k, :, wide:] = (mm(x, w[2 * D :]) + prm_r[14:15, :wide]).astype(BF)

            loop(body)

        qn, kn, cross_q, cross_kv = vmem_call(
            "cross", k_cross, [*qns, *kns, after(c_in, grad_own), prm],
            [stack(Uq, D), stack(U, D), stack(Uq, wide), stack(U, 2 * wide)],
            flops=dot * U * G * 5 // 8 // D,
        )
        ckvs = [halves(t) for t in spread_j(cross_kv)]
        c_att, dq_c, dkvs = attend_both(
            heads, cross_idq, idk, halves(cross_q), given, ckvs
        )
        dkv_c_in = [dkvs[0]] + [xor("j", n, J, dkvs[n]) for n in range(1, J)]
        dkv_c_in = [t.reshape(G, U, 2 * wide) for t in dkv_c_in]
        dq_c = dq_c.reshape(G, Uq, wide)

        cos = spread_g(c_att)

        def k_dqn(dq_ref, w, sum_ref, *rest):
            out_refs, parts = rest[:-1], rest[-1]
            sum_ref[...] = jnp.zeros_like(sum_ref)

            def body(k):
                x = dq_ref[k]
                parts[k] = mm_nt(x, w[:D])
                sum_ref[...] += jnp.sum(x.astype(F32), axis=0, keepdims=True)

            loop(body)
            deliver_each(parts, out_refs)

        dcq, *dqn_out = vmem_call(
            "dqn", k_dqn, [dq_c, c_in],
            [piece(1, F32, wide)] + [piece(Uq)] * G,
            [pltpu.VMEM((G, Uq, D), F32)],
            flops=dot * Uq * G // 4 // D,
        )
        dqn_in = swap_g(dqn_out)

        def k_dkn(*refs):
            in_refs, (w, dkv_ref, sum_ref, *rest) = refs[:J], refs[J:]
            out_refs, parts = rest[:-1], rest[-1]
            sum_ref[...] = jnp.zeros_like(sum_ref)

            def body(k):
                x = in_refs[0][k].astype(F32)
                for r in in_refs[1:]:
                    x = x + r[k].astype(F32)
                x = x.astype(BF)
                dkv_ref[k] = x
                sum_ref[...] += jnp.sum(x.astype(F32), axis=0, keepdims=True)
                parts[k] = mm_nt(x[:, :wide], w[D : 2 * D]) + mm_nt(x[:, wide:], w[2 * D :])

            loop(body)
            deliver_each(parts, out_refs)

        dkv_c, dckv, *dkn_out = vmem_call(
            "dkn", k_dkn, [*dkv_c_in, c_in],
            [stack(U, 2 * wide), piece(1, F32, 2 * wide)] + [piece(U)] * G,
            [pltpu.VMEM((G, U, D), F32)],
            flops=dot * U * G // 2 // D,
        )
        dkn_in = swap_g(dkn_out)
        dqn = sum(x.astype(F32) for x in [after(dqn_in[0], dkv_c, *cos)] + dqn_in[1:]).astype(BF)
        dqn_v = from_queries(dqn)

        def k_mix(*refs):
            o_refs, (w, prm_r, o_ref, mix_ref) = refs[:G], refs[G:]
            for k in range(G):
                o_ref[k] = jnp.concatenate(
                    [unfold(r, k ^ m) for m, r in enumerate(o_refs)], axis=1
                )
            mix_ref[...] = (mm(o_ref[0], w[...]) + prm_r[15:16]).astype(BF)

        cross_o, mix = vmem_call(
            "mix", k_mix, [*cos, after(c_out, *dkn_out), prm], [stack(Uq, D), piece(Uq)],
            flops=dot * Uq // D,
        )

        def k_dy(grad_ref, zy_ref, rs_ref, dq_ref, prm_r, *rest):
            dk_refs, (dy_ref, dm_ref, sum_ref) = rest[:G], rest[G:]
            _, _, _, kv, _ = role()
            z = zy_ref[...]
            grad = grad_ref[...].astype(F32)
            dqv = jnp.where(kv == 0, 0.0, dq_ref[...].astype(F32))
            dkv = sum(r[...].astype(F32) for r in dk_refs)
            dkv = jnp.where(kv == 2, 0.0, dkv)
            dy = grad + unit_back(z, rs_ref[...], dqv * prm_r[9:10] + dkv * prm_r[10:11])
            dm = dy.astype(BF)
            dy_ref[...] = dy
            dm_ref[...] = dm
            for i, x in enumerate([dqv * z, dqv, dkv * z, dkv, grad, dm.astype(F32)]):
                sum_ref[i : i + 1, :] = jnp.sum(x, axis=0, keepdims=True)

        dy, dm_own, sums_y = vmem_call(
            "dy", k_dy, [after(grad_own, mix), zy, rs_y, dqn_v, prm, *dkn_in],
            [piece(U, F32), piece(U), piece(8, F32)],
        )

        dms = spread_g(dm_own)

        def k_mlp_back(*refs):
            m_refs, (slope_ref, wm, dm_ref, du_ref, sum_ref, out_ref, parts) = refs[:G], refs[G:]
            stage(m_refs, dm_ref)
            sum_ref[...] = jnp.zeros_like(sum_ref)

            def body(k):
                du = (mm(dm_ref[k], wm[D:]) * slope_ref[k].astype(F32)).astype(BF)
                du_ref[k] = du
                sum_ref[...] += jnp.sum(du.astype(F32), axis=0, keepdims=True)
                parts[k] = mm_nt(du, wm[:D])

            loop(body)
            deliver(parts, out_ref)

        dm, du, dbf, dc_out = vmem_call(
            "mlp_back", k_mlp_back, [*dms, slope, w_mlp],
            [stack(U, D), stack(U, hid), piece(1, F32, hid), stack(U, D)],
            [pltpu.VMEM((G, U, D), F32)],
            flops=2 * dot * U * G // D,
        )
        dc_in = collect_g(dc_out)

        h_back = h_own
        if near:
            ckv = [(7, i * wide, wide) for i in range(2)]
            gcols = [(9 + m, wide, wide) for m in range(G)]
            b_mc = home(
                "home_mc", [c, du, dm, e, qn, kn, dq_c, dkv_c, cross_o, *given],
                [
                    ("enc", hid, r_mlp, [(0, 1, False), (2, 3, False)]),
                    (
                        "cross", wide, r_cross,
                        [(4, 6, False), (5, ckv[0], False), (5, ckv[1], False)],
                    ),
                    ("cross", wide, r_co, [(8, gcols, True)]),
                ],
            )
            h_back = after(h_own, *b_mc)

        def k_dh(got, h_ref, dy_ref, prm_r, dh_ref, dhb_ref, sum_ref):
            dn = total_of(got)
            z, rs = unit_rows(h_ref[...])
            dh = dy_ref[...] + unit_back(z, rs, dn * prm_r[1:2])
            dh_ref[...] = dh
            dhb = dh.astype(BF)
            dhb_ref[...] = dhb
            for i, x in enumerate([dn * z, dn, dhb.astype(F32)]):
                sum_ref[i : i + 1, :] = jnp.sum(x, axis=0, keepdims=True)

        dh, dh_own, sums_h = vmem_call(
            "dh", k_dh, [dc_in, h_back, dy, prm],
            [piece(U, F32), piece(U), piece(8, F32)],
        )
        dhs = spread_g(dh_own)
        if near:
            own_mc, other_mc = sum_j(b_mc, dc_in, dh_own)
            moved_mc = move_planes(other_mc)
            lse = after(lse, other_mc)
        dq, dkvs = attend_back(heads, idq, idk, q4, lse, w_out, dhs, kvs)
        dkv_in = [dkvs[0]] + [xor("j", n, J, dkvs[n]) for n in range(1, J)]
        dkv_in = [t.reshape(G, U, 2 * wide) for t in dkv_in]
        dq = dq.reshape(G, U, wide)
        if near:
            dq = after(dq, *moved_mc)
        def k_da(*refs):
            in_refs, (dq_ref, w, dkv_ref, sum_ref, out_ref, parts) = refs[:J], refs[J:]
            sum_ref[...] = jnp.zeros_like(sum_ref)

            def body(k):
                x = in_refs[0][k].astype(F32)
                for r in in_refs[1:]:
                    x = x + r[k].astype(F32)
                x = x.astype(BF)
                dkv_ref[k] = x
                dqk = dq_ref[k]
                sum_ref[0:1, :wide] += jnp.sum(dqk.astype(F32), axis=0, keepdims=True)
                sum_ref[1:2, :wide] += jnp.sum(
                    x[:, wide:].astype(F32), axis=0, keepdims=True
                )
                parts[k] = (
                    mm_nt(dqk, w[:D])
                    + mm_nt(x[:, :wide], w[D : 2 * D])
                    + mm_nt(x[:, wide:], w[2 * D :])
                )

            loop(body)
            deliver(parts, out_ref)

        dkv, sums_q, da_out = vmem_call(
            "da", k_da, [*dkv_in, dq, w_in],
            [stack(U, 2 * wide), piece(8, F32, wide), stack(U, D)],
            [pltpu.VMEM((G, U, D), F32)],
            flops=dot * U * G * 3 // 4 // D,
        )
        da_in = collect_g(da_out)
        dh_back = dh
        if near:
            own_kv = [(2, i * wide, wide) for i in range(2)]
            b_enc = home(
                "home_enc", [a, dq, dkv, o_all, *dhs],
                [
                    (
                        "enc", wide, r_in,
                        [(0, 1, False), (0, own_kv[0], False), (0, own_kv[1], False)],
                    ),
                    ("enc", wide, r_out, [(3, [4 + i for i in range(G)], True)]),
                ],
            )
            own_enc, other_enc = sum_j(b_enc, da_in, da_in)
            dh_back = after(dh, *b_enc)
        mix_v = from_queries(after(mix, da_out))

        def k_dx(got, x_ref, dh_ref, prm_r, dx_ref, sum_ref):
            da = total_of(got)
            z, rs = unit_rows(x_ref[...].astype(F32))
            dx_ref[...] = (dh_ref[...] + unit_back(z, rs, da * prm_r[0:1])).astype(BF)
            for i, x in enumerate([da * z, da]):
                sum_ref[i : i + 1, :] = jnp.sum(x, axis=0, keepdims=True)

        dx, sums_x = vmem_call(
            "dx", k_dx, [da_in, x_own, dh_back, prm], [piece(U), piece(8, F32)]
        )
        mix_v = jnp.where(v == 0, 0.0, after(mix_v, dx).astype(F32))
        last = jnp.stack([(y + mix_v).astype(BF), dx])
        if near:
            moved_enc = move_planes(other_enc)
            t_enc = sum_planes(after(own_enc, dx), moved_enc, r_out)
            t_mc = sum_planes(after(own_mc, dx), moved_mc, r_mlp)
            x_mc = lax.all_to_all(t_mc, "g", 0, 0, tiled=True)
            last, sums_x = after(last, *moved_enc), after(sums_x, *moved_enc)
        last = from_views(last)
        out_f, out_m, out_c = [t[0] for t in last]
        dx_f, dx_m, dx_c = [t[1] for t in last]

        deep_out = (-(-n_par // per) + 7) // 8 * 8
        blocks_out = -(-n_par // deep_out)

        def deal(sy, sh, sx, sq, cq_ref, ckv_ref, bf_ref, out_ref, full, ffn):
            kd, kg, kj, kv, kp = role()

            def if_view(k, x):
                return jnp.where(kv == k, x, 0.0)

            full[...] = jnp.zeros_like(full)
            ffn[...] = jnp.zeros_like(ffn)

            def at_cols(row, on, x):
                for k in range(G):
                    full[row : row + 1, k * wide : (k + 1) * wide] = jnp.where(
                        jnp.logical_and(on, kg == k), x, 0.0
                    )

            for k in range(3):
                full[2 * k : 2 * k + 1, :] = if_view(k, sx[0:1])
                full[2 * k + 1 : 2 * k + 2, :] = if_view(k, sh[0:1])
                at = 10 + 6 * k
                full[at : at + 1, :] = if_view(k, sx[1:2])
                at_cols(at + 1, kv == k, sq[0:1])
                at_cols(at + 2, kv == k, sq[1:2])
                full[at + 3 : at + 4, :] = if_view(k, sh[2:3])
                full[at + 4 : at + 5, :] = if_view(k, sh[1:2])
                full[at + 5 : at + 6, :] = if_view(k, sy[5:6])
                for i in range(G):
                    ffn[k : k + 1, i * hid : (i + 1) * hid] = jnp.where(
                        jnp.logical_and(kv == k, kg == i), bf_ref[...], 0.0
                    )
            for k in range(2):
                full[6 + 2 * k : 7 + 2 * k, :] = if_view(k + 1, sy[0:1])
                full[7 + 2 * k : 8 + 2 * k, :] = if_view(k, sy[2:3])
                at = 28 + 5 * k
                full[at : at + 1, :] = if_view(k + 1, sy[1:2])
                full[at + 1 : at + 2, :] = if_view(k, sy[3:4])
                at_cols(at + 2, kp == k, cq_ref[...])
                at_cols(at + 3, kp == k, ckv_ref[:, wide:])
                full[at + 4 : at + 5, :] = if_view(k + 1, sy[4:5])
            for i in range(n_dev):
                for r in range(3):
                    for t in range(fq):
                        to = 38 + r * fq + t
                        full[to : to + 1, i * gw : (i + 1) * gw] = ffn[
                            r : r + 1, i * fw + t * gw : i * fw + (t + 1) * gw
                        ]
            for i in range(n_dev):
                for b in range(blocks_out):
                    out_ref[i, :, b * gw : (b + 1) * gw] = full[
                        b * deep_out : (b + 1) * deep_out, i * gw : (i + 1) * gw
                    ]

        (small,) = vmem_call(
            "deal", deal, [sums_y, sums_h, sums_x, sums_q, dcq, dckv, dbf],
            [shape((n_dev, deep_out, 128), F32)],
            [pltpu.VMEM((blocks_out * deep_out, D), F32), pltpu.VMEM((3, ff), F32)],
        )
        small = lax.all_to_all(small, everyone, 0, 0, tiled=True)

        if near:
            x_enc = lax.all_to_all(
                after(t_enc, small, x_mc), "g", 0, 0, tiled=True
            )

        def my_rows(x):
            return lax.dynamic_index_in_dim(x, j, axis=2, keepdims=False)

        def send_home(grad, total, enc):
            width = grad.shape[1]
            r = total // n_dev
            if near:
                frame_rows, n_planes = total // 2, 2
                low = enc_lo if enc else cross_lo
            else:
                frame_rows, n_planes, low = total, dp, jnp.int32(0)
            if grad.shape[0] != frame_rows:
                part, n_parts = (v, 3) if enc else (p, 2)
                grad = lax.dynamic_update_slice_in_dim(
                    jnp.zeros((frame_rows, width), BF), grad.astype(BF),
                    start_of(part, n_parts, low, total), axis=0,
                )
            x = grad.astype(BF).reshape(n_planes, G, J, r, width)
            acc = lax.dynamic_index_in_dim(x, j, axis=2, keepdims=False).astype(F32)
            for n in range(1, J):
                part = lax.dynamic_index_in_dim(x, j ^ n, axis=2, keepdims=False)
                acc = acc + xor("j", n, J, part).astype(F32)
            if not near:
                acc = lax.psum_scatter(acc, "dp", scatter_dimension=0, tiled=False)
            elif enc:
                own = jnp.where(d == 0, acc[0], acc[1])
                other = jnp.where(d == 0, acc[1], acc[0]).astype(BF)
                down = lax.ppermute(other, "dp", [(1, 0), (2, 1), (3, 2)])
                upward = lax.ppermute(other, "dp", [(0, 1)])
                acc = own + down.astype(F32) + upward.astype(F32)
            else:
                odd = d % 2 == 1
                own = jnp.where(odd, acc[1], acc[0])
                other = jnp.where(odd, acc[0], acc[1]).astype(BF)
                acc = own + xor("dp", 1, dp, other).astype(F32)
            acc = acc.astype(BF).reshape(G * r, width)
            return lax.all_to_all(acc, "g", 0, 1, tiled=True).astype(F32)

        def in_order(w):
            return jnp.concatenate(
                [rows_at(w, (g ^ a) * wide, wide) for a in range(G)], axis=0
            )

        if near:
            def unpack_rows(x, i, in_ref, out_ref):
                unit = out_ref.shape[0]
                at = slice(i * wide, (i + 1) * wide)
                for b in range(4):
                    block = x[:, b * wide : (b + 1) * wide].astype(F32)
                    if b < 3:
                        in_ref[b * unit : (b + 1) * unit, at] = block
                    else:
                        out_ref[:, at] = block

            def landed(x_ref, gm_ref, gci_ref, gco_ref):
                for i in range(G):
                    gm_ref[:, i * hid : (i + 1) * hid] = x_ref[i, :r_mlp].astype(F32)
                    unpack_rows(x_ref[i, r_mlp:], i, gci_ref, gco_ref)

            grad_mlp, grad_cin, grad_cout = vmem_call(
                "landed", landed, [x_mc],
                [shape(mlp_w.shape, F32), shape(cross_in.shape, F32), shape(cross_out.shape, F32)],
            )

            def landed_enc(x_ref, gi_ref, go_ref):
                for i in range(G):
                    unpack_rows(x_ref[i], i, gi_ref, go_ref)

            grad_in, grad_out = vmem_call(
                "landed_enc", landed_enc, [x_enc],
                [shape(attn_in.shape, F32), shape(attn_out.shape, F32)],
            )
        else:
            flat = lambda t: t.reshape(-1, t.shape[-1])
            a_f, c_f, q_f, k_f = flat(a), flat(c), flat(qn), flat(kn)
            ckv, skv = flat(dkv_c), flat(dkv)
            dh_all = jnp.concatenate(dhs, axis=0)
            g_cin = jnp.concatenate(
                [mm_tn(q_f, flat(dq_c)), mm_tn(k_f, ckv[:, :wide]), mm_tn(k_f, ckv[:, wide:])],
                axis=0,
            )
            g_cols = jnp.concatenate([x[:, wide:] for x in given], axis=0)
            g_cout = in_order(mm_tn(flat(cross_o), g_cols))
            g_mlp = jnp.concatenate([mm_tn(c_f, flat(du)), mm_tn(flat(dm), flat(e))], axis=0)
            g_out = in_order(mm_tn(flat(o_all), cols(dh_all, wide)))
            g_in = jnp.concatenate(
                [mm_tn(a_f, flat(dq)), mm_tn(a_f, skv[:, :wide]), mm_tn(a_f, skv[:, wide:])],
                axis=0,
            )
            grad_cin = send_home(g_cin, n_dev * r_cross, False)
            grad_cout = send_home(g_cout, n_dev * r_co, False)
            grad_mlp = send_home(g_mlp, n_dev * r_mlp, True)
            grad_out = send_home(g_out, n_dev * r_out, True)
            grad_in = send_home(g_in, n_dev * r_in, True)

        def collect(x_ref, g_ref, b_ref, f_ref):
            x = jnp.sum(x_ref[...], axis=0)
            rows = [
                x[r % deep_out : r % deep_out + 1, r // deep_out * gw : (r // deep_out + 1) * gw]
                for r in range(n_par)
            ]
            for r in range(38):
                if r < 10:
                    g_ref[r : r + 1, :] = rows[r]
                else:
                    b_ref[r - 10 : r - 9, :] = rows[r]
            for r in range(3):
                for t in range(fq):
                    f_ref[r : r + 1, t * gw : (t + 1) * gw] = rows[38 + r * fq + t]

        grad_gains, grad_bias, grad_ffn = vmem_call(
            "collect", collect, [small],
            [shape(norm_gains.shape, F32), shape(biases.shape, F32), shape(ffn_bias.shape, F32)],
        )
        return (
            out_f[None], out_m[None], out_c[None],
            dx_f.astype(F32)[None], dx_m.astype(F32)[None], dx_c.astype(F32)[None],
            grad_in, grad_out, grad_mlp, grad_cin, grad_cout,
            grad_gains, grad_bias, grad_ffn,
        )

    tokens = P("dp", ("g", "j"), None)
    rows = P(everyone, None)
    columns = P(None, everyone)
    return jax.shard_map(
        per_device,
        mesh=mesh3,
        in_specs=(tokens,) * 6 + (P("dp", None),) + (rows,) * 5 + (columns,) * 3,
        out_specs=(tokens,) * 6 + (rows,) * 5 + (columns,) * 3,
        check_vma=False,
    )
```

```python
import math

import jax
import jax.numpy as jnp
from jax import lax
from jax.experimental import pallas as pl
from jax.experimental.pallas import tpu as pltpu
from jax.sharding import Mesh, PartitionSpec as P

D = 768
HEADS = 12
HD = 64
VIEWS = 3
EPS = 1e-06
NEG = -1e30
SCALE = HD**-0.5
BF = jnp.bfloat16
F32 = jnp.float32


def mm(a, b):
    return lax.dot_general(a, b, (((1,), (0,)), ((), ())), preferred_element_type=F32)


def mm_nt(a, b):
    return lax.dot_general(a, b, (((1,), (1,)), ((), ())), preferred_element_type=F32)


def mm_tn(a, b):
    return lax.dot_general(a, b, (((0,), (0,)), ((), ())), preferred_element_type=F32)


def unit_rows(u):
    centre = jnp.mean(u, axis=-1, keepdims=True)
    spread = u - centre
    rs = lax.rsqrt(jnp.mean(spread * spread, axis=-1, keepdims=True) + EPS)
    return spread * rs, rs


def unit_back(z, rs, dz):
    return rs * (
        dz - jnp.mean(dz, axis=-1, keepdims=True) - z * jnp.mean(dz * z, axis=-1, keepdims=True)
    )


def gelu_parts(u):
    phi = 0.5 * lax.erfc(u * (-(0.5**0.5)))
    return phi


def gelu_slope(u):
    return gelu_parts(u) + u * jnp.exp(-0.5 * u * u) * (1.0 / math.sqrt(2.0 * math.pi))


def rounds_of(moves):
    rounds = []
    for move in moves:
        for group in rounds:
            if all(move[0] != other[0] and move[1] != other[1] for other in group):
                group.append(move)
                break
        else:
            rounds.append([move])
    return rounds


def attend_kernel(heads, parts, idq_ref, idk_ref, q_ref, *rest):
    kv_refs, (o_ref, lse_ref) = rest[:parts], rest[parts:]
    wide = heads * HD
    q = q_ref[...].reshape(-1, wide)
    kv = jnp.concatenate([r[...].reshape(-1, 2 * wide) for r in kv_refs], axis=0)
    allowed = idk_ref[0] == idq_ref[0]
    outs = []
    for n in range(heads):
        cols = slice(n * HD, (n + 1) * HD)
        v_cols = slice(wide + n * HD, wide + (n + 1) * HD)
        s = jnp.where(allowed, mm_nt(kv[:, cols], q[:, cols]) * SCALE, NEG)
        top = jnp.max(s, axis=0, keepdims=True)
        p = jnp.exp(s - top)
        total = jnp.sum(p, axis=0, keepdims=True)
        lse_ref[0, n : n + 1, :] = top + jnp.log(total)
        pb = (p * (1.0 / total)).astype(BF)
        outs.append(mm(kv[:, v_cols].T, pb).T)
    put_half(o_ref, jnp.concatenate(outs, axis=1).astype(BF))


def put_half(o_ref, o):
    wide = o.shape[1]
    o = o.reshape(o_ref.shape[:2] + (wide,))

    @pl.when(pl.program_id(0) == 0)
    def _():
        o_ref[:, :, :wide] = o

    @pl.when(pl.program_id(0) == 1)
    def _():
        o_ref[:, :, wide:] = o


def attend_grads(heads, idq, idk, q, do, kv, lse):
    wide = heads * HD
    allowed = idk == idq
    os, dqs, dks, dvs = [], [], [], []
    for n in range(heads):
        cols = slice(n * HD, (n + 1) * HD)
        qn, kn, gn = q[:, cols], kv[:, cols], do[:, cols]
        vn = kv[:, wide + n * HD : wide + (n + 1) * HD]
        s = jnp.where(allowed, mm_nt(kn, qn) * SCALE, NEG)
        if lse is None:
            e = jnp.exp(s - jnp.max(s, axis=0, keepdims=True))
            p = e * (1.0 / jnp.sum(e, axis=0, keepdims=True))
        else:
            p = jnp.exp(s - lse[n : n + 1, :])
        pb = p.astype(BF)
        if lse is None:
            os.append(mm(vn.T, pb).T)
        dp = mm_nt(vn, gn)
        delta = jnp.sum(p * dp, axis=0, keepdims=True)
        ds = (p * (dp - delta)).astype(BF)
        dqs.append(mm(kn.T, ds).T * SCALE)
        dks.append(mm(ds, qn) * SCALE)
        dvs.append(mm(pb, gn))
    join = lambda xs: jnp.concatenate(xs, axis=1).astype(BF)
    return (join(os) if os else None), join(dqs), join(dks + dvs)


def put_parts(refs, x):
    rows = x.shape[0] // len(refs)
    for n, ref in enumerate(refs):
        ref[...] = x[n * rows : (n + 1) * rows].reshape(ref.shape)


def both_kernel(heads, parts, idq_ref, idk_ref, q_ref, do_ref, *rest):
    kv_refs, (o_ref, dq_ref, *dkv_refs) = rest[:parts], rest[parts:]
    wide = heads * HD
    q = q_ref[...].reshape(-1, wide)
    mine = lax.axis_index("g")
    do = jnp.concatenate([do_ref[mine ^ m, 0, :, :wide] for m in range(do_ref.shape[0])], axis=0)
    kv = jnp.concatenate([r[...].reshape(-1, 2 * wide) for r in kv_refs], axis=0)
    o, dq, dkv = attend_grads(heads, idq_ref[0], idk_ref[0], q, do, kv, None)
    put_half(o_ref, o)
    dq_ref[...] = dq.reshape(dq_ref.shape)
    put_parts(dkv_refs, dkv)


def back_kernel(heads, parts, pieces, idq_ref, idk_ref, q_ref, lse_ref, w_ref, *rest):
    dh_refs, rest = rest[:pieces], rest[pieces:]
    kv_refs, (dq_ref, *dkv_refs) = rest[:parts], rest[parts:]
    wide = heads * HD
    q = q_ref[...].reshape(-1, wide)
    dh = jnp.concatenate([r[0] for r in dh_refs], axis=0)
    do = mm_nt(dh, w_ref[...]).astype(BF)
    kv = jnp.concatenate([r[...].reshape(-1, 2 * wide) for r in kv_refs], axis=0)
    _, dq, dkv = attend_grads(heads, idq_ref[0], idk_ref[0], q, do, kv, lse_ref[0])
    dq_ref[...] = dq.reshape(dq_ref.shape)
    put_parts(dkv_refs, dkv)


def half_spec(a):
    return pl.BlockSpec((a.shape[0], 1) + a.shape[2:], lambda h: (0, h, 0, 0))


def side_by_side(q):
    return jax.ShapeDtypeStruct((q.shape[0], q.shape[2], 2 * q.shape[3]), q.dtype)


def all_spec(q):
    return pl.BlockSpec(side_by_side(q).shape, lambda h: (0, 0, 0))


def id_spec(a):
    return pl.BlockSpec((1,) + a.shape[1:], lambda h: (h, 0, 0))


def sds(a, dtype=None):
    return jax.ShapeDtypeStruct(a.shape, dtype or a.dtype)


def attention(name, kernel, ins, specs, outs, out_specs, flops, trans):
    nbytes = sum(a.size * a.dtype.itemsize for a in ins)
    return pl.pallas_call(
        kernel,
        grid=(2,),
        in_specs=specs,
        out_specs=out_specs,
        out_shape=outs,
        name=name,
        compiler_params=pltpu.CompilerParams(vmem_limit_bytes=48 * 1024 * 1024),
        cost_estimate=pl.CostEstimate(
            flops=flops, bytes_accessed=2 * nbytes, transcendentals=trans
        ),
    )(*ins)


def attend(heads, idq, idk, q, kvs):
    kernel = lambda *refs: attend_kernel(heads, len(kvs), *refs)
    ins = [idq, idk, q, *kvs]
    specs = [id_spec(idq), id_spec(idk)] + [half_spec(a) for a in ins[2:]]
    lse = jax.ShapeDtypeStruct((2, 8, idq.shape[2]), F32)
    pairs = 2 * heads * idq.shape[2] * idk.shape[1]
    return attention(
        "attend", kernel, ins, specs, [side_by_side(q), lse], [all_spec(q), id_spec(lse)],
        4 * pairs * HD, pairs,
    )


def attend_back(heads, idq, idk, q, lse, w_out, dhs, kvs):
    kernel = lambda *refs: back_kernel(heads, len(kvs), len(dhs), *refs)
    dhs = [x.reshape(2, -1, D) for x in dhs]
    ins = [idq, idk, q, lse, w_out, *dhs, *kvs]
    specs = [id_spec(idq), id_spec(idk), half_spec(q), id_spec(lse)]
    specs += [pl.BlockSpec((heads * HD, D), lambda h: (0, 0))]
    specs += [id_spec(x) for x in dhs] + [half_spec(a) for a in kvs]
    outs = [sds(q)] + [sds(a) for a in kvs]
    pairs = 2 * heads * idq.shape[2] * idk.shape[1]
    res = attention(
        "attend_back", kernel, ins, specs, outs, [half_spec(a) for a in outs],
        10 * pairs * HD, pairs,
    )
    return res[0], res[1:]


def attend_both(heads, idq, idk, q, do, kvs):
    kernel = lambda *refs: both_kernel(heads, len(kvs), *refs)
    do = do.reshape(do.shape[0], 2, -1, do.shape[-1])
    ins = [idq, idk, q, do, *kvs]
    specs = [id_spec(idq), id_spec(idk)] + [half_spec(a) for a in ins[2:]]
    outs = [side_by_side(q), sds(q)] + [sds(a) for a in kvs]
    pairs = 2 * heads * idq.shape[2] * idk.shape[1]
    res = attention(
        "attend_both", kernel, ins, specs, outs, [all_spec(q)] + [half_spec(a) for a in outs[1:]],
        12 * pairs * HD, pairs,
    )
    return res[0], res[1], res[2:]


def after(x, *others):
    return lax.optimization_barrier((x,) + others)[0]


def vmem_call(name, kernel, ins, outs, scratch=(), flops=0):
    nbytes = sum(a.size * a.dtype.itemsize for a in list(ins) + list(outs))
    spec = pl.BlockSpec(memory_space=pltpu.VMEM)
    return pl.pallas_call(
        kernel,
        in_specs=[spec] * len(ins),
        out_specs=[spec] * len(outs),
        out_shape=list(outs),
        scratch_shapes=list(scratch),
        name=name,
        compiler_params=pltpu.CompilerParams(vmem_limit_bytes=56 * 1024 * 1024),
        cost_estimate=pl.CostEstimate(flops=flops, bytes_accessed=nbytes, transcendentals=0),
    )(*ins)


def shape(dims, dtype):
    return jax.ShapeDtypeStruct(tuple(dims), dtype)


def aligned(x, n=8):
    return pl.multiple_of(x, n)


def solution(mesh):
    dp, seq = mesh.shape["dp"], mesh.shape["seq"]
    G = math.gcd(HEADS, seq)
    while G & (G - 1) or (seq // G) & (seq // G - 1):
        G //= 2
    J = seq // G
    heads = HEADS // G
    wide = heads * HD
    nf, nm = dp // 2, dp // 4
    mesh3 = Mesh(mesh.devices.reshape(dp, G, J), ("dp", "g", "j"))
    everyone = ("dp", "g", "j")

    view_of = [0 if d < nf else (1 if d < nf + nm else 2) for d in range(dp)]
    owner = [
        [r // 2 for r in range(dp)],
        [nf + r // 4 for r in range(dp)],
        [nf + nm + r // 4 for r in range(dp)],
    ]
    slot = [[r % 2 for r in range(dp)], [r % 4 for r in range(dp)], [r % 4 for r in range(dp)]]

    def xor(axis, n, size, x):
        return lax.ppermute(x, axis, [(i, i ^ n) for i in range(size)])

    def per_device(
        view_fine, view_mid, view_coarse, grad_fine, grad_mid, grad_coarse, clip_ids,
        attn_in, attn_out, mlp_w, cross_in, cross_out, norm_gains, biases, ffn_bias,
    ):
        tf, tm, tc = view_fine.shape[1], view_mid.shape[1], view_coarse.shape[1]
        U = 2 * tf
        ff = mlp_w.shape[1]
        cells = clip_ids.shape[1]
        d, g, j = lax.axis_index("dp"), lax.axis_index("g"), lax.axis_index("j")
        v = jnp.where(d < nf, 0, jnp.where(d < nf + nm, 1, 2))
        p = jnp.where(d < nf, 0, 1)

        def table(values, index=d):
            out = jnp.int32(values[-1])
            for i in range(len(values) - 1):
                out = jnp.where(index == i, jnp.int32(values[i]), out)
            return out

        def pick(tag, options, dtype=None):
            out = jnp.zeros_like(options[0])
            for k, option in enumerate(options):
                out = jnp.where(tag == k, option, out)
            return out

        def rows_at(x, start, size):
            return lax.dynamic_slice_in_dim(x, start, size, axis=0)

        sizes = (tf, tm, tc)
        moves = [
            (r, owner[w][r], (w, r))
            for w in (0, 2, 1)
            for r in range(dp)
            if r != owner[w][r]
        ]
        view_rounds = rounds_of(moves)
        back_rounds = rounds_of([m for m in moves if m[2][0] == 0]) + rounds_of(
            [m for m in moves if m[2][0] != 0]
        )

        def grow(x, rows):
            n = x.shape[-2]
            if n == rows:
                return x
            pad = jnp.zeros(x.shape[:-2] + (rows - n, x.shape[-1]), x.dtype)
            return jnp.concatenate([x, pad], axis=-2)

        def to_views(fine, mid, coarse):
            mid_p, coarse_p = grow(mid, tf), grow(coarse, tf)
            got = []
            for group in view_rounds:
                n = max(sizes[w] for _, _, (w, _) in group)
                kind = [3] * dp
                for src, _, (w, _) in group:
                    kind[src] = w
                load = pick(table(kind), [t[:, :n] for t in (fine, mid_p, coarse_p)])
                got.append(grow(lax.ppermute(load, "dp", [(s, t) for s, t, _ in group]), tf))
            local = pick(v, [fine, mid_p, coarse_p])
            rows = []
            for k in range(4):
                tag = [len(got) + 1] * dp
                for i, group in enumerate(view_rounds):
                    for _, dst, (w, r) in group:
                        if slot[w][r] == k:
                            tag[dst] = i + 1
                for r in range(dp):
                    if owner[view_of[r]][r] == r and slot[view_of[r]][r] == k:
                        tag[r] = 0
                rows.append(pick(table(tag), [local] + got))
            join = lambda xs: jnp.concatenate(xs, axis=1)
            pad = jnp.zeros((fine.shape[0], tf - 2 * tc, fine.shape[2]), fine.dtype)
            as_coarse = [rows[0][:, :tc], rows[1][:, :tc], pad, rows[2][:, :tc], rows[3][:, :tc], pad]
            return pick(
                v, [join(rows[:2]), join([x[:, :tm] for x in rows]), join(as_coarse)]
            )

        def route(name, views, moves, local, rows, zero):
            rounds = rounds_of(moves)
            heights = [max(m[2][2] for m in group) for group in rounds]

            def load(*refs):
                kd = lax.axis_index("dp")
                for group, out in zip(rounds, refs[len(views) :]):
                    for src, _, (w, first, size, _) in group:

                        @pl.when(kd == src)
                        def _(w=w, first=first, size=size, out=out):
                            out[:size, :] = refs[w][first : first + size, :]

            loads = vmem_call(name + "_load", load, views, [shape((n, D), BF) for n in heights])
            got = [
                lax.ppermute(x, "dp", [(a, b) for a, b, _ in group])
                for x, group in zip(loads, rounds)
            ]

            def unload(*refs):
                got_refs, out = refs[len(views) : -1], refs[-1]
                kd = lax.axis_index("dp")
                for here in range(dp):

                    @pl.when(kd == here)
                    def _(here=here):
                        if here in zero:
                            out[...] = jnp.zeros_like(out)
                        for src, _, (w, first, size, at) in local:
                            if src == here:
                                out[at : at + size, :] = refs[w][first : first + size, :]
                        for ref, group in zip(got_refs, rounds):
                            for _, dst, (_, _, size, at) in group:
                                if dst == here:
                                    out[at : at + size, :] = ref[:size, :]

            (out,) = vmem_call(name + "_unload", unload, views + got, [shape((rows, D), BF)])
            return out

        def grads_to_views(fine, mid, coarse):
            all_moves = [
                (r, owner[w][r], (w, 0, sizes[w], place(w, slot[w][r])))
                for w in (0, 2, 1)
                for r in range(dp)
            ]
            zero = [x for x in range(dp) if view_of[x] == 2]
            return route(
                "grads", [fine[0], mid[0], coarse[0]],
                [m for m in all_moves if m[0] != m[1]], [m for m in all_moves if m[0] == m[1]],
                U, zero,
            )

        def grads_to_queries(mid, coarse):
            all_moves = [(r, r // 2, (0, 0, tm, r % 2 * tm)) for r in range(dp)]
            all_moves += [(r, nf + r // 4, (1, 0, tc, r % 4 * tc)) for r in range(dp)]
            zero = [x for x in range(dp) if view_of[x] == 2]
            return route(
                "query_grads", [mid[0], coarse[0]],
                [m for m in all_moves if m[0] != m[1]], [m for m in all_moves if m[0] == m[1]],
                2 * tm, zero,
            )

        def place(w, k):
            return (tf * k, tm * k, tf * (k // 2) + tc * (k % 2))[w]

        def from_views(x):
            padded = grow(x, U + tf)
            rows_of = lambda start, n: lax.dynamic_slice_in_dim(padded, start, n, axis=1)
            got = []
            for group in back_rounds:
                n = max(sizes[w] for _, _, (w, _) in group)
                start = [0] * dp
                for _, src, (w, r) in group:
                    start[src] = place(w, slot[w][r])
                load = rows_of(table(start), n)
                got.append(grow(lax.ppermute(load, "dp", [(t, s) for s, t, _ in group]), tf))
            local_start = [0] * dp
            for r in range(dp):
                w = view_of[r]
                if owner[w][r] == r:
                    local_start[r] = place(w, slot[w][r])
            local = rows_of(table(local_start), tf)
            outs = []
            for w in range(VIEWS):
                tag = [0] * dp
                for i, group in enumerate(back_rounds):
                    for _, dst, (w2, r) in group:
                        if w2 == w:
                            tag[r] = i + 1
                outs.append(pick(table(tag), [local] + got)[:, : sizes[w]])
            return outs

        q_moves = [(nf + (2 * t) // 4, t, t % 2) for t in range(nf)]
        q_moves += [(nf + nm + i, nf + i, 0) for i in range(nm)]
        q_rounds = rounds_of(q_moves)

        def to_queries(x):
            dense = jnp.concatenate([x[: 2 * tc], x[tf : tf + 2 * tc]], axis=0)
            got = []
            for group in q_rounds:
                start = [0] * dp
                for src, _, h in group:
                    start[src] = h * tf
                load = jnp.where(v == 2, dense, rows_at(x, table(start), tf))
                got.append(lax.ppermute(load, "dp", [(s, t) for s, t, _ in group]))
            tag = [len(got)] * dp
            for i, group in enumerate(q_rounds):
                for _, dst, _ in group:
                    tag[dst] = i
            return pick(table(tag), got)

        def from_queries(x):
            got = [lax.ppermute(x, "dp", [(t, s) for s, t, _ in group]) for group in q_rounds]
            parts = []
            for half in range(2):
                tag = [len(got)] * dp
                for i, group in enumerate(q_rounds):
                    for src, _, h in group:
                        if h == half:
                            tag[src] = i
                parts.append(pick(table(tag), got))
            pad = jnp.zeros((tf - 2 * tc, x.shape[1]), x.dtype)
            coarse = jnp.concatenate([parts[0][: 2 * tc], pad, parts[0][2 * tc :], pad], axis=0)
            return jnp.where(v == 2, coarse, jnp.concatenate(parts, axis=0))

        def spread_g(x):
            return [x] + [xor("g", m, G, x) for m in range(1, G)]

        def sum_g(pieces):
            out = pieces[0].astype(F32)
            got = [xor("g", m, G, pieces[m].astype(BF)) for m in range(1, G)]
            for x in got:
                out = out + x.astype(F32)
            return out

        def spread_j(x):
            return [x] + [xor("j", n, J, x) for n in range(1, J)]

        n_dev = dp * seq
        gw, fw = norm_gains.shape[1], ffn_bias.shape[1]
        fq = fw // gw
        hid = ff // G
        id_rows = cells // gw
        n_vec = 38 + 3 * fq + id_rows
        n_par = 38 + 3 * fq
        per = 128 // gw
        deep = (-(-n_vec // per) + 7) // 8 * 8
        blocks = -(-n_vec // deep)

        def pack_vec(g_ref, b_ref, f_ref, i_ref, out_ref, rows):
            rows[...] = jnp.zeros_like(rows)
            rows[:10, :] = g_ref[...].astype(F32)
            rows[10:38, :] = b_ref[...].astype(F32)
            for r in range(3):
                for t in range(fq):
                    at = 38 + r * fq + t
                    rows[at : at + 1, :] = f_ref[r : r + 1, t * gw : (t + 1) * gw].astype(F32)
            for t in range(id_rows):
                at = n_par + t
                rows[at : at + 1, :] = i_ref[0:1, t * gw : (t + 1) * gw].astype(F32)
            out = [rows[b * deep : (b + 1) * deep, :] for b in range(blocks)]
            out.append(jnp.zeros((deep, 128 - blocks * gw), F32))
            out = jnp.concatenate(out, axis=1).astype(BF)
            for i in range(n_dev):
                out_ref[i] = out

        def role():
            kd, kg, kj = lax.axis_index("dp"), lax.axis_index("g"), lax.axis_index("j")
            kv = jnp.where(kd < nf, 0, jnp.where(kd < nf + nm, 1, 2))
            return kd, kg, kj, kv, jnp.where(kd < nf, 0, 1)

        def setup(vec_ref, prm_ref, idq_ref, idk_ref, cidq_ref, full, ffn):
            kd, kg, kj, kv, kp = role()
            for i in range(n_dev):
                x = vec_ref[i].astype(F32)
                for b in range(blocks):
                    full[b * deep : (b + 1) * deep, i * gw : (i + 1) * gw] = x[
                        :, b * gw : (b + 1) * gw
                    ]
            for i in range(n_dev):
                for r in range(3):
                    for t in range(fq):
                        at = i * fw + t * gw
                        ffn[r : r + 1, at : at + gw] = full[
                            38 + r * fq + t : 39 + r * fq + t, i * gw : (i + 1) * gw
                        ]

            def row(r):
                return full[r : r + 1, :]

            def by_view(rows):
                return jnp.where(kv == 0, rows[0], jnp.where(kv == 1, rows[1], rows[2]))

            def part(x, width):
                out = x[:, :width]
                for i in range(1, G):
                    out = jnp.where(kg == i, x[:, i * width : (i + 1) * width], out)
                return out

            prm_ref[...] = jnp.zeros_like(prm_ref)
            for i in range(2):
                prm_ref[i : i + 1, :] = by_view([row(2 * k + i) for k in range(3)])
            for i in range(6):
                x = by_view([row(10 + 6 * k + i) for k in range(3)])
                if i in (1, 2):
                    prm_ref[2 + i : 3 + i, :wide] = part(x, wide)
                else:
                    prm_ref[2 + i : 3 + i, :] = x
            prm_ref[8:9, :hid] = part(by_view([ffn[k : k + 1, :] for k in range(3)]), hid)
            prm_ref[9:10, :] = by_view([row(6), row(6), row(8)])
            prm_ref[10:11, :] = by_view([row(7), row(9), row(9)])
            prm_ref[11:12, :] = by_view([row(28), row(28), row(33)])
            prm_ref[12:13, :] = by_view([row(29), row(34), row(34)])
            for i in range(3):
                x = jnp.where(kp == 0, row(30 + i), row(35 + i))
                if i < 2:
                    prm_ref[13 + i : 14 + i, :wide] = part(x, wide)
                else:
                    prm_ref[13 + i : 14 + i, :] = x

            starts = []
            for r in range(dp):
                x = full[n_par:n_vec, r * seq * gw : (r * seq + 1) * gw]
                starts.append(
                    [jnp.sum((x < c).astype(F32), keepdims=True) for c in (0.5, 1.5, 2.5)]
                )

            def start_at(index):
                out = starts[0]
                for r in range(1, dp):
                    out = [jnp.where(index == r, b, a) for a, b in zip(out, starts[r])]
                return out

            def ids(first, second, unit, per_cell, cap, u, k, n):
                s = (kg ^ k) * J + (kj ^ n)
                late = u >= unit
                pos = (s * unit + u - jnp.where(late, unit, 0)).astype(F32)
                out = jnp.zeros(u.shape, F32)
                for a, b in zip(first, second):
                    edge = jnp.where(late, b, a) * per_cell.astype(F32)
                    out = out + (pos >= edge).astype(F32)
                out = out + jnp.where(late, 4.0, 0.0)
                return jnp.where(u >= cap, -1.0, out)

            unit = jnp.where(kv == 0, tf, jnp.where(kv == 1, tm, tc))
            per_cell = jnp.where(kv == 0, 4, jnp.where(kv == 1, 2, 1))
            base = jnp.where(kv == 0, 2 * kd, 4 * ((kd - nf) % nm))
            q_unit, q_cell = jnp.where(kp == 0, tm, tc), jnp.where(kp == 0, 2, 1)
            for h in range(2):
                first = start_at(base + jnp.where(kv == 0, h, 2 * h))
                second = start_at(base + 2 * h + 1)
                for k in range(G):
                    lane = lax.broadcasted_iota(jnp.int32, (1, tf), 1)
                    idq_ref[h, :, k * tf : (k + 1) * tf] = ids(
                        first, second, unit, per_cell, 2 * unit, lane, k, 0
                    )
                    lane = lax.broadcasted_iota(jnp.int32, (1, tm), 1)
                    cidq_ref[h, :, k * tm : (k + 1) * tm] = ids(
                        first, second, q_unit, q_cell, tm, lane, k, 0
                    )
                    for n in range(J):
                        deep_u = lax.broadcasted_iota(jnp.int32, (tf, 1), 0)
                        at = (n * G + k) * tf
                        idk_ref[h, at : at + tf, :] = ids(
                            first, second, unit, per_cell, 2 * unit, deep_u, k, n
                        )

        def cols(x, width):
            return lax.dynamic_slice_in_dim(x, g * width, width, axis=-1)

        near = dp == 4

        def both_sides(x):
            return xor("dp", 1, dp, x), lax.ppermute(x, "dp", [(1, 2)])

        def chunks(x):
            if near:
                twin, below = both_sides(x)
                odd = d % 2 == 1
                lo = jnp.where(d == 2, below, jnp.where(odd, twin, x))
                enc = jnp.stack([lo, jnp.where(d == 0, twin, x)])
                cross = jnp.stack([jnp.where(odd, twin, x), jnp.where(odd, x, twin)])
                return enc, cross
            everything = lax.all_gather(x, "dp", axis=0)
            return everything, everything

        enc_lo = jnp.maximum(d - 1, 0) if near else jnp.int32(0)
        cross_lo = 2 * p if near else jnp.int32(0)

        def start_of(part, n_parts, low, total):
            return part * (total // n_parts) - low * (total // dp)

        def join_j(x):
            xs = spread_j(x)
            parts = []
            for a in range(J):
                out = xs[0]
                for n in range(1, J):
                    out = jnp.where((j ^ n) == a, xs[n], out)
                parts.append(out)
            full = jnp.stack(parts, axis=2)
            return full.reshape(-1, x.shape[-1])

        r_in, r_cross = attn_in.shape[0], cross_in.shape[0]
        r_mlp, r_out, r_co = mlp_w.shape[0], attn_out.shape[0], cross_out.shape[0]

        def half_of(r):
            return (r + 15) // 16 * 8

        h_in, h_cross = half_of(r_in), half_of(r_cross)
        lanes = 2 * wide

        def pack(dst, i, at, r, x):
            half = half_of(r)
            dst[i, at : at + half, :wide] = x[:half]
            dst[i, at : at + r - half, wide:] = x[half:]

        def split_qkv(in_ref, cross_ref, qkv_ref):
            for i in range(G):
                at = slice(i * wide, (i + 1) * wide)
                pack(qkv_ref, i, 0, r_in, in_ref[:, at])
                pack(qkv_ref, i, h_in, r_cross, cross_ref[:, at])

        def split_mlp(mlp_ref, mlp_out):
            for i in range(G):
                mlp_out[i] = mlp_ref[:, i * hid : (i + 1) * hid]

        outs = jnp.concatenate([attn_out, cross_out], axis=0)
        (vec,) = vmem_call(
            "pack_vec", pack_vec, [norm_gains, biases, ffn_bias, clip_ids],
            [shape((n_dev, deep, 128), BF)], [pltpu.VMEM((blocks * deep, gw), F32)],
        )
        if near:
            (qkv,) = vmem_call(
                "split_qkv", split_qkv, [attn_in, cross_in],
                [shape((G, h_in + h_cross, lanes), BF)],
            )
            vec = after(vec, qkv)
        vecs = lax.all_to_all(vec, everyone, 0, 0, tiled=True)
        if near:
            qkv = lax.all_to_all(after(qkv, vecs), "g", 0, 0, tiled=True)
            x_own = to_views(after(view_fine, qkv), view_mid, view_coarse)[0]
            (mlp,) = vmem_call(
                "split_mlp", split_mlp, [after(mlp_w, x_own)], [shape((G, r_mlp, hid), BF)]
            )
            mlp = lax.all_to_all(mlp, "g", 0, 0, tiled=True)
        else:
            x_own = to_views(view_fine, view_mid, view_coarse)[0]
            qkv = lax.all_to_all(
                jnp.concatenate([attn_in, cross_in], axis=0), "g", 1, 0, tiled=True
            ).reshape(G, r_in + r_cross, wide)
            mlp = lax.all_to_all(mlp_w, "g", 1, 0, tiled=True).reshape(G, r_mlp, hid)
        set_outs = [
            shape((16, D), F32),
            shape((2, 1, G * tf), F32), shape((2, seq * tf, 1), F32), shape((2, 1, G * tm), F32),
        ]
        prm, idq, idk, cross_idq = pl.pallas_call(
            setup,
            grid=(1,),
            in_specs=[pl.BlockSpec((n_dev, deep, 128), lambda i: (0, 0, 0))],
            out_specs=[
                pl.BlockSpec(t.shape, lambda i, n=len(t.shape): (0,) * n) for t in set_outs
            ],
            out_shape=set_outs,
            scratch_shapes=[pltpu.VMEM((blocks * deep, D), F32), pltpu.VMEM((3, ff), F32)],
            name="setup",
            compiler_params=pltpu.CompilerParams(vmem_limit_bytes=32 * 1024 * 1024),
        )(vecs)

        def offset(kind, total, kd, kv, kp):
            low = jnp.maximum(kd - 1, 0)
            return kv * (total // 3) - low * (total // 4) if kind == "enc" else kp * 0

        gc_own = grads_to_queries(after(grad_mid, x_own), grad_coarse)

        def assemble(name, x, parts, width, sides, wait=None):
            twin, below = sides
            if wait is not None:
                twin, below = after(twin, wait), after(below, wait)
            srcs = [*spread_j(x), *spread_j(twin), *spread_j(below)]
            packed = width != x.shape[2]
            outs, scratch = [], []
            for kind, _, r in parts:
                outs.append(shape((n_dev * r // (3 if kind == "enc" else 2), width), BF))
                scratch.append(pltpu.VMEM((n_dev * r // 2, width), F32))

            def kernel(*refs):
                kd, kg, kj, kv, kp = role()
                own, twin_r, below_r = refs[:J], refs[J : 2 * J], refs[2 * J : 3 * J]
                out_refs = refs[3 * J : 3 * J + len(parts)]
                frames = refs[3 * J + len(parts) :]

                for (kind, first, r), frame in zip(parts, frames):

                    def put(t, group, first=first, r=r, frame=frame):
                        for n, ref in enumerate(group):
                            for i in range(G):
                                at = ((t * G + i) * J + (kj ^ n)) * r
                                size = half_of(r) if packed else r
                                frame[pl.ds(aligned(at), size), :] = ref[
                                    i, first : first + size, :width
                                ].astype(F32)
                                if packed:
                                    frame[pl.ds(aligned(at + size), r - size), :] = ref[
                                        i, first : first + r - size, width:
                                    ].astype(F32)

                    own_first = kd == 0 if kind == "enc" else kd % 2 == 0
                    from_below = kd == 2 if kind == "enc" else kd < 0

                    @pl.when(own_first)
                    def _(put=put):
                        put(0, own)
                        put(1, twin_r)

                    @pl.when(from_below)
                    def _(put=put):
                        put(0, below_r)
                        put(1, own)

                    @pl.when(jnp.logical_not(jnp.logical_or(own_first, from_below)))
                    def _(put=put):
                        put(0, twin_r)
                        put(1, own)

                for (kind, _, r), frame, out in zip(parts, frames, out_refs):
                    at = aligned(offset(kind, n_dev * r, kd, kv, kp))
                    out[...] = frame[pl.ds(at, out.shape[0]), :].astype(BF)

            return vmem_call(name, kernel, srcs, outs, scratch)

        if near:
            w_in, c_in = assemble(
                "assemble_in", qkv, [("enc", 0, r_in), ("cross", h_in, r_cross)], wide,
                both_sides(qkv),
            )
            mlp_sides = both_sides(after(mlp, w_in, gc_own))
        else:
            enc_c, cross_c = chunks(qkv)
            w_in = rows_at(
                join_j(enc_c[:, :, :r_in]), start_of(v, 3, enc_lo, n_dev * r_in), 3 * D
            )
            c_in = rows_at(
                join_j(cross_c[:, :, r_in:]), start_of(p, 2, cross_lo, n_dev * r_cross), 3 * D
            )

        def mlp_weights(wait):
            if near:
                return assemble(
                    "assemble_mlp", mlp, [("enc", 0, r_mlp)], hid, mlp_sides, wait
                )[0]
            enc_c, _ = chunks(mlp)
            return rows_at(join_j(enc_c), start_of(v, 3, enc_lo, n_dev * r_mlp), 2 * D)

        enc_c, cross_c = chunks(outs)
        planes = enc_c.shape[0]
        outs = jnp.concatenate([enc_c[:, :r_out], cross_c[:, r_out:]], axis=1)
        outs = lax.all_gather(outs.reshape(-1, D), ("g", "j"), axis=0)
        outs = outs.reshape(seq, planes, r_out + r_co, D)

        def arrange(x_ref, w_ref, c_ref, frame, cross_frame):
            kd, kg, kj, kv, kp = role()
            for t in range(planes):
                for i in range(seq):
                    at = (t * seq + i) * r_out
                    frame[at : at + r_out, :] = x_ref[i, t, :r_out].astype(F32)
                    at = (t * seq + i) * r_co
                    cross_frame[at : at + r_co, :] = x_ref[i, t, r_out:].astype(F32)
            low = jnp.maximum(kd - 1, 0) if near else 0
            first = kv * (n_dev * r_out // 3) - low * (n_dev * r_out // dp)
            cross_first = 0 if near else kp * (n_dev * r_co // 2)
            for m in range(G):
                to = slice(m * wide, (m + 1) * wide)
                at = aligned(first + (kg ^ m) * wide)
                w_ref[to, :] = frame[pl.ds(at, wide), :].astype(BF)
                at = aligned(cross_first + (kg ^ m) * wide)
                c_ref[to, :] = cross_frame[pl.ds(at, wide), :].astype(BF)

        def out_weights(wait):
            return vmem_call(
                "arrange_out", arrange, [after(outs, wait)],
                [shape((D, D), BF), shape((D, D), BF)],
                [
                    pltpu.VMEM((planes * seq * r_out, D), F32),
                    pltpu.VMEM((planes * seq * r_co, D), F32),
                ],
            )

        def home(name, arrays, parts):
            ins = list(arrays)
            places, row, lane = [], 0, 0
            for _, width, r, _ in parts:
                if width == D:
                    places.append((row, 0, r))
                    row += r
                else:
                    unit = n_unit(parts, width)
                    places.append((row, lane, unit))
                    lane += r // unit * width
                    if lane == D:
                        row, lane = row + unit, 0
            outs = [shape((2, G, row, D), BF) for _ in range(J)]
            scratch = [pltpu.VMEM((n_dev * r // 2, width), F32) for _, width, r, _ in parts]

            def kernel(*refs):
                kd, kg, kj, kv, kp = role()
                in_refs = refs[: len(ins)]
                out_refs = refs[len(ins) : len(ins) + J]
                frames = refs[len(ins) + J :]

                def value(key):
                    if isinstance(key, list):
                        return jnp.concatenate([value(k) for k in key], axis=0)
                    if isinstance(key, tuple) and len(key) == 4:
                        index, at, size, _ = key
                        return jnp.concatenate(
                            [in_refs[index][kg ^ m, :, at : at + size] for m in range(G)], axis=0
                        )
                    index, at, size = key if isinstance(key, tuple) else (key, 0, None)
                    x = in_refs[index][...]
                    x = x.reshape(-1, x.shape[-1])
                    return x if size is None else x[:, at : at + size]

                for (kind, width, r, mats), frame, place in zip(parts, frames, places):
                    if kind == "enc":
                        frame[...] = jnp.zeros_like(frame)
                    base = offset(kind, n_dev * r, kd, kv, kp)
                    for i, (left, right, grouped) in enumerate(mats):
                        b = value(right)
                        if b.shape[1] > width:
                            x = b[:, :wide]
                            for k in range(1, G):
                                x = jnp.where(kg == k, b[:, k * wide : (k + 1) * wide], x)
                            b = x
                        res = mm_tn(value(left), b)
                        if grouped:
                            for m in range(G):
                                at = aligned(base + i * D + (kg ^ m) * wide)
                                frame[pl.ds(at, wide), :] = res[m * wide : (m + 1) * wide]
                        else:
                            frame[pl.ds(aligned(base + i * D), D), :] = res
                    own = jnp.where(kd == 0, 0, 1) if kind == "enc" else kd % 2
                    first, lane0, unit = place
                    for n in range(J):
                        for side in range(2):
                            t = own if side == 0 else 1 - own
                            for k in range(G):
                                at = ((t * G + k) * J + (kj ^ n)) * r
                                for i in range(r // unit):
                                    to = lane0 + i * width
                                    out_refs[n][
                                        side, k, first : first + unit, to : to + width
                                    ] = frame[pl.ds(aligned(at + i * unit), unit), :].astype(BF)

            return vmem_call(name, kernel, ins, outs, scratch)

        def n_unit(parts, width):
            return min(r for _, w, r, _ in parts if w == width)

        def sum_j(blocks, ready, *wait):
            got = [xor("j", n, J, after(blocks[n], ready)) for n in range(1, J)]
            acc = after(blocks[0], *wait).astype(F32)
            for x in got:
                acc = acc + x.astype(F32)
            return acc[0].astype(BF), acc[1].astype(BF)

        def move_planes(other):
            return xor("dp", 1, dp, other), lax.ppermute(other, "dp", [(2, 1)])

        def sum_planes(own, moved, enc_rows):
            got, below = moved
            enc = lax.broadcasted_iota(jnp.int32, own.shape, 1) < enc_rows
            got = jnp.where(enc & (d == 3), 0.0, got.astype(F32))
            got = got + jnp.where(enc, below.astype(F32), 0.0)
            return (own.astype(F32) + got).astype(BF)

        Uq = 2 * tm
        dot = 2 * D * D

        def piece(rows, dtype=BF, width=D):
            return shape((rows, width), dtype)

        def stack(rows, width, dtype=BF):
            return shape((G, rows, width), dtype)

        def loop(body):
            lax.fori_loop(0, G, lambda k, c: (body(k), c)[1], 0)

        def stage(refs, dst):
            for i, ref in enumerate(refs):
                dst[i] = ref[...]

        def deliver(src, out_ref):
            for m in range(G):
                out_ref[lax.axis_index("g") ^ m] = src[m].astype(BF)

        def deliver_each(src, out_refs):
            for m, ref in enumerate(out_refs):
                ref[...] = src[m].astype(BF)

        def swap_g(pieces):
            return [pieces[0]] + [xor("g", m, G, pieces[m]) for m in range(1, G)]

        def gather_g(x):
            return collect_g(jnp.broadcast_to(x[None], (G,) + x.shape))

        def stage_all(ref, dst):
            for m in range(G):
                dst[m] = ref[lax.axis_index("g") ^ m]

        def collect_g(x):
            return lax.all_to_all(x, "g", 0, 0, tiled=True)

        def total_of(ref):
            out = ref[0].astype(F32)
            for m in range(1, G):
                out = out + ref[m].astype(F32)
            return out

        xs = gather_g(x_own)

        def k_qkv(*refs):
            x_in, w, prm_r, x_ref, a_ref, q_ref, kv_ref = refs
            stage_all(x_in, x_ref)

            def body(k):
                z, _ = unit_rows(x_ref[k].astype(F32))
                a = (z * prm_r[0:1] + prm_r[2:3]).astype(BF)
                a_ref[k] = a
                q_ref[k] = (mm(a, w[:D]) + prm_r[3:4, :wide]).astype(BF)
                kv_ref[k, :, :wide] = mm(a, w[D : 2 * D]).astype(BF)
                kv_ref[k, :, wide:] = (mm(a, w[2 * D :]) + prm_r[4:5, :wide]).astype(BF)

            loop(body)

        x_all, a, q, kv = vmem_call(
            "qkv", k_qkv, [xs, w_in, prm],
            [stack(U, D), stack(U, D), stack(U, wide), stack(U, 2 * wide)],
            flops=dot * U * G * 3 // 4 // D,
        )

        def halves(t):
            return t.reshape(G, 2, -1, t.shape[-1])

        q4 = halves(q)
        kvs = [halves(t) for t in spread_j(kv)]
        o, lse = attend(heads, idq, idk, q4, kvs)
        os = spread_g(o)

        def unfold(r, k):
            x = r[k]
            return jnp.concatenate([x[:, :wide], x[:, wide:]], axis=0)

        w_mlp = mlp_weights(kv)
        w_out, c_out = out_weights(o)

        def gelu_of(u):
            cdf = 0.5 * (1.0 + lax.erf(u * (0.5**0.5)))
            return u * cdf, cdf + u * jnp.exp(-0.5 * u * u) * (1.0 / math.sqrt(2.0 * math.pi))

        def k_mlp(*refs):
            o_refs, (x_ref, wo, wm, prm_r, *rest) = refs[:G], refs[G:]
            oa_ref, c_ref, slope_ref, e_ref, h_ref, y_ref, parts = rest

            def body(k):
                o_k = jnp.concatenate([unfold(r, k ^ m) for m, r in enumerate(o_refs)], axis=1)
                oa_ref[k] = o_k
                h = x_ref[k].astype(F32) + (mm(o_k, wo[...]) + prm_r[5:6])

                @pl.when(k == 0)
                def _():
                    h_ref[...] = h

                z, _ = unit_rows(h)
                c = (z * prm_r[1:2] + prm_r[6:7]).astype(BF)
                c_ref[k] = c
                e, slope = gelu_of(mm(c, wm[:D]) + prm_r[8:9, :hid])
                e = e.astype(BF)
                e_ref[k] = e
                slope_ref[k] = slope.astype(BF)
                parts[k] = mm_nt(e, wm[D:])

            loop(body)
            deliver(parts, y_ref)

        o_all, c, slope, e, h_own, y_out = vmem_call(
            "mlp", k_mlp, [*os, x_all, w_out, w_mlp, prm],
            [stack(U, D), stack(U, D), stack(U, hid), stack(U, hid), piece(U, F32), stack(U, D)],
            [pltpu.VMEM((G, U, D), F32)],
            flops=3 * dot * U * G // D,
        )
        y_in = collect_g(y_out)

        def k_given(g_ref, w, out_ref):
            grad = g_ref[...]
            kg = lax.axis_index("g")
            for m in range(G):
                out_ref[kg ^ m, :, :wide] = mm_nt(grad, w[m * wide : (m + 1) * wide]).astype(BF)
            for k in range(G):
                out_ref[k, :, wide:] = grad[:, k * wide : (k + 1) * wide]

        (given,) = vmem_call("given", k_given, [gc_own, c_out], [stack(Uq, 2 * wide)])
        given = collect_g(given)
        h_own = after(h_own, given)

        def k_norm(h_ref, got, prm_r, y_ref, zy_ref, rs_ref, kn_ref, qn_ref):
            y = total_of(got) + h_ref[...] + prm_r[7:8]
            y_ref[...] = y
            z, rs = unit_rows(y)
            zy_ref[...] = z
            rs_ref[...] = rs
            kn_ref[...] = (z * prm_r[10:11] + prm_r[12:13]).astype(BF)
            qn_ref[...] = (z * prm_r[9:10] + prm_r[11:12]).astype(BF)

        y, zy, rs_y, kn_v, qn_v = vmem_call(
            "norm_y", k_norm, [h_own, y_in, prm],
            [piece(U, F32), piece(U, F32), piece(U, F32, 1), piece(U), piece(U)],
        )
        kns = spread_g(kn_v)
        qns = spread_g(to_queries(qn_v))

        grad_own = grads_to_views(after(grad_fine, kns[1]), grad_mid, grad_coarse)

        def k_cross(*refs):
            q_refs, k_refs, (w, prm_r, qn_ref, kn_ref, q_ref, kv_ref) = (
                refs[:G], refs[G : 2 * G], refs[2 * G :],
            )
            stage(q_refs, qn_ref)
            stage(k_refs, kn_ref)

            def body(k):
                q_ref[k] = (mm(qn_ref[k], w[:D]) + prm_r[13:14, :wide]).astype(BF)
                x = kn_ref[k]
                kv_ref[k, :, :wide] = mm(x, w[D : 2 * D]).astype(BF)
                kv_ref[k, :, wide:] = (mm(x, w[2 * D :]) + prm_r[14:15, :wide]).astype(BF)

            loop(body)

        qn, kn, cross_q, cross_kv = vmem_call(
            "cross", k_cross, [*qns, *kns, after(c_in, grad_own), prm],
            [stack(Uq, D), stack(U, D), stack(Uq, wide), stack(U, 2 * wide)],
            flops=dot * U * G * 5 // 8 // D,
        )
        ckvs = [halves(t) for t in spread_j(cross_kv)]
        c_att, dq_c, dkvs = attend_both(
            heads, cross_idq, idk, halves(cross_q), given, ckvs
        )
        dkv_c_in = [dkvs[0]] + [xor("j", n, J, dkvs[n]) for n in range(1, J)]
        dkv_c_in = [t.reshape(G, U, 2 * wide) for t in dkv_c_in]
        dq_c = dq_c.reshape(G, Uq, wide)

        cos = spread_g(c_att)

        def k_dqn(dq_ref, w, sum_ref, *rest):
            out_refs, parts = rest[:-1], rest[-1]
            sum_ref[...] = jnp.zeros_like(sum_ref)

            def body(k):
                x = dq_ref[k]
                parts[k] = mm_nt(x, w[:D])
                sum_ref[...] += jnp.sum(x.astype(F32), axis=0, keepdims=True)

            loop(body)
            deliver_each(parts, out_refs)

        dcq, *dqn_out = vmem_call(
            "dqn", k_dqn, [dq_c, c_in],
            [piece(1, F32, wide)] + [piece(Uq)] * G,
            [pltpu.VMEM((G, Uq, D), F32)],
            flops=dot * Uq * G // 4 // D,
        )
        dqn_in = swap_g(dqn_out)

        def k_dkn(*refs):
            in_refs, (w, dkv_ref, sum_ref, *rest) = refs[:J], refs[J:]
            out_refs, parts = rest[:-1], rest[-1]
            sum_ref[...] = jnp.zeros_like(sum_ref)

            def body(k):
                x = in_refs[0][k].astype(F32)
                for r in in_refs[1:]:
                    x = x + r[k].astype(F32)
                x = x.astype(BF)
                dkv_ref[k] = x
                sum_ref[...] += jnp.sum(x.astype(F32), axis=0, keepdims=True)
                parts[k] = mm_nt(x[:, :wide], w[D : 2 * D]) + mm_nt(x[:, wide:], w[2 * D :])

            loop(body)
            deliver_each(parts, out_refs)

        dkv_c, dckv, *dkn_out = vmem_call(
            "dkn", k_dkn, [*dkv_c_in, c_in],
            [stack(U, 2 * wide), piece(1, F32, 2 * wide)] + [piece(U)] * G,
            [pltpu.VMEM((G, U, D), F32)],
            flops=dot * U * G // 2 // D,
        )
        dkn_in = swap_g(dkn_out)
        dqn = sum(x.astype(F32) for x in [after(dqn_in[0], dkv_c, *cos)] + dqn_in[1:]).astype(BF)
        dqn_v = from_queries(dqn)

        def k_mix(*refs):
            o_refs, (w, prm_r, o_ref, mix_ref) = refs[:G], refs[G:]
            for k in range(G):
                o_ref[k] = jnp.concatenate(
                    [unfold(r, k ^ m) for m, r in enumerate(o_refs)], axis=1
                )
            mix_ref[...] = (mm(o_ref[0], w[...]) + prm_r[15:16]).astype(BF)

        cross_o, mix = vmem_call(
            "mix", k_mix, [*cos, after(c_out, *dkn_out), prm], [stack(Uq, D), piece(Uq)],
            flops=dot * Uq // D,
        )

        def k_dy(grad_ref, zy_ref, rs_ref, dq_ref, prm_r, *rest):
            dk_refs, (dy_ref, dm_ref, sum_ref) = rest[:G], rest[G:]
            _, _, _, kv, _ = role()
            z = zy_ref[...]
            grad = grad_ref[...].astype(F32)
            dqv = jnp.where(kv == 0, 0.0, dq_ref[...].astype(F32))
            dkv = sum(r[...].astype(F32) for r in dk_refs)
            dkv = jnp.where(kv == 2, 0.0, dkv)
            dy = grad + unit_back(z, rs_ref[...], dqv * prm_r[9:10] + dkv * prm_r[10:11])
            dm = dy.astype(BF)
            dy_ref[...] = dy
            dm_ref[...] = dm
            for i, x in enumerate([dqv * z, dqv, dkv * z, dkv, grad, dm.astype(F32)]):
                sum_ref[i : i + 1, :] = jnp.sum(x, axis=0, keepdims=True)

        dy, dm_own, sums_y = vmem_call(
            "dy", k_dy, [after(grad_own, mix), zy, rs_y, dqn_v, prm, *dkn_in],
            [piece(U, F32), piece(U), piece(8, F32)],
        )

        dms = spread_g(dm_own)

        def k_mlp_back(*refs):
            m_refs, (slope_ref, wm, dm_ref, du_ref, sum_ref, out_ref, parts) = refs[:G], refs[G:]
            stage(m_refs, dm_ref)
            sum_ref[...] = jnp.zeros_like(sum_ref)

            def body(k):
                du = (mm(dm_ref[k], wm[D:]) * slope_ref[k].astype(F32)).astype(BF)
                du_ref[k] = du
                sum_ref[...] += jnp.sum(du.astype(F32), axis=0, keepdims=True)
                parts[k] = mm_nt(du, wm[:D])

            loop(body)
            deliver(parts, out_ref)

        dm, du, dbf, dc_out = vmem_call(
            "mlp_back", k_mlp_back, [*dms, slope, w_mlp],
            [stack(U, D), stack(U, hid), piece(1, F32, hid), stack(U, D)],
            [pltpu.VMEM((G, U, D), F32)],
            flops=2 * dot * U * G // D,
        )
        dc_in = collect_g(dc_out)

        h_back = h_own
        if near:
            ckv = [(7, i * wide, wide) for i in range(2)]
            gcols = (9, wide, wide, "chips")
            b_mc = home(
                "home_mc", [c, du, dm, e, qn, kn, dq_c, dkv_c, cross_o, given],
                [
                    ("enc", hid, r_mlp, [(0, 1, False), (2, 3, False)]),
                    (
                        "cross", wide, r_cross,
                        [(4, 6, False), (5, ckv[0], False), (5, ckv[1], False)],
                    ),
                    ("cross", wide, r_co, [(8, gcols, True)]),
                ],
            )
            h_back = after(h_own, *b_mc)

        def k_dh(got, h_ref, dy_ref, prm_r, dh_ref, dhb_ref, sum_ref):
            dn = total_of(got)
            z, rs = unit_rows(h_ref[...])
            dh = dy_ref[...] + unit_back(z, rs, dn * prm_r[1:2])
            dh_ref[...] = dh
            dhb = dh.astype(BF)
            dhb_ref[...] = dhb
            for i, x in enumerate([dn * z, dn, dhb.astype(F32)]):
                sum_ref[i : i + 1, :] = jnp.sum(x, axis=0, keepdims=True)

        dh, dh_own, sums_h = vmem_call(
            "dh", k_dh, [dc_in, h_back, dy, prm],
            [piece(U, F32), piece(U), piece(8, F32)],
        )
        dhs = spread_g(dh_own)
        if near:
            own_mc, other_mc = sum_j(b_mc, dc_in, dh_own)
            moved_mc = move_planes(other_mc)
            lse = after(lse, other_mc)
        dq, dkvs = attend_back(heads, idq, idk, q4, lse, w_out, dhs, kvs)
        dkv_in = [dkvs[0]] + [xor("j", n, J, dkvs[n]) for n in range(1, J)]
        dkv_in = [t.reshape(G, U, 2 * wide) for t in dkv_in]
        dq = dq.reshape(G, U, wide)
        if near:
            dq = after(dq, *moved_mc)
        def k_da(*refs):
            in_refs, (dq_ref, w, dkv_ref, sum_ref, out_ref, parts) = refs[:J], refs[J:]
            sum_ref[...] = jnp.zeros_like(sum_ref)

            def body(k):
                x = in_refs[0][k].astype(F32)
                for r in in_refs[1:]:
                    x = x + r[k].astype(F32)
                x = x.astype(BF)
                dkv_ref[k] = x
                dqk = dq_ref[k]
                sum_ref[0:1, :wide] += jnp.sum(dqk.astype(F32), axis=0, keepdims=True)
                sum_ref[1:2, :wide] += jnp.sum(
                    x[:, wide:].astype(F32), axis=0, keepdims=True
                )
                parts[k] = (
                    mm_nt(dqk, w[:D])
                    + mm_nt(x[:, :wide], w[D : 2 * D])
                    + mm_nt(x[:, wide:], w[2 * D :])
                )

            loop(body)
            deliver(parts, out_ref)

        dkv, sums_q, da_out = vmem_call(
            "da", k_da, [*dkv_in, dq, w_in],
            [stack(U, 2 * wide), piece(8, F32, wide), stack(U, D)],
            [pltpu.VMEM((G, U, D), F32)],
            flops=dot * U * G * 3 // 4 // D,
        )
        da_in = collect_g(da_out)
        dh_back = dh
        if near:
            own_kv = [(2, i * wide, wide) for i in range(2)]
            b_enc = home(
                "home_enc", [a, dq, dkv, o_all, *dhs],
                [
                    (
                        "enc", wide, r_in,
                        [(0, 1, False), (0, own_kv[0], False), (0, own_kv[1], False)],
                    ),
                    ("enc", wide, r_out, [(3, [4 + i for i in range(G)], True)]),
                ],
            )
            dh_back = after(dh, *b_enc)
        mix_v = from_queries(after(mix, da_out))

        def k_dx(got, x_ref, dh_ref, prm_r, dx_ref, sum_ref):
            da = total_of(got)
            z, rs = unit_rows(x_ref[...].astype(F32))
            dx_ref[...] = (dh_ref[...] + unit_back(z, rs, da * prm_r[0:1])).astype(BF)
            for i, x in enumerate([da * z, da]):
                sum_ref[i : i + 1, :] = jnp.sum(x, axis=0, keepdims=True)

        dx, sums_x = vmem_call(
            "dx", k_dx, [da_in, x_own, dh_back, prm], [piece(U), piece(8, F32)]
        )
        mix_v = jnp.where(v == 0, 0.0, after(mix_v, dx).astype(F32))
        last = jnp.stack([(y + mix_v).astype(BF), dx])
        if near:
            own_enc, other_enc = sum_j(b_enc, dx, dx)
            moved_enc = move_planes(other_enc)
            t_enc = sum_planes(after(own_enc, dx), moved_enc, r_out)
            t_mc = sum_planes(after(own_mc, dx), moved_mc, r_mlp)
            x_mc = lax.all_to_all(t_mc, "g", 0, 0, tiled=True)
            last, sums_x = after(last, *moved_enc), after(sums_x, other_enc)
        last = from_views(last)
        out_f, out_m, out_c = [t[0] for t in last]
        dx_f, dx_m, dx_c = [t[1] for t in last]

        deep_out = (-(-n_par // per) + 7) // 8 * 8
        blocks_out = -(-n_par // deep_out)

        def deal(sy, sh, sx, sq, cq_ref, ckv_ref, bf_ref, out_ref, full, ffn):
            kd, kg, kj, kv, kp = role()

            def if_view(k, x):
                return jnp.where(kv == k, x, 0.0)

            full[...] = jnp.zeros_like(full)
            ffn[...] = jnp.zeros_like(ffn)

            def at_cols(row, on, x):
                for k in range(G):
                    full[row : row + 1, k * wide : (k + 1) * wide] = jnp.where(
                        jnp.logical_and(on, kg == k), x, 0.0
                    )

            for k in range(3):
                full[2 * k : 2 * k + 1, :] = if_view(k, sx[0:1])
                full[2 * k + 1 : 2 * k + 2, :] = if_view(k, sh[0:1])
                at = 10 + 6 * k
                full[at : at + 1, :] = if_view(k, sx[1:2])
                at_cols(at + 1, kv == k, sq[0:1])
                at_cols(at + 2, kv == k, sq[1:2])
                full[at + 3 : at + 4, :] = if_view(k, sh[2:3])
                full[at + 4 : at + 5, :] = if_view(k, sh[1:2])
                full[at + 5 : at + 6, :] = if_view(k, sy[5:6])
                for i in range(G):
                    ffn[k : k + 1, i * hid : (i + 1) * hid] = jnp.where(
                        jnp.logical_and(kv == k, kg == i), bf_ref[...], 0.0
                    )
            for k in range(2):
                full[6 + 2 * k : 7 + 2 * k, :] = if_view(k + 1, sy[0:1])
                full[7 + 2 * k : 8 + 2 * k, :] = if_view(k, sy[2:3])
                at = 28 + 5 * k
                full[at : at + 1, :] = if_view(k + 1, sy[1:2])
                full[at + 1 : at + 2, :] = if_view(k, sy[3:4])
                at_cols(at + 2, kp == k, cq_ref[...])
                at_cols(at + 3, kp == k, ckv_ref[:, wide:])
                full[at + 4 : at + 5, :] = if_view(k + 1, sy[4:5])
            for i in range(n_dev):
                for r in range(3):
                    for t in range(fq):
                        to = 38 + r * fq + t
                        full[to : to + 1, i * gw : (i + 1) * gw] = ffn[
                            r : r + 1, i * fw + t * gw : i * fw + (t + 1) * gw
                        ]
            for i in range(n_dev):
                for b in range(blocks_out):
                    out_ref[i, :, b * gw : (b + 1) * gw] = full[
                        b * deep_out : (b + 1) * deep_out, i * gw : (i + 1) * gw
                    ]

        (small,) = vmem_call(
            "deal", deal, [sums_y, sums_h, sums_x, sums_q, dcq, dckv, dbf],
            [shape((n_dev, deep_out, 128), F32)],
            [pltpu.VMEM((blocks_out * deep_out, D), F32), pltpu.VMEM((3, ff), F32)],
        )
        small = lax.all_to_all(small, everyone, 0, 0, tiled=True)

        if near:
            x_enc = lax.all_to_all(
                after(t_enc, x_mc), "g", 0, 0, tiled=True
            )

        def my_rows(x):
            return lax.dynamic_index_in_dim(x, j, axis=2, keepdims=False)

        def send_home(grad, total, enc):
            width = grad.shape[1]
            r = total // n_dev
            if near:
                frame_rows, n_planes = total // 2, 2
                low = enc_lo if enc else cross_lo
            else:
                frame_rows, n_planes, low = total, dp, jnp.int32(0)
            if grad.shape[0] != frame_rows:
                part, n_parts = (v, 3) if enc else (p, 2)
                grad = lax.dynamic_update_slice_in_dim(
                    jnp.zeros((frame_rows, width), BF), grad.astype(BF),
                    start_of(part, n_parts, low, total), axis=0,
                )
            x = grad.astype(BF).reshape(n_planes, G, J, r, width)
            acc = lax.dynamic_index_in_dim(x, j, axis=2, keepdims=False).astype(F32)
            for n in range(1, J):
                part = lax.dynamic_index_in_dim(x, j ^ n, axis=2, keepdims=False)
                acc = acc + xor("j", n, J, part).astype(F32)
            if not near:
                acc = lax.psum_scatter(acc, "dp", scatter_dimension=0, tiled=False)
            elif enc:
                own = jnp.where(d == 0, acc[0], acc[1])
                other = jnp.where(d == 0, acc[1], acc[0]).astype(BF)
                down = lax.ppermute(other, "dp", [(1, 0), (2, 1), (3, 2)])
                upward = lax.ppermute(other, "dp", [(0, 1)])
                acc = own + down.astype(F32) + upward.astype(F32)
            else:
                odd = d % 2 == 1
                own = jnp.where(odd, acc[1], acc[0])
                other = jnp.where(odd, acc[0], acc[1]).astype(BF)
                acc = own + xor("dp", 1, dp, other).astype(F32)
            acc = acc.astype(BF).reshape(G * r, width)
            return lax.all_to_all(acc, "g", 0, 1, tiled=True).astype(F32)

        def in_order(w):
            return jnp.concatenate(
                [rows_at(w, (g ^ a) * wide, wide) for a in range(G)], axis=0
            )

        if near:
            def unpack_rows(x, i, in_ref, out_ref):
                unit = out_ref.shape[0]
                at = slice(i * wide, (i + 1) * wide)
                for b in range(4):
                    block = x[:, b * wide : (b + 1) * wide].astype(F32)
                    if b < 3:
                        in_ref[b * unit : (b + 1) * unit, at] = block
                    else:
                        out_ref[:, at] = block

            def landed(x_ref, gm_ref, gci_ref, gco_ref):
                for i in range(G):
                    gm_ref[:, i * hid : (i + 1) * hid] = x_ref[i, :r_mlp].astype(F32)
                    unpack_rows(x_ref[i, r_mlp:], i, gci_ref, gco_ref)

            grad_mlp, grad_cin, grad_cout = vmem_call(
                "landed", landed, [after(x_mc, small)],
                [shape(mlp_w.shape, F32), shape(cross_in.shape, F32), shape(cross_out.shape, F32)],
            )

            def landed_enc(x_ref, gi_ref, go_ref):
                for i in range(G):
                    unpack_rows(x_ref[i], i, gi_ref, go_ref)

            grad_in, grad_out = vmem_call(
                "landed_enc", landed_enc, [x_enc],
                [shape(attn_in.shape, F32), shape(attn_out.shape, F32)],
            )
        else:
            flat = lambda t: t.reshape(-1, t.shape[-1])
            a_f, c_f, q_f, k_f = flat(a), flat(c), flat(qn), flat(kn)
            ckv, skv = flat(dkv_c), flat(dkv)
            dh_all = jnp.concatenate(dhs, axis=0)
            g_cin = jnp.concatenate(
                [mm_tn(q_f, flat(dq_c)), mm_tn(k_f, ckv[:, :wide]), mm_tn(k_f, ckv[:, wide:])],
                axis=0,
            )
            g_cols = jnp.concatenate(
                [rows_at(given, g ^ m, 1)[0][:, wide:] for m in range(G)], axis=0
            )
            g_cout = in_order(mm_tn(flat(cross_o), g_cols))
            g_mlp = jnp.concatenate([mm_tn(c_f, flat(du)), mm_tn(flat(dm), flat(e))], axis=0)
            g_out = in_order(mm_tn(flat(o_all), cols(dh_all, wide)))
            g_in = jnp.concatenate(
                [mm_tn(a_f, flat(dq)), mm_tn(a_f, skv[:, :wide]), mm_tn(a_f, skv[:, wide:])],
                axis=0,
            )
            grad_cin = send_home(g_cin, n_dev * r_cross, False)
            grad_cout = send_home(g_cout, n_dev * r_co, False)
            grad_mlp = send_home(g_mlp, n_dev * r_mlp, True)
            grad_out = send_home(g_out, n_dev * r_out, True)
            grad_in = send_home(g_in, n_dev * r_in, True)

        def collect(x_ref, g_ref, b_ref, f_ref):
            x = jnp.sum(x_ref[...], axis=0)
            rows = [
                x[r % deep_out : r % deep_out + 1, r // deep_out * gw : (r // deep_out + 1) * gw]
                for r in range(n_par)
            ]
            for r in range(38):
                if r < 10:
                    g_ref[r : r + 1, :] = rows[r]
                else:
                    b_ref[r - 10 : r - 9, :] = rows[r]
            for r in range(3):
                for t in range(fq):
                    f_ref[r : r + 1, t * gw : (t + 1) * gw] = rows[38 + r * fq + t]

        grad_gains, grad_bias, grad_ffn = vmem_call(
            "collect", collect, [small],
            [shape(norm_gains.shape, F32), shape(biases.shape, F32), shape(ffn_bias.shape, F32)],
        )
        return (
            out_f[None], out_m[None], out_c[None],
            dx_f.astype(F32)[None], dx_m.astype(F32)[None], dx_c.astype(F32)[None],
            grad_in, grad_out, grad_mlp, grad_cin, grad_cout,
            grad_gains, grad_bias, grad_ffn,
        )

    tokens = P("dp", ("g", "j"), None)
    rows = P(everyone, None)
    columns = P(None, everyone)
    return jax.shard_map(
        per_device,
        mesh=mesh3,
        in_specs=(tokens,) * 6 + (P("dp", None),) + (rows,) * 5 + (columns,) * 3,
        out_specs=(tokens,) * 6 + (rows,) * 5 + (columns,) * 3,
        check_vma=False,
    )
```
